256 devices in a mesh: tm: 8 (over x, core), strip: 32 (over z, y).
Axes of the slice: x: 4, y: 4, z: 8, core: 2. Of those that a mesh axis runs over, the one named last changes fastest.
Arguments:
- feature: bfloat16 [8, 64, 160, 384], P('tm', 'strip'), may hold values from -100 to 100
- frame_cache: bfloat16 [2, 64, 160, 384], P(None, 'strip'), may hold values from -6 to 6
- norm_gain: float32 [384], replicated, may hold values from 0.1 to 1.9
- conv_weight: bfloat16 [3, 3, 3, 384, 384], replicated, may hold values from -0.0625 to 0.0625
- conv_bias: float32 [384], replicated, may hold values from -3 to 3
- attn_gain: float32 [384], replicated, may hold values from 0.1 to 1.9
- qkv_weight: bfloat16 [384, 1152], replicated, may hold values from -2 to 2
- qkv_bias: float32 [1152], replicated, may hold values from -2 to 2
- out_weight: bfloat16 [384, 384], replicated, may hold values from -0.3125 to 0.3125
- out_bias: float32 [384], replicated, may hold values from -2 to 2
Outputs:
- mixed: bfloat16 [8, 64, 160, 384], P('tm', 'strip')
The draws below stay inside these ranges and needn't reach their ends.
All inputs are finite; a program needn't handle non-finite values.
Results may differ from the reference program's by a relative error of at most 0.017.
Values may be sent and summed in bfloat16 or wider, within the bound.
No kernel may reach another device: no remote copies, remote signals or barrier semaphores. Data moves between devices by JAX's collectives and lax.ppermute only.
A program may use at most 128 MiB of HBM per device.

```python
import math
import jax
import jax.numpy as jnp
from jax import lax

CHANNELS = 384
WIDTH = 160
HEIGHT = 64
FRAMES = 8


def shared_signs(key, salt):
    bits = jax.random.randint(jax.random.fold_in(key, salt), (CHANNELS,), 0, 2)
    return (2 * bits - 1).astype(jnp.float32)


def draw_feature(key, part):
    base_key, scale_key, offset_key, place_key, first_key, second_key = [jax.random.fold_in(key, number) for number in range(6)]
    shape = (FRAMES, HEIGHT, WIDTH, CHANNELS)
    height_frac = jnp.arange(HEIGHT, dtype=jnp.float32) / max(HEIGHT - 1, 1)
    row_scale = 0.4 * jnp.power(10.0, height_frac)
    channel_scale = jnp.exp(jax.random.uniform(scale_key, (CHANNELS,), jnp.float32, math.log(0.5), math.log(2.0)))
    channel_offset = 0.5 * jax.random.normal(offset_key, (CHANNELS,), jnp.float32)
    noise = jax.random.normal(base_key, shape, jnp.float32)
    values = noise * row_scale[None, :, None, None] * channel_scale + channel_offset
    signs = shared_signs(key, 101)
    strengths = jnp.array([0.98, 0.85, 0.7], jnp.float32)[None, :, None]
    partners = strengths - 0.01
    first_noise = jax.random.normal(first_key, (FRAMES, 3, CHANNELS), jnp.float32)
    second_noise = jax.random.normal(second_key, (FRAMES, 3, CHANNELS), jnp.float32)
    first = 20.0 * (strengths * signs + jnp.sqrt(1.0 - strengths * strengths) * first_noise)
    second = 20.0 * (partners * signs + jnp.sqrt(1.0 - partners * partners) * second_noise)
    tokens = values.reshape(FRAMES, HEIGHT * WIDTH, CHANNELS)
    places = jax.random.randint(place_key, (FRAMES, 3), 0, HEIGHT * WIDTH - 1)
    frame_ids = jnp.arange(FRAMES)[:, None]
    tokens = tokens.at[frame_ids, places].set(first)
    tokens = tokens.at[frame_ids, places + 1].set(second)
    values = tokens.reshape(shape)
    return jnp.clip(values, -90.0, 90.0).astype(jnp.bfloat16)


def draw_qkv_weight(key, part):
    noise_key = jax.random.fold_in(key, 7)
    spread = math.sqrt(3.0 / CHANNELS)
    noise = jnp.clip(jax.random.normal(noise_key, (CHANNELS, 3 * CHANNELS), jnp.float32), -5.0, 5.0) * spread
    inner = shared_signs(key, 101) / math.sqrt(CHANNELS)
    outer = shared_signs(key, 102) / math.sqrt(CHANNELS)
    aligned = 3.5 * inner[:, None] * outer[None, :]
    shared = jnp.concatenate([aligned, aligned, jnp.zeros((CHANNELS, CHANNELS), jnp.float32)], axis=1)
    return (noise + shared).astype(jnp.bfloat16)


def levels(rng, extent, pieces, smallest, top_value):
    loudness = 1.0
    for dim, shards_of in pieces:
        draws = jax.random.uniform(jax.random.fold_in(jax.random.fold_in(rng, 6), dim), (shards_of,), jnp.float32, smallest / len(pieces), top_value / len(pieces))
        loudness = loudness * jnp.repeat(jnp.exp(draws), extent[dim] // shards_of).reshape((-1,) + (1,) * (len(extent) - 1 - dim))
    return loudness


def centred(key, dims, scale, limit, pieces=(), kind=jnp.bfloat16):
    level = levels(key, dims, pieces, -0.22, 0.18) if pieces else 1.0
    values = jax.random.normal(key, dims, jnp.float32) * scale * level
    return jnp.minimum(jnp.maximum(values, -limit), limit).astype(kind)


def setup_inputs(seed: int = 0) -> dict:
    key_of = jax.random.split(jax.random.key(seed), 11)
    feature = draw_feature(jax.random.fold_in(key_of[10], 71), 0)
    frame_cache = centred(key_of[1], (2, HEIGHT, WIDTH, CHANNELS), 1.0, 6.0, ((1, 32),))
    norm_gain = jnp.clip(1.0 + 0.18 * jax.random.normal(key_of[2], (CHANNELS,), jnp.float32), 0.1, 1.9)
    conv_weight = centred(key_of[3], (3, 3, 3, CHANNELS, CHANNELS), (27 * CHANNELS) ** -0.5, 0.0625)
    conv_bias = centred(key_of[4], (CHANNELS,), 0.5, 3.0, (), jnp.float32)
    attn_gain = jnp.clip(1.0 + 0.18 * jax.random.normal(key_of[5], (CHANNELS,), jnp.float32), 0.1, 1.9)
    qkv_weight = draw_qkv_weight(jax.random.fold_in(key_of[10], 71), 0)
    qkv_bias = centred(key_of[7], (3 * CHANNELS,), 0.3, 2.0, (), jnp.float32)
    out_weight = centred(key_of[8], (CHANNELS, CHANNELS), CHANNELS ** -0.5, 0.3125)
    out_bias = centred(key_of[9], (CHANNELS,), 0.3, 2.0, (), jnp.float32)
    return dict(feature=feature, frame_cache=frame_cache, norm_gain=norm_gain, conv_weight=conv_weight, conv_bias=conv_bias, attn_gain=attn_gain, qkv_weight=qkv_weight, qkv_bias=qkv_bias, out_weight=out_weight, out_bias=out_bias)


epsilon = 1e-06

def rms_norm(values, gain):
    mean_square = lax.optimization_barrier(jnp.mean(jnp.square(values), axis=-1, keepdims=True))
    return values * lax.rsqrt(mean_square + epsilon) * gain

def reference(feature, frame_cache, norm_gain, conv_weight, conv_bias, attn_gain, qkv_weight, qkv_bias, out_weight, out_bias):
    values = feature.astype(jnp.float32)
    activated = jax.nn.silu(rms_norm(values, norm_gain)).astype(jnp.bfloat16)
    extended = jnp.concatenate([frame_cache, activated], axis=0)
    padded = jnp.pad(extended, ((0, 0), (1, 1), (1, 1), (0, 0))).astype(jnp.float32)
    kernel = conv_weight.astype(jnp.float32)

    def conv_frame(frame_number):
        window = lax.dynamic_slice_in_dim(padded, frame_number, 3, 0)
        result = jnp.zeros((HEIGHT * WIDTH, CHANNELS), jnp.float32)
        for frame_tap in range(3):
            for row_tap in range(3):
                row_band = window[frame_tap, row_tap:row_tap + HEIGHT]
                columns = jnp.concatenate([row_band[:, col_tap:col_tap + WIDTH] for col_tap in range(3)], axis=-1)
                columns = columns.reshape(HEIGHT * WIDTH, 3 * CHANNELS)
                result = result + jnp.dot(columns, kernel[frame_tap, row_tap].reshape(3 * CHANNELS, CHANNELS), preferred_element_type=jnp.float32)
        return result
    branch = lax.map(conv_frame, jnp.arange(FRAMES, dtype=jnp.int32)).reshape(FRAMES, HEIGHT, WIDTH, CHANNELS)
    hidden = (values + (branch + conv_bias)).astype(jnp.bfloat16)
    normed = rms_norm(hidden.astype(jnp.float32), attn_gain).astype(jnp.bfloat16)
    projected = jnp.dot(normed.reshape(-1, CHANNELS).astype(jnp.float32), qkv_weight.astype(jnp.float32), preferred_element_type=jnp.float32) + qkv_bias
    projected = projected.astype(jnp.bfloat16).reshape(FRAMES, HEIGHT * WIDTH, 3 * CHANNELS)
    score_scale = 1.0 / math.sqrt(CHANNELS)

    def attend(frame_rows):
        queries = frame_rows[:, :CHANNELS].astype(jnp.float32).reshape(HEIGHT, WIDTH, CHANNELS)
        key_rows = frame_rows[:, CHANNELS:2 * CHANNELS].astype(jnp.float32)
        value_rows = frame_rows[:, 2 * CHANNELS:].astype(jnp.float32)

        def query_block(block_rows):
            scores = jnp.dot(block_rows, key_rows.T, preferred_element_type=jnp.float32) * score_scale
            highest = lax.optimization_barrier(jnp.max(scores, axis=1, keepdims=True))
            weights = jnp.exp(scores - highest)
            denominator = lax.optimization_barrier(jnp.sum(weights, axis=1, keepdims=True))
            rounded = lax.optimization_barrier(weights.astype(jnp.bfloat16)).astype(jnp.float32)
            numerator = jnp.dot(rounded, value_rows, preferred_element_type=jnp.float32)
            return (numerator / denominator).astype(jnp.bfloat16)
        return lax.map(query_block, queries).reshape(HEIGHT * WIDTH, CHANNELS)
    attended = lax.map(attend, projected).reshape(-1, CHANNELS)
    result = jnp.dot(attended.astype(jnp.float32), out_weight.astype(jnp.float32), preferred_element_type=jnp.float32) + out_bias
    result = result + hidden.reshape(-1, CHANNELS).astype(jnp.float32)
    return result.astype(jnp.bfloat16).reshape(FRAMES, HEIGHT, WIDTH, CHANNELS)
```

```python
import functools
import math

import jax
import jax.numpy as jnp
from jax import lax
from jax.experimental import pallas as pl
from jax.experimental.pallas import tpu as pltpu
from jax.sharding import PartitionSpec as P

EPSILON = 1e-06
FRAMES = 8
ROW_STRIPS = 32
RING = 8
GROUP = 4
STAT_ROWS = 16
VMEM = pl.BlockSpec(memory_space=pltpu.VMEM)
SMEM = pl.BlockSpec(memory_space=pltpu.SMEM)
ANY = pl.BlockSpec(memory_space=pl.ANY)
F32 = jnp.float32
BF16 = jnp.bfloat16
VMEM_LIMIT = 48 << 20


def call(body, name, outs, in_specs, flops, scratch=()):
    return pl.pallas_call(
        body,
        name=name,
        out_shape=[jax.ShapeDtypeStruct(*out) for out in outs],
        in_specs=in_specs,
        out_specs=[VMEM] * len(outs),
        scratch_shapes=list(scratch),
        cost_estimate=pl.CostEstimate(flops=int(flops), bytes_accessed=2 << 20, transcendentals=0),
        compiler_params=pltpu.CompilerParams(vmem_limit_bytes=VMEM_LIMIT),
    )


def rms_scaled(values, gain):
    mean_square = jnp.mean(values * values, axis=-1, keepdims=True)
    return values * lax.rsqrt(mean_square + EPSILON) * gain


def activate(row, gain):
    u = rms_scaled(row.astype(F32), gain)
    return u / (1.0 + jnp.exp(-u))


def put_columns(target, place, row):
    width, channels = row.shape
    column = lax.broadcasted_iota(jnp.int32, row.shape, 0)
    left = jnp.where(column == 0, 0.0, pltpu.roll(row, 1, 0))
    right = jnp.where(column == width - 1, 0.0, pltpu.roll(row, width - 1, 0))
    rows = pl.ds(place * width, width)
    target[rows, 0:channels] = left.astype(BF16)
    target[rows, channels : 2 * channels] = row.astype(BF16)
    target[rows, 2 * channels : 3 * channels] = right.astype(BF16)


def nine_taps(columns, weights, total, width):
    rows = total.shape[0]
    for row_tap in range(3):
        product = jnp.dot(
            columns[row_tap * width : row_tap * width + rows, :],
            weights(row_tap),
            preferred_element_type=F32,
        )
        if row_tap == 0:
            total[...] = product
        else:
            total[...] += product


def conv_later_body(frame, feat, above, below, cache, gain, weight, two_later, one_later,
                    columns, held, total, sems):
    width = feat.shape[1]
    copies = []
    for frame_tap in range(2):
        for row_tap in range(3):
            copy = pltpu.make_async_copy(
                weight.at[frame_tap, row_tap], held.at[frame_tap, row_tap],
                sems.at[frame_tap, row_tap],
            )
            copy.start()
            copies.append(copy)
    for place, row in enumerate((above[0], feat[0], feat[1], below[0])):
        put_columns(columns.at[0], place, activate(row, gain[...]))

    @pl.when(frame[0] >= FRAMES - 2)
    def _():
        for place, row in enumerate((above[1], cache[0], cache[1], below[1])):
            put_columns(columns.at[1], place, row.astype(F32))

    for frame_tap, out in ((0, two_later), (1, one_later)):
        source = jnp.where(frame[0] >= FRAMES - 2 + frame_tap, 1, 0)

        def weights(row_tap):
            copies[3 * frame_tap + row_tap].wait()
            return held[frame_tap, row_tap]

        nine_taps(columns.at[source], weights, total, width)
        out[...] = total[...].astype(BF16)


def conv_own_body(feat, above, below, gain, weight, own, columns, held, sems):
    width = feat.shape[1]
    copies = []
    for row_tap in range(3):
        copy = pltpu.make_async_copy(weight.at[2, row_tap], held.at[row_tap], sems.at[row_tap])
        copy.start()
        copies.append(copy)
    for place, row in enumerate((above[0], feat[0], feat[1], below[0])):
        put_columns(columns, place, activate(row, gain[...]))

    def weights(row_tap):
        copies[row_tap].wait()
        return held[row_tap]

    nine_taps(columns, weights, own, width)


def hidden_body(feat, own, one, two, bias, gain, hidden, first, second):
    rows = own.shape[0]
    values = feat[...].astype(F32).reshape(own.shape)
    branch = own[...] + one[...].astype(F32) + two[...].astype(F32) + bias[...]
    result = (values + branch).astype(BF16)
    hidden[...] = result
    normed = rms_scaled(result.astype(F32), gain[...]).astype(BF16)
    first[...] = normed[: rows // 2]
    second[...] = normed[rows // 2 :]


def query_body(first, second, weight, bias, query, shift):
    channels = first.shape[1]
    scale = math.log2(math.e) / math.sqrt(channels)
    normed = jnp.concatenate([first[...], second[...]], axis=0)
    q = jnp.dot(normed, weight[:, :channels], preferred_element_type=F32) + bias[:, :channels]
    q = q.astype(BF16)
    absorbed = lax.dot_general(
        q, weight[:, channels : 2 * channels], (((1,), (1,)), ((), ())), preferred_element_type=F32
    )
    query[...] = (absorbed * scale).astype(BF16)
    key_bias = bias[:, channels : 2 * channels]
    shift[...] = jnp.sum(q.astype(F32) * key_bias, axis=-1, keepdims=True) * scale


def attend_body(chunks, started, final, *refs):
    queries, refs = refs[:GROUP], refs[GROUP:]
    pieces, refs = refs[:chunks], refs[chunks:]
    if started:
        (total_in, top_in, sum_in), refs = refs[:3], refs[3:]
    outs, (keys,) = refs[:-1], refs[-1:]
    length = pieces[0].shape[0]
    for number, piece in enumerate(pieces):
        keys[number * length : (number + 1) * length, :] = piece[...]
    rows, channels = queries[0].shape
    for number, query in enumerate(queries):
        scores = lax.dot_general(
            query[...], keys[...], (((1,), (1,)), ((), ())), preferred_element_type=F32
        )
        top = jnp.max(scores, axis=1, keepdims=True)
        if started:
            old_top = top_in[number][:, :1]
            top = jnp.maximum(top, old_top)
        weights = jnp.exp2(scores - top)
        denominator = jnp.sum(weights, axis=1, keepdims=True)
        total = jnp.dot(weights.astype(BF16), keys[...], preferred_element_type=F32)
        if started:
            factor = jnp.exp2(old_top - top)
            denominator = denominator + sum_in[number][:, :1] * factor
            total = total + total_in[number] * factor
        if not final:
            outs[0][number] = total
            outs[1][number] = jnp.broadcast_to(top, (rows, 128))
            outs[2][number] = jnp.broadcast_to(denominator, (rows, 128))
            continue
        out = outs[number]
        out[:rows, :] = (total / denominator).astype(BF16)
        level = top + jnp.log2(denominator)
        row = lax.broadcasted_iota(jnp.int32, (rows, channels), 0)
        lane = lax.broadcasted_iota(jnp.int32, (rows, channels), 1)
        level = jnp.sum(jnp.where(row == lane, level, 0.0), axis=0, keepdims=True)
        high = level.astype(BF16).astype(F32)
        middle = (level - high).astype(BF16).astype(F32)
        low = level - high - middle
        row = lax.broadcasted_iota(jnp.int32, (STAT_ROWS, channels), 0)
        stats = jnp.where(row == 0, high, jnp.where(row == 1, middle, jnp.where(row == 2, low, 0.0)))
        out[rows:, :] = stats.astype(BF16)


def merge_body(part0, part1, part2, part3, shift, hidden, weight, bias, out_weight, out_bias, mixed):
    rows, channels = hidden.shape
    row = lax.broadcasted_iota(jnp.int32, (rows, channels), 0)
    lane = lax.broadcasted_iota(jnp.int32, (rows, channels), 1)
    parts = (part0, part1, part2, part3)
    levels = []
    for part in parts:
        stats = part[rows:, :].astype(F32)
        level = stats[0:1] + stats[1:2] + stats[2:3]
        level = jnp.sum(jnp.where(row == lane, level, 0.0), axis=1, keepdims=True)
        levels.append(level + shift[...])
    top = functools.reduce(jnp.maximum, levels)
    shares = [jnp.exp2(level - top) for level in levels]
    inverse = 1.0 / sum(shares)
    total = sum(share * inverse * part[:rows, :].astype(F32) for share, part in zip(shares, parts))
    attended = jnp.dot(
        total.astype(BF16), weight[:, 2 * channels :], preferred_element_type=F32
    ) + bias[:, 2 * channels :]
    result = jnp.dot(attended.astype(BF16), out_weight[...], preferred_element_type=F32)
    result = result + out_bias[...] + hidden[...].astype(F32)
    mixed[...] = result.astype(BF16)


def along_y(x, by):
    pairs = [
        (z * GROUP + y, z * GROUP + (y + by) % GROUP) for z in range(RING) for y in range(GROUP)
    ]
    return lax.ppermute(x, "strip", pairs)


def along_z(x, by):
    pairs = [
        (z * GROUP + y, (z + by) % RING * GROUP + y) for z in range(RING) for y in range(GROUP)
    ]
    return lax.ppermute(x, "strip", pairs)


def local(
    feature,
    frame_cache,
    norm_gain,
    conv_weight,
    conv_bias,
    attn_gain,
    qkv_weight,
    qkv_bias,
    out_weight,
    out_bias,
):
    _, height, width, channels = feature.shape
    rows = height * width
    half = rows // 2
    feat = feature[0]
    frame = lax.axis_index("tm")
    gain = norm_gain.reshape(1, channels)
    weight = conv_weight.reshape(3, 3, 3 * channels, channels)
    qkv_bias = qkv_bias.reshape(1, 3 * channels)

    cache = lax.dynamic_index_in_dim(
        frame_cache, jnp.where(frame == FRAMES - 2, 0, 1), 0, keepdims=False
    )
    down = [(s, s + 1) for s in range(ROW_STRIPS - 1)]
    up = [(s + 1, s) for s in range(ROW_STRIPS - 1)]
    above = lax.ppermute(jnp.stack([feat[height - 1], cache[height - 1]]), "strip", down)
    below = lax.ppermute(jnp.stack([feat[0], cache[0]]), "strip", up)

    tap_flops = 2 * rows * 9 * channels * channels
    two_later, one_later = call(
        conv_later_body,
        "conv_later",
        [((rows, channels), BF16)] * 2,
        [SMEM, VMEM, VMEM, VMEM, VMEM, VMEM, ANY],
        2 * tap_flops,
        [
            pltpu.VMEM((2, 4 * width, 3 * channels), BF16),
            pltpu.VMEM((2, 3, 3 * channels, channels), BF16),
            pltpu.VMEM((rows, channels), F32),
            pltpu.SemaphoreType.DMA((2, 3)),
        ],
    )(frame.reshape(1).astype(jnp.int32), feat, above, below, cache, gain, weight)
    two = lax.ppermute(two_later, "tm", [(f, (f + 2) % FRAMES) for f in range(FRAMES)])
    one = lax.ppermute(one_later, "tm", [(f, (f + 1) % FRAMES) for f in range(FRAMES)])
    (own,) = call(
        conv_own_body,
        "conv_own",
        [((rows, channels), F32)],
        [VMEM, VMEM, VMEM, VMEM, ANY],
        tap_flops,
        [
            pltpu.VMEM((4 * width, 3 * channels), BF16),
            pltpu.VMEM((3, 3 * channels, channels), BF16),
            pltpu.SemaphoreType.DMA((3,)),
        ],
    )(feat, above, below, gain, weight)
    hidden, first, second = call(
        hidden_body,
        "hidden",
        [((rows, channels), BF16)] + [((half, channels), BF16)] * 2,
        [VMEM] * 6,
        rows * channels * 20,
    )(feat, own, one, two, conv_bias.reshape(1, channels), attn_gain.reshape(1, channels))

    forward = [(first, second)]
    backward = [(first, second)]
    for step in range(3):
        forward.append(tuple(along_z(x, 1) for x in forward[-1]))
        backward.append(tuple(along_z(x, -1) for x in backward[-1]))
    last = (along_z(forward[3][0], 1), along_z(backward[3][1], -1))

    query, shift = call(
        query_body,
        "query",
        [((rows, channels), BF16), ((rows, 1), F32)],
        [VMEM] * 4,
        4 * rows * channels * channels,
    )(first, second, qkv_weight, qkv_bias)
    queries = [query] + [along_y(query, -by) for by in range(1, GROUP)]

    def attend(name, pieces, state, final):
        if final:
            outs = [((rows + STAT_ROWS, channels), BF16)] * GROUP
        else:
            outs = [((GROUP, rows, channels), F32)] + [((GROUP, rows, 128), F32)] * 2
        keys = len(pieces) * half
        return call(
            functools.partial(attend_body, len(pieces), bool(state), final),
            name,
            outs,
            [VMEM] * (GROUP + len(pieces) + len(state)),
            4 * GROUP * rows * keys * channels,
            [pltpu.VMEM((keys, channels), BF16)],
        )(*queries, *pieces, *state)

    early = [first, second]
    for step in (1, 2):
        early += [*forward[step], *backward[step]]
    state = attend("attend_early", early, (), False)
    parts = attend("attend_late", [*forward[3], *backward[3], *last], tuple(state), True)
    arrived = [along_y(parts[by], by) for by in range(1, GROUP)]
    (mixed,) = call(
        merge_body,
        "merge",
        [((rows, channels), BF16)],
        [VMEM] * 10,
        4 * rows * channels * channels,
    )(parts[0], *arrived, shift, hidden, qkv_weight, qkv_bias, out_weight, out_bias.reshape(1, channels))
    return mixed.reshape(feature.shape)


def solution(mesh):
    in_specs = (P("tm", "strip", None, None), P(None, "strip", None, None)) + (P(),) * 8
    out_specs = P("tm", "strip", None, None)
    return jax.shard_map(local, mesh=mesh, in_specs=in_specs, out_specs=out_specs, check_vma=False)
```

```python
import functools
import math

import jax
import jax.numpy as jnp
from jax import lax
from jax.experimental import pallas as pl
from jax.experimental.pallas import tpu as pltpu
from jax.sharding import PartitionSpec as P

EPSILON = 1e-06
FRAMES = 8
ROW_STRIPS = 32
RING = 8
GROUP = 4
STAT_ROWS = 16
VMEM = pl.BlockSpec(memory_space=pltpu.VMEM)
SMEM = pl.BlockSpec(memory_space=pltpu.SMEM)
ANY = pl.BlockSpec(memory_space=pl.ANY)
F32 = jnp.float32
BF16 = jnp.bfloat16
VMEM_LIMIT = 32 << 20


def call(body, name, outs, in_specs, flops, scratch=()):
    return pl.pallas_call(
        body,
        name=name,
        out_shape=[jax.ShapeDtypeStruct(*out) for out in outs],
        in_specs=in_specs,
        out_specs=[VMEM] * len(outs),
        scratch_shapes=list(scratch),
        cost_estimate=pl.CostEstimate(flops=int(flops), bytes_accessed=2 << 20, transcendentals=0),
        compiler_params=pltpu.CompilerParams(vmem_limit_bytes=VMEM_LIMIT),
    )


def rms_scaled(values, gain):
    mean_square = jnp.mean(values * values, axis=-1, keepdims=True)
    return values * lax.rsqrt(mean_square + EPSILON) * gain


def activate(row, gain):
    u = rms_scaled(row.astype(F32), gain)
    return u / (1.0 + jnp.exp(-u))


def put_columns(target, place, row):
    width, channels = row.shape
    column = lax.broadcasted_iota(jnp.int32, row.shape, 0)
    left = jnp.where(column == 0, 0.0, pltpu.roll(row, 1, 0))
    right = jnp.where(column == width - 1, 0.0, pltpu.roll(row, width - 1, 0))
    rows = pl.ds(place * width, width)
    target[rows, 0:channels] = left.astype(BF16)
    target[rows, channels : 2 * channels] = row.astype(BF16)
    target[rows, 2 * channels : 3 * channels] = right.astype(BF16)


def conv_local_body(frame, feat, cache, gain, weight, two_later, one_later, own,
                    columns, held, sems):
    width = feat.shape[1]
    copies = {}
    for frame_tap in range(3):
        for row_tap in (1, 0, 2):
            place = frame_tap, row_tap
            copies[place] = pltpu.make_async_copy(weight.at[place], held.at[place], sems.at[place])
            copies[place].start()
    for row in range(2):
        put_columns(columns.at[0], row, activate(feat[row], gain[...]))

    @pl.when(frame[0] >= FRAMES - 2)
    def _():
        for row in range(2):
            put_columns(columns.at[1], row, cache[row].astype(F32))

    for frame_tap, out in ((0, two_later), (1, one_later), (2, own)):
        if frame_tap < 2:
            source = columns.at[jnp.where(frame[0] >= FRAMES - 2 + frame_tap, 1, 0)]
        else:
            source = columns.at[0]
        for row_tap, start, first, count in ((1, 0, 0, 2), (0, 1, 0, 1), (2, 0, 1, 1)):
            copies[frame_tap, row_tap].wait()
            product = jnp.dot(
                source[first * width : (first + count) * width, :],
                held[frame_tap, row_tap],
                preferred_element_type=F32,
            )
            rows = pl.ds(start * width, count * width)
            if row_tap == 1:
                out[rows, :] = product
            else:
                out[rows, :] += product


def conv_edges_body(frame, above, below, gain, weight, two_local, one_local, two_later, one_later,
                    columns):
    width = above.shape[1]
    for place, halo in enumerate((above, below)):

        @pl.when(frame[0] < FRAMES - 1)
        def _():
            put_columns(columns.at[0], place, activate(halo[0], gain[...]))

        @pl.when(frame[0] >= FRAMES - 2)
        def _():
            put_columns(columns.at[1], place, halo[1].astype(F32))

    for frame_tap, start, out in ((0, two_local, two_later), (1, one_local, one_later)):
        source = columns.at[jnp.where(frame[0] >= FRAMES - 2 + frame_tap, 1, 0)]
        for place in range(2):
            rows = pl.ds(place * width, width)
            product = jnp.dot(
                source[place * width : (place + 1) * width, :],
                weight[frame_tap, 2 * place],
                preferred_element_type=F32,
            )
            out[rows, :] = (start[rows, :] + product).astype(BF16)


def conv_own_body(above, below, gain, weight, own_local, own, columns):
    width = above.shape[1]
    for place, halo in enumerate((above, below)):
        put_columns(columns, place, activate(halo[0], gain[...]))
        rows = pl.ds(place * width, width)
        product = jnp.dot(
            columns[place * width : (place + 1) * width, :],
            weight[2, 2 * place],
            preferred_element_type=F32,
        )
        own[rows, :] = own_local[rows, :] + product


def hidden_body(feat, own, one, two, bias, gain, hidden, normed):
    values = feat[...].astype(F32).reshape(own.shape)
    branch = own[...] + one[...].astype(F32) + two[...].astype(F32) + bias[...]
    result = (values + branch).astype(BF16)
    hidden[...] = result
    normed[...] = rms_scaled(result.astype(F32), gain[...]).astype(BF16)


def query_body(normed, weight, bias, query, shift):
    channels = normed.shape[1]
    scale = math.log2(math.e) / math.sqrt(channels)
    q = jnp.dot(normed[...], weight[:, :channels], preferred_element_type=F32) + bias[:, :channels]
    q = q.astype(BF16)
    absorbed = lax.dot_general(
        q, weight[:, channels : 2 * channels], (((1,), (1,)), ((), ())), preferred_element_type=F32
    )
    query[...] = (absorbed * scale).astype(BF16)
    key_bias = bias[:, channels : 2 * channels]
    shift[...] = jnp.sum(q.astype(F32) * key_bias, axis=-1, keepdims=True) * scale


def attend_body(chunks, started, final, *refs):
    queries, refs = refs[:GROUP], refs[GROUP:]
    pieces, refs = refs[:chunks], refs[chunks:]
    if started:
        (total_in, top_in, sum_in), refs = refs[:3], refs[3:]
    outs, (keys,) = refs[:-1], refs[-1:]
    start = 0
    for piece in pieces:
        keys[start : start + piece.shape[0], :] = piece[...]
        start += piece.shape[0]
    rows, channels = queries[0].shape
    for number, query in enumerate(queries):
        scores = lax.dot_general(
            query[...], keys[...], (((1,), (1,)), ((), ())), preferred_element_type=F32
        )
        top = jnp.max(scores, axis=1, keepdims=True)
        if started:
            old_top = top_in[number][:, :1]
            top = jnp.maximum(top, old_top)
        weights = jnp.exp2(scores - top)
        denominator = jnp.sum(weights, axis=1, keepdims=True)
        total = jnp.dot(weights.astype(BF16), keys[...], preferred_element_type=F32)
        if started:
            factor = jnp.exp2(old_top - top)
            denominator = denominator + sum_in[number][:, :1] * factor
            total = total + total_in[number] * factor
        if not final:
            outs[0][number] = total
            outs[1][number] = jnp.broadcast_to(top, (rows, 128))
            outs[2][number] = jnp.broadcast_to(denominator, (rows, 128))
            continue
        out = outs[number]
        out[:rows, :] = (total / denominator).astype(BF16)
        level = top + jnp.log2(denominator)
        row = lax.broadcasted_iota(jnp.int32, (rows, channels), 0)
        lane = lax.broadcasted_iota(jnp.int32, (rows, channels), 1)
        level = jnp.sum(jnp.where(row == lane, level, 0.0), axis=0, keepdims=True)
        high = level.astype(BF16).astype(F32)
        middle = (level - high).astype(BF16).astype(F32)
        low = level - high - middle
        row = lax.broadcasted_iota(jnp.int32, (STAT_ROWS, channels), 0)
        stats = jnp.where(row == 0, high, jnp.where(row == 1, middle, jnp.where(row == 2, low, 0.0)))
        out[rows:, :] = stats.astype(BF16)


def merge_body(part0, part1, part2, part3, shift, hidden, weight, bias, out_weight, out_bias, mixed):
    rows, channels = hidden.shape
    row = lax.broadcasted_iota(jnp.int32, (rows, channels), 0)
    lane = lax.broadcasted_iota(jnp.int32, (rows, channels), 1)
    parts = (part0, part1, part2, part3)
    levels = []
    for part in parts:
        stats = part[rows:, :].astype(F32)
        level = stats[0:1] + stats[1:2] + stats[2:3]
        level = jnp.sum(jnp.where(row == lane, level, 0.0), axis=1, keepdims=True)
        levels.append(level + shift[...])
    top = functools.reduce(jnp.maximum, levels)
    shares = [jnp.exp2(level - top) for level in levels]
    inverse = 1.0 / sum(shares)
    total = sum(share * inverse * part[:rows, :].astype(F32) for share, part in zip(shares, parts))
    attended = jnp.dot(
        total.astype(BF16), weight[:, 2 * channels :], preferred_element_type=F32
    ) + bias[:, 2 * channels :]
    result = jnp.dot(attended.astype(BF16), out_weight[...], preferred_element_type=F32)
    result = result + out_bias[...] + hidden[...].astype(F32)
    mixed[...] = result.astype(BF16)


def along_y(x, by):
    pairs = [
        (z * GROUP + y, z * GROUP + (y + by) % GROUP) for z in range(RING) for y in range(GROUP)
    ]
    return lax.ppermute(x, "strip", pairs)


def along_z(x, by):
    pairs = [
        (z * GROUP + y, (z + by) % RING * GROUP + y) for z in range(RING) for y in range(GROUP)
    ]
    return lax.ppermute(x, "strip", pairs)


def local(
    feature,
    frame_cache,
    norm_gain,
    conv_weight,
    conv_bias,
    attn_gain,
    qkv_weight,
    qkv_bias,
    out_weight,
    out_bias,
):
    _, height, width, channels = feature.shape
    rows = height * width
    half = rows // 2
    feat = feature[0]
    frame = lax.axis_index("tm")
    gain = norm_gain.reshape(1, channels)
    weight = conv_weight.reshape(3, 3, 3 * channels, channels)
    qkv_bias = qkv_bias.reshape(1, 3 * channels)

    cache = lax.dynamic_index_in_dim(
        frame_cache, jnp.where(frame == FRAMES - 2, 0, 1), 0, keepdims=False
    )
    down = [(s, s + 1) for s in range(ROW_STRIPS - 1)]
    up = [(s + 1, s) for s in range(ROW_STRIPS - 1)]
    above = lax.ppermute(jnp.stack([feat[height - 1], cache[height - 1]]), "strip", down)
    below = lax.ppermute(jnp.stack([feat[0], cache[0]]), "strip", up)

    flops = 2 * rows * 3 * channels * channels
    frame_number = frame.reshape(1).astype(jnp.int32)
    two_local, one_local, own_local = call(
        conv_local_body,
        "conv_local",
        [((rows, channels), F32)] * 3,
        [SMEM, VMEM, VMEM, VMEM, ANY],
        6 * flops,
        [
            pltpu.VMEM((2, rows, 3 * channels), BF16),
            pltpu.VMEM((3, 3, 3 * channels, channels), BF16),
            pltpu.SemaphoreType.DMA((3, 3)),
        ],
    )(frame_number, feat, cache, gain, weight)
    two_later, one_later = call(
        conv_edges_body,
        "conv_edges",
        [((rows, channels), BF16)] * 2,
        [SMEM] + [VMEM] * 6,
        2 * flops,
        [pltpu.VMEM((2, rows, 3 * channels), BF16)],
    )(frame_number, above, below, gain, weight, two_local, one_local)
    two = lax.ppermute(two_later, "tm", [(f, (f + 2) % FRAMES) for f in range(FRAMES)])
    one = lax.ppermute(one_later, "tm", [(f, (f + 1) % FRAMES) for f in range(FRAMES)])
    (own,) = call(
        conv_own_body,
        "conv_own",
        [((rows, channels), F32)],
        [VMEM] * 5,
        flops,
        [pltpu.VMEM((rows, 3 * channels), BF16)],
    )(above, below, gain, weight, own_local)
    hidden, normed = call(
        hidden_body,
        "hidden",
        [((rows, channels), BF16)] * 2,
        [VMEM] * 6,
        rows * channels * 20,
    )(feat, own, one, two, conv_bias.reshape(1, channels), attn_gain.reshape(1, channels))
    query, shift = call(
        query_body,
        "query",
        [((rows, channels), BF16), ((rows, 1), F32)],
        [VMEM] * 3,
        4 * rows * channels * channels,
    )(normed, qkv_weight, qkv_bias)
    queries = [query] + [along_y(query, -by) for by in range(1, GROUP)]

    def attend(name, pieces, state, final):
        if final:
            outs = [((rows + STAT_ROWS, channels), BF16)] * GROUP
        else:
            outs = [((GROUP, rows, channels), F32)] + [((GROUP, rows, 128), F32)] * 2
        keys = sum(piece.shape[0] for piece in pieces)
        return call(
            functools.partial(attend_body, len(pieces), bool(state), final),
            name,
            outs,
            [VMEM] * (GROUP + len(pieces) + len(state)),
            4 * GROUP * rows * keys * channels,
            [pltpu.VMEM((keys, channels), BF16)],
        )(*queries, *pieces, *state)

    forward, backward = along_z(normed, 1), along_z(normed, -1)
    pieces, state = [normed, forward, backward], ()
    for step in range(2):
        state = attend(f"attend_{step}", pieces, state, False)
        forward, backward = along_z(forward, 1), along_z(backward, -1)
        pieces = [forward, backward]
        if step == 0:
            forward, backward, *state = lax.optimization_barrier((forward, backward, *state))
    forward, backward, *state = lax.optimization_barrier((forward, backward, *state))
    last = [along_z(forward[:half], 1), along_z(backward[half:], -1)]
    state = attend("attend_2", pieces, state, False)
    parts = attend("attend_3", last, state, True)
    arrived = [along_y(parts[by], by) for by in range(1, GROUP)]
    (mixed,) = call(
        merge_body,
        "merge",
        [((rows, channels), BF16)],
        [VMEM] * 10,
        4 * rows * channels * channels,
    )(parts[0], *arrived, shift, hidden, qkv_weight, qkv_bias, out_weight, out_bias.reshape(1, channels))
    return mixed.reshape(feature.shape)


def solution(mesh):
    in_specs = (P("tm", "strip", None, None), P(None, "strip", None, None)) + (P(),) * 8
    out_specs = P("tm", "strip", None, None)
    return jax.shard_map(local, mesh=mesh, in_specs=in_specs, out_specs=out_specs, check_vma=False)
```

```python
import functools
import math

import jax
import jax.numpy as jnp
from jax import lax
from jax.experimental import pallas as pl
from jax.experimental.pallas import tpu as pltpu
from jax.sharding import PartitionSpec as P

EPSILON = 1e-06
FRAMES = 8
ROW_STRIPS = 32
RING = 8
GROUP = 4
STAT_ROWS = 16
BLOCKS = 2
VMEM = pl.BlockSpec(memory_space=pltpu.VMEM)
SMEM = pl.BlockSpec(memory_space=pltpu.SMEM)
HBM = pl.BlockSpec(memory_space=pltpu.HBM)
F32 = jnp.float32
BF16 = jnp.bfloat16
VMEM_LIMIT = 16 << 20
WEIGHT_LIMIT = 52 << 20


def call(body, name, outs, in_specs, flops, scratch=(), limit=VMEM_LIMIT):
    return pl.pallas_call(
        body,
        name=name,
        out_shape=[jax.ShapeDtypeStruct(*out) for out in outs],
        in_specs=in_specs,
        out_specs=[VMEM] * len(outs),
        scratch_shapes=list(scratch),
        cost_estimate=pl.CostEstimate(flops=int(flops), bytes_accessed=2 << 20, transcendentals=0),
        compiler_params=pltpu.CompilerParams(vmem_limit_bytes=limit),
    )


def rms_scaled(values, gain):
    mean_square = jnp.mean(values * values, axis=-1, keepdims=True)
    return values * lax.rsqrt(mean_square + EPSILON) * gain


def activate(row, gain):
    u = rms_scaled(row.astype(F32), gain)
    return u / (1.0 + jnp.exp(-u))


def put_columns(target, place, row):
    width, channels = row.shape
    column = lax.broadcasted_iota(jnp.int32, row.shape, 0)
    left = jnp.where(column == 0, 0.0, pltpu.roll(row, 1, 0))
    right = jnp.where(column == width - 1, 0.0, pltpu.roll(row, width - 1, 0))
    rows = pl.ds(place * width, width)
    target[rows, 0:channels] = left.astype(BF16)
    target[rows, channels : 2 * channels] = row.astype(BF16)
    target[rows, 2 * channels : 3 * channels] = right.astype(BF16)


def conv_local_body(frame, feat, cache, gain, weight, two_later, one_later, own,
                    columns, held, sems):
    width = feat.shape[1]
    copies = {}
    for frame_tap in range(3):
        for row_tap in (1, 0, 2):
            place = frame_tap, row_tap
            copies[place] = pltpu.make_async_copy(weight.at[place], held.at[place], sems.at[place])
            copies[place].start()
    for row in range(2):
        put_columns(columns.at[0], row, activate(feat[row], gain[...]))

    @pl.when(frame[0] >= FRAMES - 2)
    def _():
        for row in range(2):
            put_columns(columns.at[1], row, cache[row].astype(F32))

    for frame_tap, out in ((0, two_later), (1, one_later), (2, own)):
        if frame_tap < 2:
            source = columns.at[jnp.where(frame[0] >= FRAMES - 2 + frame_tap, 1, 0)]
        else:
            source = columns.at[0]
        copies[frame_tap, 1].wait()
        out[...] = jnp.dot(source[...], held[frame_tap, 1], preferred_element_type=F32)
        for side in range(2):
            copies[frame_tap, 2 * side].wait()
            out[pl.ds((1 - side) * width, width), :] += jnp.dot(
                source[side * width : (side + 1) * width, :],
                held[frame_tap, 2 * side],
                preferred_element_type=F32,
            )


def fetch_outer_taps(frame_taps, weight, held, sems):
    copies = {}
    for frame_tap in frame_taps:
        for side in range(2):
            copies[frame_tap, side] = pltpu.make_async_copy(
                weight.at[frame_tap, 2 * side],
                held.at[frame_tap - frame_taps[0], side],
                sems.at[frame_tap - frame_taps[0], side],
            )
            copies[frame_tap, side].start()
    return copies


def conv_edges_body(frame, above, below, gain, weight, two_local, one_local, two_later, one_later,
                    columns, held, sems):
    width = above.shape[1]
    copies = fetch_outer_taps((0, 1), weight, held, sems)

    @pl.when(frame[0] < FRAMES - 1)
    def _():
        put_columns(columns.at[0], 0, activate(above[0], gain[...]))
        put_columns(columns.at[0], 1, activate(below[0], gain[...]))

    @pl.when(frame[0] >= FRAMES - 2)
    def _():
        put_columns(columns.at[1], 0, above[1].astype(F32))
        put_columns(columns.at[1], 1, below[1].astype(F32))

    for frame_tap, start, out in ((0, two_local, two_later), (1, one_local, one_later)):
        source = columns.at[jnp.where(frame[0] >= FRAMES - 2 + frame_tap, 1, 0)]
        for side in range(2):
            copies[frame_tap, side].wait()
            rows = pl.ds(side * width, width)
            product = jnp.dot(
                source[side * width : (side + 1) * width, :],
                held[frame_tap, side],
                preferred_element_type=F32,
            )
            out[rows, :] = (start[rows, :] + product).astype(BF16)


def conv_own_body(above, below, gain, weight, own_local, own, columns, held, sems):
    width = above.shape[1]
    copies = fetch_outer_taps((2,), weight, held, sems)
    for side, halo in enumerate((above, below)):
        put_columns(columns, side, activate(halo[0], gain[...]))
        rows = pl.ds(side * width, width)
        copies[2, side].wait()
        product = jnp.dot(
            columns[side * width : (side + 1) * width, :],
            held[0, side],
            preferred_element_type=F32,
        )
        own[rows, :] = own_local[rows, :] + product


def hidden_body(feat, own, one, two, bias, gain, hidden, normed):
    values = feat[...].astype(F32).reshape(own.shape)
    branch = own[...] + one[...].astype(F32) + two[...].astype(F32) + bias[...]
    result = (values + branch).astype(BF16)
    hidden[...] = result
    normed[...] = rms_scaled(result.astype(F32), gain[...]).astype(BF16)


def query_body(normed, weight, bias, query, shift):
    channels = normed.shape[1]
    scale = math.log2(math.e) / math.sqrt(channels)
    q = jnp.dot(normed[...], weight[:, :channels], preferred_element_type=F32) + bias[:, :channels]
    q = q.astype(BF16)
    absorbed = lax.dot_general(
        q, weight[:, channels : 2 * channels], (((1,), (1,)), ((), ())), preferred_element_type=F32
    )
    query[...] = (absorbed * scale).astype(BF16)
    key_bias = bias[:, channels : 2 * channels]
    shift[...] = jnp.sum(q.astype(F32) * key_bias, axis=-1, keepdims=True) * scale


def attend_body(chunks, first, final, *refs):
    count = GROUP if first else 1
    given, refs = refs[:count], refs[count:]
    pieces, refs = refs[:chunks], refs[chunks:]
    if not first:
        (total_in, top_in, sum_in), refs = refs[:3], refs[3:]
    outs, keys = refs[:-1], refs[-1]
    if first:
        queries = outs[3]
        strip = given[0].shape[0]
        for number, query in enumerate(given):
            queries[number * strip : (number + 1) * strip, :] = query[...]
    else:
        queries = given[0]
    start = 0
    for piece in pieces:
        keys[start : start + piece.shape[0], :] = piece[...]
        start += piece.shape[0]
    channels = queries.shape[1]
    strip = queries.shape[0] // GROUP
    rows = queries.shape[0] // BLOCKS
    blocks = [slice(block * rows, (block + 1) * rows) for block in range(BLOCKS)]
    scores = [
        lax.dot_general(
            queries[block, :], keys[...], (((1,), (1,)), ((), ())), preferred_element_type=F32
        )
        for block in blocks
    ]
    for number, block in enumerate(blocks):
        top = jnp.max(scores[number], axis=1, keepdims=True)
        if not first:
            old_top = top_in[block, :1]
            top = jnp.maximum(top, old_top)
        weights = jnp.exp2(scores[number] - top)
        denominator = jnp.sum(weights, axis=1, keepdims=True)
        total = jnp.dot(weights.astype(BF16), keys[...], preferred_element_type=F32)
        if not first:
            factor = jnp.exp2(old_top - top)
            denominator = denominator + sum_in[block, :1] * factor
            total = total + total_in[block, :] * factor
        if not final:
            outs[0][block, :] = total
            outs[1][block, :] = jnp.broadcast_to(top, (rows, 128))
            outs[2][block, :] = jnp.broadcast_to(denominator, (rows, 128))
            continue
        mean = (total / denominator).astype(BF16)
        levels = top + jnp.log2(denominator)
        row = lax.broadcasted_iota(jnp.int32, (strip, channels), 0)
        lane = lax.broadcasted_iota(jnp.int32, (strip, channels), 1)
        for part in range(rows // strip):
            inside = slice(part * strip, (part + 1) * strip)
            out = outs[number * (rows // strip) + part]
            out[:strip, :] = mean[inside]
            level = jnp.sum(jnp.where(row == lane, levels[inside], 0.0), axis=0, keepdims=True)
            high = level.astype(BF16).astype(F32)
            middle = (level - high).astype(BF16).astype(F32)
            low = level - high - middle
            stat = lax.broadcasted_iota(jnp.int32, (STAT_ROWS, channels), 0)
            stats = jnp.where(stat == 0, high, jnp.where(stat == 1, middle, jnp.where(stat == 2, low, 0.0)))
            out[strip:, :] = stats.astype(BF16)


def merge_body(part0, part1, part2, part3, shift, hidden, weight, bias, out_weight, out_bias, mixed):
    rows, channels = hidden.shape
    row = lax.broadcasted_iota(jnp.int32, (rows, channels), 0)
    lane = lax.broadcasted_iota(jnp.int32, (rows, channels), 1)
    parts = (part0, part1, part2, part3)
    levels = []
    for part in parts:
        stats = part[rows:, :].astype(F32)
        level = stats[0:1] + stats[1:2] + stats[2:3]
        level = jnp.sum(jnp.where(row == lane, level, 0.0), axis=1, keepdims=True)
        levels.append(level + shift[...])
    top = functools.reduce(jnp.maximum, levels)
    shares = [jnp.exp2(level - top) for level in levels]
    inverse = 1.0 / sum(shares)
    total = sum(share * inverse * part[:rows, :].astype(F32) for share, part in zip(shares, parts))
    attended = jnp.dot(
        total.astype(BF16), weight[:, 2 * channels :], preferred_element_type=F32
    ) + bias[:, 2 * channels :]
    result = jnp.dot(attended.astype(BF16), out_weight[...], preferred_element_type=F32)
    result = result + out_bias[...] + hidden[...].astype(F32)
    mixed[...] = result.astype(BF16)


def along_y(x, by):
    pairs = [
        (z * GROUP + y, z * GROUP + (y + by) % GROUP) for z in range(RING) for y in range(GROUP)
    ]
    return lax.ppermute(x, "strip", pairs)


def along_z(x, by):
    pairs = [
        (z * GROUP + y, (z + by) % RING * GROUP + y) for z in range(RING) for y in range(GROUP)
    ]
    return lax.ppermute(x, "strip", pairs)


def local(
    feature,
    frame_cache,
    norm_gain,
    conv_weight,
    conv_bias,
    attn_gain,
    qkv_weight,
    qkv_bias,
    out_weight,
    out_bias,
):
    _, height, width, channels = feature.shape
    rows = height * width
    half = rows // 2
    feat = feature[0]
    frame = lax.axis_index("tm")
    gain = norm_gain.reshape(1, channels)
    weight = conv_weight.reshape(3, 3, 3 * channels, channels)
    qkv_bias = qkv_bias.reshape(1, 3 * channels)

    cache = lax.dynamic_index_in_dim(
        frame_cache, jnp.where(frame == FRAMES - 2, 0, 1), 0, keepdims=False
    )
    down = [(s, s + 1) for s in range(ROW_STRIPS - 1)]
    up = [(s + 1, s) for s in range(ROW_STRIPS - 1)]
    above = lax.ppermute(jnp.stack([feat[height - 1], cache[height - 1]]), "strip", down)
    below = lax.ppermute(jnp.stack([feat[0], cache[0]]), "strip", up)

    flops = 2 * rows * 3 * channels * channels
    frame_number = frame.reshape(1).astype(jnp.int32)
    two_local, one_local, own_local = call(
        conv_local_body,
        "conv_local",
        [((rows, channels), F32)] * 3,
        [SMEM, VMEM, VMEM, VMEM, HBM],
        6 * flops,
        [
            pltpu.VMEM((2, rows, 3 * channels), BF16),
            pltpu.VMEM((3, 3, 3 * channels, channels), BF16),
            pltpu.SemaphoreType.DMA((3, 3)),
        ],
        WEIGHT_LIMIT,
    )(frame_number, feat, cache, gain, weight)
    two_later, one_later = call(
        conv_edges_body,
        "conv_edges",
        [((rows, channels), BF16)] * 2,
        [SMEM, VMEM, VMEM, VMEM, HBM, VMEM, VMEM],
        2 * flops,
        [
            pltpu.VMEM((2, rows, 3 * channels), BF16),
            pltpu.VMEM((2, 2, 3 * channels, channels), BF16),
            pltpu.SemaphoreType.DMA((2, 2)),
        ],
        WEIGHT_LIMIT,
    )(frame_number, above, below, gain, weight, two_local, one_local)
    two = lax.ppermute(two_later, "tm", [(f, (f + 2) % FRAMES) for f in range(FRAMES)])
    one = lax.ppermute(one_later, "tm", [(f, (f + 1) % FRAMES) for f in range(FRAMES)])
    (own,) = call(
        conv_own_body,
        "conv_own",
        [((rows, channels), F32)],
        [VMEM, VMEM, VMEM, HBM, VMEM],
        flops,
        [
            pltpu.VMEM((rows, 3 * channels), BF16),
            pltpu.VMEM((1, 2, 3 * channels, channels), BF16),
            pltpu.SemaphoreType.DMA((1, 2)),
        ],
        WEIGHT_LIMIT,
    )(above, below, gain, weight, own_local)
    hidden, normed = call(
        hidden_body,
        "hidden",
        [((rows, channels), BF16)] * 2,
        [VMEM] * 6,
        rows * channels * 20,
    )(feat, own, one, two, conv_bias.reshape(1, channels), attn_gain.reshape(1, channels))
    query, shift = call(
        query_body,
        "query",
        [((rows, channels), BF16), ((rows, 1), F32)],
        [VMEM] * 3,
        4 * rows * channels * channels,
    )(normed, qkv_weight, qkv_bias)

    def attend(name, given, pieces, state, final):
        if final:
            outs = [((rows + STAT_ROWS, channels), BF16)] * GROUP
        else:
            outs = [((GROUP * rows, channels), F32)] + [((GROUP * rows, 128), F32)] * 2
        if not state:
            outs.append(((GROUP * rows, channels), BF16))
        keys = sum(piece.shape[0] for piece in pieces)
        return call(
            functools.partial(attend_body, len(pieces), not state, final),
            name,
            outs,
            [VMEM] * (len(given) + len(pieces) + len(state)),
            4 * GROUP * rows * keys * channels,
            [pltpu.VMEM((keys, channels), BF16)],
            32 << 20,
        )(*given, *pieces, *state)

    forward, backward = [normed], [normed]
    queries = [query] + [along_y(query, -by) for by in range(1, GROUP)]
    for step in range(3):
        forward.append(along_z(forward[-1], 1))
        backward.append(along_z(backward[-1], -1))
        if step == 0:
            forward[1], backward[1], _ = lax.optimization_barrier(
                (forward[1], backward[1], query)
            )
    *state, query_rows = attend("attend_near", queries, forward[:3] + backward[1:3], [], False)
    forward[3], backward[3], *state = lax.optimization_barrier((forward[3], backward[3], *state))
    last = [along_z(forward[3][:half], 1), along_z(backward[3][half:], -1)]
    state = attend("attend_far", [query_rows], [forward[3], backward[3]], state, False)
    parts = attend("attend_last", [query_rows], last, state, True)
    arrived = [along_y(parts[by], by) for by in range(1, GROUP)]
    (mixed,) = call(
        merge_body,
        "merge",
        [((rows, channels), BF16)],
        [VMEM] * 10,
        4 * rows * channels * channels,
    )(parts[0], *arrived, shift, hidden, qkv_weight, qkv_bias, out_weight, out_bias.reshape(1, channels))
    return mixed.reshape(feature.shape)


def solution(mesh):
    in_specs = (P("tm", "strip", None, None), P(None, "strip", None, None)) + (P(),) * 8
    out_specs = P("tm", "strip", None, None)
    return jax.shard_map(local, mesh=mesh, in_specs=in_specs, out_specs=out_specs, check_vma=False)
```

```python
import functools
import math

import jax
import jax.numpy as jnp
from jax import lax
from jax.experimental import pallas as pl
from jax.experimental.pallas import tpu as pltpu
from jax.sharding import PartitionSpec as P

EPSILON = 1e-06
FRAMES = 8
ROW_STRIPS = 32
RING = 8
GROUP = 4
STAT_ROWS = 16
LANES = 128
BLOCKS = 2
VMEM = pl.BlockSpec(memory_space=pltpu.VMEM)
SMEM = pl.BlockSpec(memory_space=pltpu.SMEM)
HBM = pl.BlockSpec(memory_space=pltpu.HBM)
F32 = jnp.float32
BF16 = jnp.bfloat16
VMEM_LIMIT = 16 << 20
WEIGHT_LIMIT = 52 << 20


def call(body, name, outs, in_specs, flops, scratch=(), limit=VMEM_LIMIT):
    return pl.pallas_call(
        body,
        name=name,
        out_shape=[jax.ShapeDtypeStruct(*out) for out in outs],
        in_specs=in_specs,
        out_specs=[VMEM] * len(outs),
        scratch_shapes=list(scratch),
        cost_estimate=pl.CostEstimate(flops=int(flops), bytes_accessed=2 << 20, transcendentals=0),
        compiler_params=pltpu.CompilerParams(vmem_limit_bytes=limit),
    )


def rms_scaled(values, gain):
    mean_square = jnp.mean(values * values, axis=-1, keepdims=True)
    return values * lax.rsqrt(mean_square + EPSILON) * gain


def activate(row, gain):
    u = rms_scaled(row.astype(F32), gain)
    return u / (1.0 + jnp.exp(-u))


def put_columns(target, place, row):
    width, channels = row.shape
    column = lax.broadcasted_iota(jnp.int32, row.shape, 0)
    left = jnp.where(column == 0, 0.0, pltpu.roll(row, 1, 0))
    right = jnp.where(column == width - 1, 0.0, pltpu.roll(row, width - 1, 0))
    rows = pl.ds(place * width, width)
    target[rows, 0:channels] = left.astype(BF16)
    target[rows, channels : 2 * channels] = row.astype(BF16)
    target[rows, 2 * channels : 3 * channels] = right.astype(BF16)


def conv_local_body(frame, feat, cache, gain, weight, two_later, one_later, own,
                    columns, held, sems):
    width = feat.shape[1]
    copies = {}
    for frame_tap in range(3):
        for row_tap in (1, 0, 2):
            place = frame_tap, row_tap
            copies[place] = pltpu.make_async_copy(weight.at[place], held.at[place], sems.at[place])
            copies[place].start()
    for row in range(2):
        put_columns(columns.at[0], row, activate(feat[row], gain[...]))

    @pl.when(frame[0] >= FRAMES - 2)
    def _():
        for row in range(2):
            put_columns(columns.at[1], row, cache[row].astype(F32))

    for frame_tap, out in ((0, two_later), (1, one_later), (2, own)):
        if frame_tap < 2:
            source = columns.at[jnp.where(frame[0] >= FRAMES - 2 + frame_tap, 1, 0)]
        else:
            source = columns.at[0]
        copies[frame_tap, 1].wait()
        out[...] = jnp.dot(source[...], held[frame_tap, 1], preferred_element_type=F32)
        for side in range(2):
            copies[frame_tap, 2 * side].wait()
            out[pl.ds((1 - side) * width, width), :] += jnp.dot(
                source[side * width : (side + 1) * width, :],
                held[frame_tap, 2 * side],
                preferred_element_type=F32,
            )


def fetch_outer_taps(frame_taps, weight, held, sems):
    copies = {}
    for frame_tap in frame_taps:
        for side in range(2):
            copies[frame_tap, side] = pltpu.make_async_copy(
                weight.at[frame_tap, 2 * side],
                held.at[frame_tap - frame_taps[0], side],
                sems.at[frame_tap - frame_taps[0], side],
            )
            copies[frame_tap, side].start()
    return copies


def conv_edges_body(frame, above, below, gain, weight, two_local, one_local, two_later, one_later,
                    columns, held, sems):
    width = above.shape[1]
    copies = fetch_outer_taps((0, 1), weight, held, sems)

    @pl.when(frame[0] < FRAMES - 1)
    def _():
        put_columns(columns.at[0], 0, activate(above[0], gain[...]))
        put_columns(columns.at[0], 1, activate(below[0], gain[...]))

    @pl.when(frame[0] >= FRAMES - 2)
    def _():
        put_columns(columns.at[1], 0, above[1].astype(F32))
        put_columns(columns.at[1], 1, below[1].astype(F32))

    for frame_tap, start, out in ((0, two_local, two_later), (1, one_local, one_later)):
        source = columns.at[jnp.where(frame[0] >= FRAMES - 2 + frame_tap, 1, 0)]
        for side in range(2):
            copies[frame_tap, side].wait()
            rows = pl.ds(side * width, width)
            product = jnp.dot(
                source[side * width : (side + 1) * width, :],
                held[frame_tap, side],
                preferred_element_type=F32,
            )
            out[rows, :] = (start[rows, :] + product).astype(BF16)


def conv_own_body(above, below, gain, weight, own_local, own, columns, held, sems):
    width = above.shape[1]
    copies = fetch_outer_taps((2,), weight, held, sems)
    for side, halo in enumerate((above, below)):
        put_columns(columns, side, activate(halo[0], gain[...]))
        rows = pl.ds(side * width, width)
        copies[2, side].wait()
        product = jnp.dot(
            columns[side * width : (side + 1) * width, :],
            held[0, side],
            preferred_element_type=F32,
        )
        own[rows, :] = own_local[rows, :] + product


def hidden_body(feat, own, one, two, bias, gain, hidden, normed):
    values = feat[...].astype(F32).reshape(own.shape)
    branch = own[...] + one[...].astype(F32) + two[...].astype(F32) + bias[...]
    result = (values + branch).astype(BF16)
    hidden[...] = result
    normed[...] = rms_scaled(result.astype(F32), gain[...]).astype(BF16)


def query_body(normed, weight, bias, query, shift):
    channels = normed.shape[1]
    scale = math.log2(math.e) / math.sqrt(channels)
    q = jnp.dot(normed[...], weight[:, :channels], preferred_element_type=F32) + bias[:, :channels]
    q = q.astype(BF16)
    absorbed = lax.dot_general(
        q, weight[:, channels : 2 * channels], (((1,), (1,)), ((), ())), preferred_element_type=F32
    )
    query[...] = (absorbed * scale).astype(BF16)
    key_bias = bias[:, channels : 2 * channels]
    shift[...] = jnp.sum(q.astype(F32) * key_bias, axis=-1, keepdims=True) * scale


def widen(lanes, width):
    return jnp.concatenate([lanes] * (-(-width // LANES)), axis=1)[:, :width]


def attend_body(chunks, first, strips, *refs):
    count = GROUP if first else 1
    given, refs = refs[:count], refs[count:]
    pieces, refs = refs[:chunks], refs[chunks:]
    if not first:
        (total_in, top_in), refs = refs[:2], refs[2:]
    outs, keys = refs[:-1], refs[-1]
    channels = pieces[0].shape[1]
    if first:
        queries = outs[2]
        strip = given[0].shape[0]
        for number, query in enumerate(given):
            queries[number * strip : (number + 1) * strip, :] = query[...]
    else:
        queries = given[0]
    strip = queries.shape[0] // GROUP
    start = 0
    for piece in pieces:
        keys[start : start + piece.shape[0], :channels] = piece[...]
        start += piece.shape[0]
    keys[:, channels:] = jnp.ones((start, LANES), BF16)
    if strips:
        blocks = [slice(number * strip, (number + 1) * strip) for number in strips]
    else:
        rows = queries.shape[0] // BLOCKS
        blocks = [slice(block * rows, (block + 1) * rows) for block in range(BLOCKS)]
    for number, block in enumerate(blocks):
        scores = lax.dot_general(
            queries[block, :], keys[:, :channels], (((1,), (1,)), ((), ())),
            preferred_element_type=F32,
        )
        top = jnp.broadcast_to(jnp.max(scores, axis=1, keepdims=True), (scores.shape[0], LANES))
        if not first:
            old_top = top_in[block, :]
            top = jnp.maximum(top, old_top)
        weights = jnp.exp2(scores - widen(top, start)).astype(BF16)
        total = jnp.dot(weights, keys[...], preferred_element_type=F32)
        if not first:
            factor = jnp.exp2(old_top - top)
            total = total + total_in[block, :] * widen(factor, channels + LANES)
        if not strips:
            outs[0][block, :] = total
            outs[1][block, :] = top
            continue
        out = outs[number]
        denominator = total[:, channels:]
        out[:strip, :] = (total[:, :channels] * widen(1.0 / denominator, channels)).astype(BF16)
        row = lax.broadcasted_iota(jnp.int32, (strip, channels), 0)
        lane = lax.broadcasted_iota(jnp.int32, (strip, channels), 1)
        level = widen(top + jnp.log2(denominator), channels)
        level = jnp.sum(jnp.where(row == lane, level, 0.0), axis=0, keepdims=True)
        high = level.astype(BF16).astype(F32)
        middle = (level - high).astype(BF16).astype(F32)
        low = level - high - middle
        stat = lax.broadcasted_iota(jnp.int32, (STAT_ROWS, channels), 0)
        stats = jnp.where(stat == 0, high, jnp.where(stat == 1, middle, jnp.where(stat == 2, low, 0.0)))
        out[strip:, :] = stats.astype(BF16)


def merge_body(part0, part1, part2, part3, shift, hidden, weight, bias, out_weight, out_bias, mixed):
    rows, channels = hidden.shape
    row = lax.broadcasted_iota(jnp.int32, (rows, channels), 0)
    lane = lax.broadcasted_iota(jnp.int32, (rows, channels), 1)
    parts = (part0, part1, part2, part3)
    levels = []
    for part in parts:
        stats = part[rows:, :].astype(F32)
        level = stats[0:1] + stats[1:2] + stats[2:3]
        level = jnp.sum(jnp.where(row == lane, level, 0.0), axis=1, keepdims=True)
        levels.append(level + shift[...])
    top = functools.reduce(jnp.maximum, levels)
    shares = [jnp.exp2(level - top) for level in levels]
    inverse = 1.0 / sum(shares)
    total = sum(share * inverse * part[:rows, :].astype(F32) for share, part in zip(shares, parts))
    attended = jnp.dot(
        total.astype(BF16), weight[:, 2 * channels :], preferred_element_type=F32
    ) + bias[:, 2 * channels :]
    result = jnp.dot(attended.astype(BF16), out_weight[...], preferred_element_type=F32)
    result = result + out_bias[...] + hidden[...].astype(F32)
    mixed[...] = result.astype(BF16)


def along_y(x, by):
    pairs = [
        (z * GROUP + y, z * GROUP + (y + by) % GROUP) for z in range(RING) for y in range(GROUP)
    ]
    return lax.ppermute(x, "strip", pairs)


def along_z(x, by):
    pairs = [
        (z * GROUP + y, (z + by) % RING * GROUP + y) for z in range(RING) for y in range(GROUP)
    ]
    return lax.ppermute(x, "strip", pairs)


def local(
    feature,
    frame_cache,
    norm_gain,
    conv_weight,
    conv_bias,
    attn_gain,
    qkv_weight,
    qkv_bias,
    out_weight,
    out_bias,
):
    _, height, width, channels = feature.shape
    rows = height * width
    half = rows // 2
    feat = feature[0]
    frame = lax.axis_index("tm")
    gain = norm_gain.reshape(1, channels)
    weight = conv_weight.reshape(3, 3, 3 * channels, channels)
    qkv_bias = qkv_bias.reshape(1, 3 * channels)

    cache = lax.dynamic_index_in_dim(
        frame_cache, jnp.where(frame == FRAMES - 2, 0, 1), 0, keepdims=False
    )
    down = [(s, s + 1) for s in range(ROW_STRIPS - 1)]
    up = [(s + 1, s) for s in range(ROW_STRIPS - 1)]
    above = lax.ppermute(jnp.stack([feat[height - 1], cache[height - 1]]), "strip", down)
    below = lax.ppermute(jnp.stack([feat[0], cache[0]]), "strip", up)

    flops = 2 * rows * 3 * channels * channels
    frame_number = frame.reshape(1).astype(jnp.int32)
    two_local, one_local, own_local = call(
        conv_local_body,
        "conv_local",
        [((rows, channels), F32)] * 3,
        [SMEM, VMEM, VMEM, VMEM, HBM],
        6 * flops,
        [
            pltpu.VMEM((2, rows, 3 * channels), BF16),
            pltpu.VMEM((3, 3, 3 * channels, channels), BF16),
            pltpu.SemaphoreType.DMA((3, 3)),
        ],
        WEIGHT_LIMIT,
    )(frame_number, feat, cache, gain, weight)
    two_later, one_later = call(
        conv_edges_body,
        "conv_edges",
        [((rows, channels), BF16)] * 2,
        [SMEM, VMEM, VMEM, VMEM, HBM, VMEM, VMEM],
        2 * flops,
        [
            pltpu.VMEM((2, rows, 3 * channels), BF16),
            pltpu.VMEM((2, 2, 3 * channels, channels), BF16),
            pltpu.SemaphoreType.DMA((2, 2)),
        ],
        WEIGHT_LIMIT,
    )(frame_number, above, below, gain, weight, two_local, one_local)
    two = lax.ppermute(two_later, "tm", [(f, (f + 2) % FRAMES) for f in range(FRAMES)])
    one = lax.ppermute(one_later, "tm", [(f, (f + 1) % FRAMES) for f in range(FRAMES)])
    (own,) = call(
        conv_own_body,
        "conv_own",
        [((rows, channels), F32)],
        [VMEM, VMEM, VMEM, HBM, VMEM],
        flops,
        [
            pltpu.VMEM((rows, 3 * channels), BF16),
            pltpu.VMEM((1, 2, 3 * channels, channels), BF16),
            pltpu.SemaphoreType.DMA((1, 2)),
        ],
        WEIGHT_LIMIT,
    )(above, below, gain, weight, own_local)
    hidden, normed = call(
        hidden_body,
        "hidden",
        [((rows, channels), BF16)] * 2,
        [VMEM] * 6,
        rows * channels * 20,
    )(feat, own, one, two, conv_bias.reshape(1, channels), attn_gain.reshape(1, channels))
    query, shift = call(
        query_body,
        "query",
        [((rows, channels), BF16), ((rows, 1), F32)],
        [VMEM] * 3,
        4 * rows * channels * channels,
    )(normed, qkv_weight, qkv_bias)

    def attend(name, given, pieces, state=(), strips=()):
        if strips:
            outs = [((rows + STAT_ROWS, channels), BF16)] * len(strips)
        else:
            outs = [((GROUP * rows, channels + LANES), F32), ((GROUP * rows, LANES), F32)]
        if not state:
            outs.append(((GROUP * rows, channels), BF16))
        keys = sum(piece.shape[0] for piece in pieces)
        return call(
            functools.partial(attend_body, len(pieces), not state, strips),
            name,
            outs,
            [VMEM] * (len(given) + len(pieces) + len(state)),
            4 * (len(strips) or GROUP) * rows * keys * channels,
            [pltpu.VMEM((keys, channels + LANES), BF16)],
            32 << 20,
        )(*given, *pieces, *state)

    queries = [query] + [along_y(query, -by) for by in range(1, GROUP)]
    forward, backward = [normed], [normed]
    for step in range(3):
        forward.append(along_z(forward[-1], 1))
        backward.append(along_z(backward[-1], -1))
        if step == 0:
            forward[1], backward[1], _ = lax.optimization_barrier(
                (forward[1], backward[1], query)
            )
        if step == 1:
            forward[2], backward[2], *queries = lax.optimization_barrier(
                (forward[2], backward[2], *queries)
            )
    *state, query_rows = attend("attend_near", queries, forward[:3] + backward[1:3])
    forward[3], backward[3], *state = lax.optimization_barrier((forward[3], backward[3], *state))
    last = [along_z(forward[3][:half], 1), along_z(backward[3][half:], -1)]
    state = attend("attend_far", [query_rows], [forward[3], backward[3]], state)
    parts = {}
    for strips in ((2,), (1, 3), (0,)):
        name = "attend_last_" + "_".join(map(str, strips))
        parts.update(zip(strips, attend(name, [query_rows], last, state, strips)))
    arrived = {by: along_y(parts[by], by) for by in (2, 1, 3)}
    arrived = [arrived[by] for by in range(1, GROUP)]
    (mixed,) = call(
        merge_body,
        "merge",
        [((rows, channels), BF16)],
        [VMEM] * 10,
        4 * rows * channels * channels,
    )(parts[0], *arrived, shift, hidden, qkv_weight, qkv_bias, out_weight, out_bias.reshape(1, channels))
    return mixed.reshape(feature.shape)


def solution(mesh):
    in_specs = (P("tm", "strip", None, None), P(None, "strip", None, None)) + (P(),) * 8
    out_specs = P("tm", "strip", None, None)
    return jax.shard_map(local, mesh=mesh, in_specs=in_specs, out_specs=out_specs, check_vma=False)
```

```python
import functools
import math

import jax
import jax.numpy as jnp
from jax import lax
from jax.experimental import pallas as pl
from jax.experimental.pallas import tpu as pltpu
from jax.sharding import PartitionSpec as P

EPSILON = 1e-06
FRAMES = 8
ROW_STRIPS = 32
RING = 8
GROUP = 4
STAT_ROWS = 16
LANES = 128
BLOCKS = 2
VMEM = pl.BlockSpec(memory_space=pltpu.VMEM)
SMEM = pl.BlockSpec(memory_space=pltpu.SMEM)
HBM = pl.BlockSpec(memory_space=pltpu.HBM)
F32 = jnp.float32
BF16 = jnp.bfloat16
VMEM_LIMIT = 16 << 20
WEIGHT_LIMIT = 46 << 20


def call(body, name, outs, in_specs, flops, scratch=(), limit=VMEM_LIMIT):
    return pl.pallas_call(
        body,
        name=name,
        out_shape=[jax.ShapeDtypeStruct(*out) for out in outs],
        in_specs=in_specs,
        out_specs=[VMEM] * len(outs),
        scratch_shapes=list(scratch),
        cost_estimate=pl.CostEstimate(flops=int(flops), bytes_accessed=2 << 20, transcendentals=0),
        compiler_params=pltpu.CompilerParams(vmem_limit_bytes=limit),
    )


def rms_scaled(values, gain):
    mean_square = jnp.mean(values * values, axis=-1, keepdims=True)
    return values * lax.rsqrt(mean_square + EPSILON) * gain


def activate(row, gain):
    u = rms_scaled(row.astype(F32), gain)
    return u / (1.0 + jnp.exp(-u))


def put_columns(target, place, row):
    width, channels = row.shape
    column = lax.broadcasted_iota(jnp.int32, row.shape, 0)
    left = jnp.where(column == 0, 0.0, pltpu.roll(row, 1, 0))
    right = jnp.where(column == width - 1, 0.0, pltpu.roll(row, width - 1, 0))
    rows = pl.ds(place * width, width)
    target[rows, 0:channels] = left.astype(BF16)
    target[rows, channels : 2 * channels] = row.astype(BF16)
    target[rows, 2 * channels : 3 * channels] = right.astype(BF16)


def conv_local_body(frame, feat, cache, gain, weight, two_later, one_later, own, outer,
                    columns, held, sems):
    width = feat.shape[1]
    copies, weights = {}, {}
    for frame_tap in range(3):
        for row_tap in (1, 0, 2):
            place = frame_tap, row_tap
            if frame_tap < 2 and row_tap != 1:
                weights[place] = outer.at[frame_tap, row_tap // 2]
            else:
                weights[place] = held.at[row_tap if frame_tap == 2 else 3 + frame_tap]
            copies[place] = pltpu.make_async_copy(weight.at[place], weights[place], sems.at[place])
            copies[place].start()
    scale = gain[...].reshape(1, -1)
    for row in range(2):
        put_columns(columns.at[0], row, activate(feat[row], scale))
    chosen = jnp.where(frame[0] == FRAMES - 2, 0, 1)

    @pl.when(frame[0] >= FRAMES - 2)
    def _():
        for row in range(2):
            put_columns(columns.at[1], row, cache[chosen, row].astype(F32))

    for frame_tap, out in ((0, two_later), (1, one_later), (2, own)):
        if frame_tap < 2:
            source = columns.at[jnp.where(frame[0] >= FRAMES - 2 + frame_tap, 1, 0)]
        else:
            source = columns.at[0]
        copies[frame_tap, 1].wait()
        out[...] = jnp.dot(source[...], weights[frame_tap, 1][...], preferred_element_type=F32)
        for side in range(2):
            copies[frame_tap, 2 * side].wait()
            out[pl.ds((1 - side) * width, width), :] += jnp.dot(
                source[side * width : (side + 1) * width, :],
                weights[frame_tap, 2 * side][...],
                preferred_element_type=F32,
            )


def conv_edges_body(frame_tap, frame, above, below, gain, outer, local_sum, out, columns):
    width = above.shape[1]
    scale = gain[...].reshape(1, -1)
    cached = frame[0] >= FRAMES - 2 + frame_tap

    @pl.when(cached)
    def _():
        for side, halo in enumerate((above, below)):
            put_columns(columns, side, halo[1].astype(F32))

    @pl.when(jnp.logical_not(cached))
    def _():
        for side, halo in enumerate((above, below)):
            put_columns(columns, side, activate(halo[0], scale))

    for side in range(2):
        rows = pl.ds(side * width, width)
        product = jnp.dot(
            columns[side * width : (side + 1) * width, :],
            outer[frame_tap, side],
            preferred_element_type=F32,
        )
        out[rows, :] = (local_sum[rows, :] + product).astype(BF16)


def conv_own_body(above, below, gain, weight, own_local, own, columns, held, sems):
    width = above.shape[1]
    copies = []
    for side in range(2):
        copies.append(pltpu.make_async_copy(weight.at[2, 2 * side], held.at[side], sems.at[side]))
        copies[side].start()
    scale = gain[...].reshape(1, -1)
    for side, halo in enumerate((above, below)):
        put_columns(columns, side, activate(halo[0], scale))
        rows = pl.ds(side * width, width)
        copies[side].wait()
        product = jnp.dot(
            columns[side * width : (side + 1) * width, :],
            held[side],
            preferred_element_type=F32,
        )
        own[rows, :] = own_local[rows, :] + product


def hidden_body(feat, own, one, two, bias, gain, hidden, normed):
    values = feat[...].astype(F32).reshape(own.shape)
    branch = own[...] + one[...].astype(F32) + two[...].astype(F32) + bias[...]
    result = (values + branch).astype(BF16)
    hidden[...] = result
    normed[...] = rms_scaled(result.astype(F32), gain[...]).astype(BF16)


def query_body(normed, weight, bias, query, shift):
    channels = normed.shape[1]
    scale = math.log2(math.e) / math.sqrt(channels)
    q = jnp.dot(normed[...], weight[:, :channels], preferred_element_type=F32) + bias[:, :channels]
    q = q.astype(BF16)
    absorbed = lax.dot_general(
        q, weight[:, channels : 2 * channels], (((1,), (1,)), ((), ())), preferred_element_type=F32
    )
    query[...] = (absorbed * scale).astype(BF16)
    key_bias = bias[:, channels : 2 * channels]
    shift[...] = as_row(jnp.sum(q.astype(F32) * key_bias, axis=-1, keepdims=True) * scale, channels)


def as_row(column, width):
    shape = column.shape[0], width
    row = lax.broadcasted_iota(jnp.int32, shape, 0)
    lane = lax.broadcasted_iota(jnp.int32, shape, 1)
    return jnp.sum(jnp.where(row == lane, column, 0.0), axis=0, keepdims=True)


def widen(lanes, width):
    return jnp.concatenate([lanes] * (-(-width // LANES)), axis=1)[:, :width]


def attend_body(chunks, first, strips, *refs):
    count = GROUP if first else 1
    given, refs = refs[:count], refs[count:]
    pieces, refs = refs[:chunks], refs[chunks:]
    if not first:
        (total_in, top_in), refs = refs[:2], refs[2:]
    outs, keys = refs[:-1], refs[-1]
    channels = pieces[0].shape[1]
    if first:
        queries = outs[2]
        strip = given[0].shape[0]
        for number, query in enumerate(given):
            queries[number * strip : (number + 1) * strip, :] = query[...]
    else:
        queries = given[0]
    strip = queries.shape[0] // GROUP
    start = 0
    for piece in pieces:
        keys[start : start + piece.shape[0], :channels] = piece[...]
        start += piece.shape[0]
    keys[:, channels:] = jnp.ones((start, LANES), BF16)
    if strips:
        blocks = [slice(number * strip, (number + 1) * strip) for number in strips]
    else:
        rows = queries.shape[0] // BLOCKS
        blocks = [slice(block * rows, (block + 1) * rows) for block in range(BLOCKS)]
    for number, block in enumerate(blocks):
        scores = lax.dot_general(
            queries[block, :], keys[:, :channels], (((1,), (1,)), ((), ())),
            preferred_element_type=F32,
        )
        top = jnp.broadcast_to(jnp.max(scores, axis=1, keepdims=True), (scores.shape[0], LANES))
        if not first:
            old_top = top_in[block, :]
            top = jnp.maximum(top, old_top)
        weights = jnp.exp2(scores - widen(top, start)).astype(BF16)
        total = jnp.dot(weights, keys[...], preferred_element_type=F32)
        if not first:
            factor = jnp.exp2(old_top - top)
            total = total + total_in[block, :] * widen(factor, channels + LANES)
        if not strips:
            outs[0][block, :] = total
            outs[1][block, :] = top
            continue
        out = outs[number]
        denominator = total[:, channels:]
        out[:strip, :] = (total[:, :channels] * widen(1.0 / denominator, channels)).astype(BF16)
        level = as_row(widen(top + jnp.log2(denominator), channels), channels)
        high = level.astype(BF16).astype(F32)
        middle = (level - high).astype(BF16).astype(F32)
        low = level - high - middle
        stat = lax.broadcasted_iota(jnp.int32, (STAT_ROWS, channels), 0)
        stats = jnp.where(stat == 0, high, jnp.where(stat == 1, middle, jnp.where(stat == 2, low, 0.0)))
        out[strip:, :] = stats.astype(BF16)


def merge_body(part0, part1, part2, part3, shift, hidden, weight, bias, out_weight, out_bias, mixed):
    rows, channels = hidden.shape
    parts = (part0, part1, part2, part3)
    levels = []
    for part in parts:
        stats = part[rows:, :].astype(F32)
        levels.append(stats[0:1] + stats[1:2] + stats[2:3] + shift[...])
    top = functools.reduce(jnp.maximum, levels)
    shares = [jnp.exp2(level - top) for level in levels]
    inverse = 1.0 / sum(shares)
    shares = jnp.concatenate([share * inverse for share in shares] * 2, axis=0)
    shares = jnp.transpose(shares)[:rows]
    total = sum(
        shares[:, number : number + 1] * part[:rows, :].astype(F32)
        for number, part in enumerate(parts)
    )
    attended = jnp.dot(
        total.astype(BF16), weight[:, 2 * channels :], preferred_element_type=F32
    ) + bias[:, 2 * channels :]
    result = jnp.dot(attended.astype(BF16), out_weight[...], preferred_element_type=F32)
    result = result + out_bias[...] + hidden[...].astype(F32)
    mixed[...] = result.astype(BF16)


def along_y(x, by):
    pairs = [
        (z * GROUP + y, z * GROUP + (y + by) % GROUP) for z in range(RING) for y in range(GROUP)
    ]
    return lax.ppermute(x, "strip", pairs)


def along_z(x, by):
    pairs = [
        (z * GROUP + y, (z + by) % RING * GROUP + y) for z in range(RING) for y in range(GROUP)
    ]
    return lax.ppermute(x, "strip", pairs)


def local(
    feature,
    frame_cache,
    norm_gain,
    conv_weight,
    conv_bias,
    attn_gain,
    qkv_weight,
    qkv_bias,
    out_weight,
    out_bias,
):
    _, height, width, channels = feature.shape
    rows = height * width
    half = rows // 2
    feat = feature[0]
    frame = lax.axis_index("tm")
    weight = conv_weight.reshape(3, 3, 3 * channels, channels)
    qkv_bias = qkv_bias.reshape(1, 3 * channels)

    cache = lax.dynamic_index_in_dim(
        frame_cache, jnp.where(frame == FRAMES - 2, 0, 1), 0, keepdims=False
    )
    down = [(s, s + 1) for s in range(ROW_STRIPS - 1)]
    up = [(s + 1, s) for s in range(ROW_STRIPS - 1)]
    above = lax.ppermute(jnp.stack([feat[height - 1], cache[height - 1]]), "strip", down)
    below = lax.ppermute(jnp.stack([feat[0], cache[0]]), "strip", up)

    flops = 2 * rows * 3 * channels * channels
    frame_number = frame.reshape(1).astype(jnp.int32)
    two_local, one_local, own_local, outer = call(
        conv_local_body,
        "conv_local",
        [((rows, channels), F32)] * 3 + [((2, 2, 3 * channels, channels), BF16)],
        [SMEM, VMEM, VMEM, VMEM, HBM],
        6 * flops,
        [
            pltpu.VMEM((2, rows, 3 * channels), BF16),
            pltpu.VMEM((5, 3 * channels, channels), BF16),
            pltpu.SemaphoreType.DMA((3, 3)),
        ],
        WEIGHT_LIMIT,
    )(frame_number, feat, frame_cache, norm_gain, weight)

    def conv_edges(name, frame_tap, local_sum):
        return call(
            functools.partial(conv_edges_body, frame_tap),
            name,
            [((rows, channels), BF16)],
            [SMEM] + [VMEM] * 5,
            flops,
            [pltpu.VMEM((rows, 3 * channels), BF16)],
        )(frame_number, above, below, norm_gain, outer, local_sum)[0]

    two = lax.ppermute(
        conv_edges("conv_edges_two", 0, two_local),
        "tm",
        [(f, (f + 2) % FRAMES) for f in range(FRAMES)],
    )
    one = lax.ppermute(
        conv_edges("conv_edges_one", 1, one_local),
        "tm",
        [(f, (f + 1) % FRAMES) for f in range(FRAMES)],
    )
    (own,) = call(
        conv_own_body,
        "conv_own",
        [((rows, channels), F32)],
        [VMEM, VMEM, VMEM, HBM, VMEM],
        flops,
        [
            pltpu.VMEM((rows, 3 * channels), BF16),
            pltpu.VMEM((2, 3 * channels, channels), BF16),
            pltpu.SemaphoreType.DMA((2,)),
        ],
        WEIGHT_LIMIT,
    )(above, below, norm_gain, weight, own_local)
    hidden, normed = call(
        hidden_body,
        "hidden",
        [((rows, channels), BF16)] * 2,
        [VMEM] * 6,
        rows * channels * 20,
    )(feat, own, one, two, conv_bias.reshape(1, channels), attn_gain.reshape(1, channels))
    query, shift = call(
        query_body,
        "query",
        [((rows, channels), BF16), ((1, channels), F32)],
        [VMEM] * 3,
        4 * rows * channels * channels,
    )(normed, qkv_weight, qkv_bias)

    def attend(name, given, pieces, state=(), strips=()):
        if strips:
            outs = [((rows + STAT_ROWS, channels), BF16)] * len(strips)
        else:
            outs = [((GROUP * rows, channels + LANES), F32), ((GROUP * rows, LANES), F32)]
        if not state:
            outs.append(((GROUP * rows, channels), BF16))
        keys = sum(piece.shape[0] for piece in pieces)
        return call(
            functools.partial(attend_body, len(pieces), not state, strips),
            name,
            outs,
            [VMEM] * (len(given) + len(pieces) + len(state)),
            4 * (len(strips) or GROUP) * rows * keys * channels,
            [pltpu.VMEM((keys, channels + LANES), BF16)],
            32 << 20,
        )(*given, *pieces, *state)

    queries = [query] + [along_y(query, -by) for by in range(1, GROUP)]
    forward, backward = [normed], [normed]
    for step in range(3):
        forward.append(along_z(forward[-1], 1))
        backward.append(along_z(backward[-1], -1))
        if step == 0:
            forward[1], backward[1], _ = lax.optimization_barrier(
                (forward[1], backward[1], query)
            )
        if step == 1:
            forward[2], backward[2], *queries = lax.optimization_barrier(
                (forward[2], backward[2], *queries)
            )
    *state, query_rows = attend("attend_near", queries, forward[:3] + backward[1:3])
    forward[3], backward[3], *state = lax.optimization_barrier((forward[3], backward[3], *state))
    last = [along_z(forward[3][:half], 1), along_z(backward[3][half:], -1)]
    state = attend("attend_far", [query_rows], [forward[3], backward[3]], state)
    parts = {}
    for strips in ((2,), (1, 3), (0,)):
        name = "attend_last_" + "_".join(map(str, strips))
        parts.update(zip(strips, attend(name, [query_rows], last, state, strips)))
    arrived = {by: along_y(parts[by], by) for by in (2, 1, 3)}
    arrived = [arrived[by] for by in range(1, GROUP)]
    (mixed,) = call(
        merge_body,
        "merge",
        [((rows, channels), BF16)],
        [VMEM] * 10,
        4 * rows * channels * channels,
    )(parts[0], *arrived, shift, hidden, qkv_weight, qkv_bias, out_weight, out_bias.reshape(1, channels))
    return mixed.reshape(feature.shape)


def solution(mesh):
    in_specs = (P("tm", "strip", None, None), P(None, "strip", None, None)) + (P(),) * 8
    out_specs = P("tm", "strip", None, None)
    return jax.shard_map(local, mesh=mesh, in_specs=in_specs, out_specs=out_specs, check_vma=False)
```

```python
import functools
import math

import jax
import jax.numpy as jnp
from jax import lax
from jax.experimental import pallas as pl
from jax.experimental.pallas import tpu as pltpu
from jax.sharding import PartitionSpec as P

EPSILON = 1e-06
FRAMES = 8
ROW_STRIPS = 32
RING = 8
GROUP = 4
STAT_ROWS = 16
LANES = 128
BLOCKS = 2
VMEM = pl.BlockSpec(memory_space=pltpu.VMEM)
SMEM = pl.BlockSpec(memory_space=pltpu.SMEM)
HBM = pl.BlockSpec(memory_space=pltpu.HBM)
F32 = jnp.float32
BF16 = jnp.bfloat16
VMEM_LIMIT = 16 << 20


def pinned(x):
    return pltpu.with_memory_space_constraint(x, pltpu.HBM)


def call(body, name, outs, in_specs, flops, scratch=(), limit=VMEM_LIMIT):
    return pl.pallas_call(
        body,
        name=name,
        out_shape=[jax.ShapeDtypeStruct(*out) for out in outs],
        in_specs=in_specs,
        out_specs=[VMEM] * len(outs),
        scratch_shapes=list(scratch),
        cost_estimate=pl.CostEstimate(flops=int(flops), bytes_accessed=2 << 20, transcendentals=0),
        compiler_params=pltpu.CompilerParams(vmem_limit_bytes=limit),
    )


def rms_scaled(values, gain):
    mean_square = jnp.mean(values * values, axis=-1, keepdims=True)
    return values * lax.rsqrt(mean_square + EPSILON) * gain


def activate(row, gain):
    u = rms_scaled(row.astype(F32), gain)
    return u / (1.0 + jnp.exp(-u))


def put_columns(target, place, row):
    width, channels = row.shape
    column = lax.broadcasted_iota(jnp.int32, row.shape, 0)
    left = jnp.where(column == 0, 0.0, pltpu.roll(row, 1, 0))
    right = jnp.where(column == width - 1, 0.0, pltpu.roll(row, width - 1, 0))
    rows = pl.ds(place * width, width)
    target[rows, 0:channels] = left.astype(BF16)
    target[rows, channels : 2 * channels] = row.astype(BF16)
    target[rows, 2 * channels : 3 * channels] = right.astype(BF16)


def halo_body(frame, feature, frame_cache, to_below, to_above, sems):
    chosen = jnp.where(frame[0] == FRAMES - 2, 0, 1)
    last = feature.shape[0] - 1
    copies = [
        pltpu.make_async_copy(feature.at[last], to_below.at[0], sems.at[0]),
        pltpu.make_async_copy(frame_cache.at[chosen, last], to_below.at[1], sems.at[1]),
        pltpu.make_async_copy(feature.at[0], to_above.at[0], sems.at[2]),
        pltpu.make_async_copy(frame_cache.at[chosen, 0], to_above.at[1], sems.at[3]),
    ]
    for copy in copies:
        copy.start()
    for copy in copies:
        copy.wait()


def conv_local_body(frame, feature, frame_cache, norm_gain, weight, two_later, one_later, outer,
                    columns, row_gain, feat, cache, gain, middle, sems, feat_sem, cache_sem, gain_sem):
    width = feat.shape[1]
    chosen = jnp.where(frame[0] == FRAMES - 2, 0, 1)
    fetch_gain = pltpu.make_async_copy(norm_gain, gain, gain_sem)
    fetch_feat = pltpu.make_async_copy(feature, feat, feat_sem)
    fetch_cache = pltpu.make_async_copy(frame_cache.at[chosen], cache, cache_sem)
    fetch_gain.start()
    fetch_feat.start()
    fetch_cache.start()
    copies, weights = {}, {}
    for frame_tap in range(2):
        for row_tap in (1, 0, 2):
            place = frame_tap, row_tap
            if row_tap == 1:
                weights[place] = middle.at[frame_tap]
            else:
                weights[place] = outer.at[frame_tap, row_tap // 2]
            copies[place] = pltpu.make_async_copy(weight.at[place], weights[place], sems.at[place])
            copies[place].start()
    fetch_gain.wait()
    fetch_feat.wait()
    fetch_cache.wait()
    scale = gain[...].reshape(1, -1)
    row_gain[...] = scale
    for row in range(2):
        put_columns(columns.at[0], row, activate(feat[row], scale))

    @pl.when(frame[0] >= FRAMES - 2)
    def _():
        for row in range(2):
            put_columns(columns.at[1], row, cache[row].astype(F32))

    for frame_tap, out in ((0, two_later), (1, one_later)):
        source = columns.at[jnp.where(frame[0] >= FRAMES - 2 + frame_tap, 1, 0)]
        copies[frame_tap, 1].wait()
        out[...] = jnp.dot(source[...], weights[frame_tap, 1][...], preferred_element_type=F32)
        for side in range(2):
            copies[frame_tap, 2 * side].wait()
            out[pl.ds((1 - side) * width, width), :] += jnp.dot(
                source[side * width : (side + 1) * width, :],
                weights[frame_tap, 2 * side][...],
                preferred_element_type=F32,
            )


def conv_edges_body(frame_tap, frame, above, below, gain, outer, local_sum, out, columns):
    width = above.shape[1]
    cached = frame[0] >= FRAMES - 2 + frame_tap

    @pl.when(cached)
    def _():
        for side, halo in enumerate((above, below)):
            put_columns(columns, side, halo[1].astype(F32))

    @pl.when(jnp.logical_not(cached))
    def _():
        for side, halo in enumerate((above, below)):
            put_columns(columns, side, activate(halo[0], gain[...]))

    for side in range(2):
        rows = pl.ds(side * width, width)
        product = jnp.dot(
            columns[side * width : (side + 1) * width, :],
            outer[frame_tap, side],
            preferred_element_type=F32,
        )
        out[rows, :] = (local_sum[rows, :] + product).astype(BF16)


def conv_own_body(above, below, gain, weight, inner, own, columns, held, sems):
    width = above.shape[1]
    rows = own.shape[0]
    copies = []
    for row_tap in range(3):
        copies.append(pltpu.make_async_copy(weight.at[2, row_tap], held.at[row_tap], sems.at[row_tap]))
        copies[row_tap].start()
    put_columns(columns, 0, activate(above[0], gain[...]))
    columns[width : width + rows, :] = inner[0]
    put_columns(columns, 1 + rows // width, activate(below[0], gain[...]))
    for row_tap in range(3):
        copies[row_tap].wait()
        product = jnp.dot(
            columns[row_tap * width : row_tap * width + rows, :],
            held[row_tap],
            preferred_element_type=F32,
        )
        if row_tap == 0:
            own[...] = product
        else:
            own[...] += product


def hidden_body(feat, own, one, two, bias, gain, hidden, normed):
    values = feat[...].astype(F32).reshape(own.shape)
    branch = own[...] + one[...].astype(F32) + two[...].astype(F32) + bias[...]
    result = (values + branch).astype(BF16)
    hidden[...] = result
    normed[...] = rms_scaled(result.astype(F32), gain[...]).astype(BF16)


def query_body(normed, weight, bias, query, shift):
    channels = normed.shape[1]
    scale = math.log2(math.e) / math.sqrt(channels)
    q = jnp.dot(normed[...], weight[:, :channels], preferred_element_type=F32) + bias[:, :channels]
    q = q.astype(BF16)
    absorbed = lax.dot_general(
        q, weight[:, channels : 2 * channels], (((1,), (1,)), ((), ())), preferred_element_type=F32
    )
    query[...] = (absorbed * scale).astype(BF16)
    key_bias = bias[:, channels : 2 * channels]
    shift[...] = as_row(jnp.sum(q.astype(F32) * key_bias, axis=-1, keepdims=True) * scale, channels)


def as_row(column, width):
    shape = column.shape[0], width
    row = lax.broadcasted_iota(jnp.int32, shape, 0)
    lane = lax.broadcasted_iota(jnp.int32, shape, 1)
    return jnp.sum(jnp.where(row == lane, column, 0.0), axis=0, keepdims=True)


def widen(lanes, width):
    return jnp.concatenate([lanes] * (-(-width // LANES)), axis=1)[:, :width]


def attend_body(chunks, first, strips, *refs):
    count = GROUP if first else 1
    given, refs = refs[:count], refs[count:]
    pieces, refs = refs[:chunks], refs[chunks:]
    if not first:
        (total_in, top_in), refs = refs[:2], refs[2:]
    outs, keys = refs[:-1], refs[-1]
    channels = pieces[0].shape[1]
    if first:
        queries = outs[2]
        strip = given[0].shape[0]
        for number, query in enumerate(given):
            queries[number * strip : (number + 1) * strip, :] = query[...]
    else:
        queries = given[0]
    strip = queries.shape[0] // GROUP
    start = 0
    for piece in pieces:
        keys[start : start + piece.shape[0], :channels] = piece[...]
        start += piece.shape[0]
    keys[:, channels:] = jnp.ones((start, LANES), BF16)
    if strips:
        blocks = [slice(number * strip, (number + 1) * strip) for number in strips]
    else:
        rows = queries.shape[0] // BLOCKS
        blocks = [slice(block * rows, (block + 1) * rows) for block in range(BLOCKS)]
    for number, block in enumerate(blocks):
        scores = lax.dot_general(
            queries[block, :], keys[:, :channels], (((1,), (1,)), ((), ())),
            preferred_element_type=F32,
        )
        top = jnp.broadcast_to(jnp.max(scores, axis=1, keepdims=True), (scores.shape[0], LANES))
        if not first:
            old_top = top_in[block, :]
            top = jnp.maximum(top, old_top)
        weights = jnp.exp2(scores - widen(top, start)).astype(BF16)
        total = jnp.dot(weights, keys[...], preferred_element_type=F32)
        if not first:
            factor = jnp.exp2(old_top - top)
            total = total + total_in[block, :] * widen(factor, channels + LANES)
        if not strips:
            outs[0][block, :] = total
            outs[1][block, :] = top
            continue
        out = outs[number]
        denominator = total[:, channels:]
        out[:strip, :] = (total[:, :channels] * widen(1.0 / denominator, channels)).astype(BF16)
        level = as_row(widen(top + jnp.log2(denominator), channels), channels)
        high = level.astype(BF16).astype(F32)
        middle = (level - high).astype(BF16).astype(F32)
        low = level - high - middle
        stat = lax.broadcasted_iota(jnp.int32, (STAT_ROWS, channels), 0)
        stats = jnp.where(stat == 0, high, jnp.where(stat == 1, middle, jnp.where(stat == 2, low, 0.0)))
        out[strip:, :] = stats.astype(BF16)


def merge_body(part0, part1, part2, part3, shift, hidden, weight, bias, out_weight, out_bias, mixed):
    rows, channels = hidden.shape
    parts = (part0, part1, part2, part3)
    levels = []
    for part in parts:
        stats = part[rows:, :].astype(F32)
        levels.append(stats[0:1] + stats[1:2] + stats[2:3] + shift[...])
    top = functools.reduce(jnp.maximum, levels)
    shares = [jnp.exp2(level - top) for level in levels]
    inverse = 1.0 / sum(shares)
    shares = jnp.concatenate([share * inverse for share in shares] * 2, axis=0)
    shares = jnp.transpose(shares)[:rows]
    total = sum(
        shares[:, number : number + 1] * part[:rows, :].astype(F32)
        for number, part in enumerate(parts)
    )
    attended = jnp.dot(
        total.astype(BF16), weight[:, 2 * channels :], preferred_element_type=F32
    ) + bias[:, 2 * channels :]
    result = jnp.dot(attended.astype(BF16), out_weight[...], preferred_element_type=F32)
    result = result + out_bias[...] + hidden[...].astype(F32)
    mixed[...] = result.astype(BF16)


def along_y(x, by):
    pairs = [
        (z * GROUP + y, z * GROUP + (y + by) % GROUP) for z in range(RING) for y in range(GROUP)
    ]
    return lax.ppermute(x, "strip", pairs)


def along_z(x, by):
    pairs = [
        (z * GROUP + y, (z + by) % RING * GROUP + y) for z in range(RING) for y in range(GROUP)
    ]
    return lax.ppermute(x, "strip", pairs)


def local(
    feature,
    frame_cache,
    norm_gain,
    conv_weight,
    conv_bias,
    attn_gain,
    qkv_weight,
    qkv_bias,
    out_weight,
    out_bias,
):
    _, height, width, channels = feature.shape
    rows = height * width
    half = rows // 2
    feat = feature[0]
    frame = lax.axis_index("tm")
    weight = pinned(conv_weight.reshape(3, 3, 3 * channels, channels))
    qkv_bias = qkv_bias.reshape(1, 3 * channels)

    frame_number = frame.reshape(1).astype(jnp.int32)
    feature_rows, cache_rows = pinned(feat), pinned(frame_cache)
    to_below, to_above = call(
        halo_body,
        "halo",
        [((2, width, channels), BF16)] * 2,
        [SMEM, HBM, HBM],
        1 << 20,
        [pltpu.SemaphoreType.DMA((4,))],
    )(frame_number, feature_rows, cache_rows)
    above = lax.ppermute(to_below, "strip", [(s, s + 1) for s in range(ROW_STRIPS - 1)])
    below = lax.ppermute(to_above, "strip", [(s + 1, s) for s in range(ROW_STRIPS - 1)])

    flops = 2 * rows * 3 * channels * channels
    two_local, one_local, outer, inner, gain = call(
        conv_local_body,
        "conv_local",
        [
            ((rows, channels), F32),
            ((rows, channels), F32),
            ((2, 2, 3 * channels, channels), BF16),
            ((2, rows, 3 * channels), BF16),
            ((1, channels), F32),
        ],
        [SMEM, HBM, HBM, HBM, HBM],
        4 * flops,
        [
            pltpu.VMEM((height, width, channels), BF16),
            pltpu.VMEM((height, width, channels), BF16),
            pltpu.VMEM((channels,), F32),
            pltpu.VMEM((2, 3 * channels, channels), BF16),
            pltpu.SemaphoreType.DMA((2, 3)),
            pltpu.SemaphoreType.DMA,
            pltpu.SemaphoreType.DMA,
            pltpu.SemaphoreType.DMA,
        ],
    )(frame_number, feature_rows, cache_rows, pinned(norm_gain), weight)

    def conv_edges(name, frame_tap, local_sum):
        return call(
            functools.partial(conv_edges_body, frame_tap),
            name,
            [((rows, channels), BF16)],
            [SMEM] + [VMEM] * 5,
            flops,
            [pltpu.VMEM((rows, 3 * channels), BF16)],
        )(frame_number, above, below, gain, outer, local_sum)[0]

    two = lax.ppermute(
        conv_edges("conv_edges_two", 0, two_local),
        "tm",
        [(f, (f + 2) % FRAMES) for f in range(FRAMES)],
    )
    one = lax.ppermute(
        conv_edges("conv_edges_one", 1, one_local),
        "tm",
        [(f, (f + 1) % FRAMES) for f in range(FRAMES)],
    )
    (own,) = call(
        conv_own_body,
        "conv_own",
        [((rows, channels), F32)],
        [VMEM, VMEM, VMEM, HBM, VMEM],
        3 * flops,
        [
            pltpu.VMEM((2 * width + rows, 3 * channels), BF16),
            pltpu.VMEM((3, 3 * channels, channels), BF16),
            pltpu.SemaphoreType.DMA((3,)),
        ],
    )(above, below, gain, weight, inner)
    hidden, normed = call(
        hidden_body,
        "hidden",
        [((rows, channels), BF16)] * 2,
        [VMEM] * 6,
        rows * channels * 20,
    )(feat, own, one, two, conv_bias.reshape(1, channels), attn_gain.reshape(1, channels))
    query, shift = call(
        query_body,
        "query",
        [((rows, channels), BF16), ((1, channels), F32)],
        [VMEM] * 3,
        4 * rows * channels * channels,
    )(normed, qkv_weight, qkv_bias)

    def attend(name, given, pieces, state=(), strips=()):
        if strips:
            outs = [((rows + STAT_ROWS, channels), BF16)] * len(strips)
        else:
            outs = [((GROUP * rows, channels + LANES), F32), ((GROUP * rows, LANES), F32)]
        if not state:
            outs.append(((GROUP * rows, channels), BF16))
        keys = sum(piece.shape[0] for piece in pieces)
        return call(
            functools.partial(attend_body, len(pieces), not state, strips),
            name,
            outs,
            [VMEM] * (len(given) + len(pieces) + len(state)),
            4 * (len(strips) or GROUP) * rows * keys * channels,
            [pltpu.VMEM((keys, channels + LANES), BF16)],
            32 << 20,
        )(*given, *pieces, *state)

    queries = [query] + [along_y(query, -by) for by in range(1, GROUP)]
    forward, backward = [normed], [normed]
    for step in range(3):
        forward.append(along_z(forward[-1], 1))
        backward.append(along_z(backward[-1], -1))
        if step == 0:
            forward[1], backward[1], _ = lax.optimization_barrier(
                (forward[1], backward[1], query)
            )
        if step == 1:
            forward[2], backward[2], queries[1], queries[3] = lax.optimization_barrier(
                (forward[2], backward[2], queries[1], queries[3])
            )
    *state, query_rows = attend("attend_near", queries, forward[:3] + backward[1:2])
    forward[3], backward[3], *state = lax.optimization_barrier((forward[3], backward[3], *state))
    last = [along_z(forward[3][:half], 1), along_z(backward[3][half:], -1)]
    state = attend("attend_far", [query_rows], [backward[2], forward[3], backward[3]], state)
    parts = {}
    for strips in ((2,), (1, 3), (0,)):
        name = "attend_last_" + "_".join(map(str, strips))
        parts.update(zip(strips, attend(name, [query_rows], last, state, strips)))
    arrived = {by: along_y(parts[by], by) for by in (2, 1, 3)}
    arrived = [arrived[by] for by in range(1, GROUP)]
    (mixed,) = call(
        merge_body,
        "merge",
        [((rows, channels), BF16)],
        [VMEM] * 10,
        4 * rows * channels * channels,
    )(parts[0], *arrived, shift, hidden, qkv_weight, qkv_bias, out_weight, out_bias.reshape(1, channels))
    return mixed.reshape(feature.shape)


def solution(mesh):
    in_specs = (P("tm", "strip", None, None), P(None, "strip", None, None)) + (P(),) * 8
    out_specs = P("tm", "strip", None, None)
    return jax.shard_map(local, mesh=mesh, in_specs=in_specs, out_specs=out_specs, check_vma=False)
```

```python
import functools
import math

import jax
import jax.numpy as jnp
from jax import lax
from jax.experimental import pallas as pl
from jax.experimental.pallas import tpu as pltpu
from jax.sharding import PartitionSpec as P

EPSILON = 1e-06
FRAMES = 8
ROW_STRIPS = 32
RING = 8
GROUP = 4
STAT_ROWS = 16
LANES = 128
BLOCKS = 2
VMEM = pl.BlockSpec(memory_space=pltpu.VMEM)
SMEM = pl.BlockSpec(memory_space=pltpu.SMEM)
HBM = pl.BlockSpec(memory_space=pltpu.HBM)
F32 = jnp.float32
BF16 = jnp.bfloat16
VMEM_LIMIT = 16 << 20


def pinned(x):
    return pltpu.with_memory_space_constraint(x, pltpu.HBM)


def call(body, name, outs, in_specs, flops, scratch=(), limit=VMEM_LIMIT):
    return pl.pallas_call(
        body,
        name=name,
        out_shape=[jax.ShapeDtypeStruct(*out) for out in outs],
        in_specs=in_specs,
        out_specs=[VMEM] * len(outs),
        scratch_shapes=list(scratch),
        cost_estimate=pl.CostEstimate(flops=int(flops), bytes_accessed=2 << 20, transcendentals=0),
        compiler_params=pltpu.CompilerParams(vmem_limit_bytes=limit),
    )


def rms_scaled(values, gain):
    mean_square = jnp.mean(values * values, axis=-1, keepdims=True)
    return values * lax.rsqrt(mean_square + EPSILON) * gain


def activate(row, gain):
    u = rms_scaled(row.astype(F32), gain)
    return u / (1.0 + jnp.exp(-u))


def put_columns(target, place, row):
    width, channels = row.shape
    column = lax.broadcasted_iota(jnp.int32, row.shape, 0)
    left = jnp.where(column == 0, 0.0, pltpu.roll(row, 1, 0))
    right = jnp.where(column == width - 1, 0.0, pltpu.roll(row, width - 1, 0))
    rows = pl.ds(place * width, width)
    target[rows, 0:channels] = left.astype(BF16)
    target[rows, channels : 2 * channels] = row.astype(BF16)
    target[rows, 2 * channels : 3 * channels] = right.astype(BF16)


def halo_body(frame, feature, frame_cache, to_below, to_above, sems):
    chosen = jnp.where(frame[0] == FRAMES - 2, 0, 1)
    last = feature.shape[0] - 1
    copies = [
        pltpu.make_async_copy(feature.at[last], to_below.at[0], sems.at[0]),
        pltpu.make_async_copy(frame_cache.at[chosen, last], to_below.at[1], sems.at[1]),
        pltpu.make_async_copy(feature.at[0], to_above.at[0], sems.at[2]),
        pltpu.make_async_copy(frame_cache.at[chosen, 0], to_above.at[1], sems.at[3]),
    ]
    for copy in copies:
        copy.start()
    for copy in copies:
        copy.wait()


def conv_local_body(frame, feat, cache, gain, weight, two_later, one_later, columns, row_gain):
    width = feat.shape[1]
    scale = gain[...].reshape(1, -1)
    row_gain[...] = scale
    for row in range(2):
        put_columns(columns.at[0], row, activate(feat[row], scale))

    @pl.when(frame[0] >= FRAMES - 2)
    def _():
        chosen = jnp.where(frame[0] == FRAMES - 2, 0, 1)
        for row in range(2):
            put_columns(columns.at[1], row, cache[chosen, row].astype(F32))

    for frame_tap, out in ((0, two_later), (1, one_later)):
        source = columns.at[jnp.where(frame[0] >= FRAMES - 2 + frame_tap, 1, 0)]
        out[...] = jnp.dot(source[...], weight[frame_tap, 1], preferred_element_type=F32)
        for side in range(2):
            out[pl.ds((1 - side) * width, width), :] += jnp.dot(
                source[side * width : (side + 1) * width, :],
                weight[frame_tap, 2 * side],
                preferred_element_type=F32,
            )


def conv_edges_body(frame_tap, frame, above, below, gain, weight, local_sum, out, columns):
    width = above.shape[1]
    cached = frame[0] >= FRAMES - 2 + frame_tap

    @pl.when(cached)
    def _():
        for side, halo in enumerate((above, below)):
            put_columns(columns, side, halo[1].astype(F32))

    @pl.when(jnp.logical_not(cached))
    def _():
        for side, halo in enumerate((above, below)):
            put_columns(columns, side, activate(halo[0], gain[...]))

    for side in range(2):
        rows = pl.ds(side * width, width)
        product = jnp.dot(
            columns[side * width : (side + 1) * width, :],
            weight[frame_tap, 2 * side],
            preferred_element_type=F32,
        )
        out[rows, :] = (local_sum[rows, :] + product).astype(BF16)


def conv_own_body(above, below, gain, weight, inner, own, columns):
    width = above.shape[1]
    rows = own.shape[0]
    put_columns(columns, 0, activate(above[0], gain[...]))
    columns[width : width + rows, :] = inner[0]
    put_columns(columns, 1 + rows // width, activate(below[0], gain[...]))
    for row_tap in range(3):
        product = jnp.dot(
            columns[row_tap * width : row_tap * width + rows, :],
            weight[2, row_tap],
            preferred_element_type=F32,
        )
        if row_tap == 0:
            own[...] = product
        else:
            own[...] += product


def hidden_body(feat, own, one, two, bias, gain, hidden, normed):
    values = feat[...].astype(F32).reshape(own.shape)
    branch = own[...] + one[...].astype(F32) + two[...].astype(F32) + bias[...]
    result = (values + branch).astype(BF16)
    hidden[...] = result
    normed[...] = rms_scaled(result.astype(F32), gain[...]).astype(BF16)


def query_body(normed, weight, bias, query, shift):
    channels = normed.shape[1]
    scale = math.log2(math.e) / math.sqrt(channels)
    q = jnp.dot(normed[...], weight[:, :channels], preferred_element_type=F32) + bias[:, :channels]
    q = q.astype(BF16)
    absorbed = lax.dot_general(
        q, weight[:, channels : 2 * channels], (((1,), (1,)), ((), ())), preferred_element_type=F32
    )
    query[...] = (absorbed * scale).astype(BF16)
    key_bias = bias[:, channels : 2 * channels]
    shift[...] = as_row(jnp.sum(q.astype(F32) * key_bias, axis=-1, keepdims=True) * scale, channels)


def as_row(column, width):
    shape = column.shape[0], width
    row = lax.broadcasted_iota(jnp.int32, shape, 0)
    lane = lax.broadcasted_iota(jnp.int32, shape, 1)
    return jnp.sum(jnp.where(row == lane, column, 0.0), axis=0, keepdims=True)


def widen(lanes, width):
    return jnp.concatenate([lanes] * (-(-width // LANES)), axis=1)[:, :width]


def attend_body(chunks, first, strips, *refs):
    count = GROUP if first else 1
    given, refs = refs[:count], refs[count:]
    pieces, refs = refs[:chunks], refs[chunks:]
    if not first:
        (total_in, top_in), refs = refs[:2], refs[2:]
    outs, keys = refs[:-1], refs[-1]
    channels = pieces[0].shape[1]
    if first:
        queries = outs[2]
        strip = given[0].shape[0]
        for number, query in enumerate(given):
            queries[number * strip : (number + 1) * strip, :] = query[...]
    else:
        queries = given[0]
    strip = queries.shape[0] // GROUP
    start = 0
    for piece in pieces:
        keys[start : start + piece.shape[0], :channels] = piece[...]
        start += piece.shape[0]
    keys[:, channels:] = jnp.ones((start, LANES), BF16)
    if strips:
        blocks = [slice(number * strip, (number + 1) * strip) for number in strips]
    else:
        rows = queries.shape[0] // BLOCKS
        blocks = [slice(block * rows, (block + 1) * rows) for block in range(BLOCKS)]
    for number, block in enumerate(blocks):
        scores = lax.dot_general(
            queries[block, :], keys[:, :channels], (((1,), (1,)), ((), ())),
            preferred_element_type=F32,
        )
        top = jnp.broadcast_to(jnp.max(scores, axis=1, keepdims=True), (scores.shape[0], LANES))
        if not first:
            old_top = top_in[block, :]
            top = jnp.maximum(top, old_top)
        weights = jnp.exp2(scores - widen(top, start)).astype(BF16)
        total = jnp.dot(weights, keys[...], preferred_element_type=F32)
        if not first:
            factor = jnp.exp2(old_top - top)
            total = total + total_in[block, :] * widen(factor, channels + LANES)
        if not strips:
            outs[0][block, :] = total
            outs[1][block, :] = top
            continue
        out = outs[number]
        denominator = total[:, channels:]
        out[:strip, :] = (total[:, :channels] * widen(1.0 / denominator, channels)).astype(BF16)
        level = as_row(widen(top + jnp.log2(denominator), channels), channels)
        high = level.astype(BF16).astype(F32)
        middle = (level - high).astype(BF16).astype(F32)
        low = level - high - middle
        stat = lax.broadcasted_iota(jnp.int32, (STAT_ROWS, channels), 0)
        stats = jnp.where(stat == 0, high, jnp.where(stat == 1, middle, jnp.where(stat == 2, low, 0.0)))
        out[strip:, :] = stats.astype(BF16)


def merge_body(part0, part1, part2, part3, shift, hidden, weight, bias, out_weight, out_bias, mixed):
    rows, channels = hidden.shape
    parts = (part0, part1, part2, part3)
    levels = []
    for part in parts:
        stats = part[rows:, :].astype(F32)
        levels.append(stats[0:1] + stats[1:2] + stats[2:3] + shift[...])
    top = functools.reduce(jnp.maximum, levels)
    shares = [jnp.exp2(level - top) for level in levels]
    inverse = 1.0 / sum(shares)
    shares = jnp.concatenate([share * inverse for share in shares] * 2, axis=0)
    shares = jnp.transpose(shares)[:rows]
    total = sum(
        shares[:, number : number + 1] * part[:rows, :].astype(F32)
        for number, part in enumerate(parts)
    )
    attended = jnp.dot(
        total.astype(BF16), weight[:, 2 * channels :], preferred_element_type=F32
    ) + bias[:, 2 * channels :]
    result = jnp.dot(attended.astype(BF16), out_weight[...], preferred_element_type=F32)
    result = result + out_bias[...] + hidden[...].astype(F32)
    mixed[...] = result.astype(BF16)


def along_y(x, by):
    pairs = [
        (z * GROUP + y, z * GROUP + (y + by) % GROUP) for z in range(RING) for y in range(GROUP)
    ]
    return lax.ppermute(x, "strip", pairs)


def along_z(x, by):
    pairs = [
        (z * GROUP + y, (z + by) % RING * GROUP + y) for z in range(RING) for y in range(GROUP)
    ]
    return lax.ppermute(x, "strip", pairs)


def local(
    feature,
    frame_cache,
    norm_gain,
    conv_weight,
    conv_bias,
    attn_gain,
    qkv_weight,
    qkv_bias,
    out_weight,
    out_bias,
):
    _, height, width, channels = feature.shape
    rows = height * width
    half = rows // 2
    feat = feature[0]
    frame = lax.axis_index("tm")
    weight = conv_weight.reshape(3, 3, 3 * channels, channels)
    qkv_bias = qkv_bias.reshape(1, 3 * channels)

    frame_number = frame.reshape(1).astype(jnp.int32)
    to_below, to_above = call(
        halo_body,
        "halo",
        [((2, width, channels), BF16)] * 2,
        [SMEM, HBM, HBM],
        20 << 30,
        [pltpu.SemaphoreType.DMA((4,))],
    )(frame_number, pinned(feat), pinned(frame_cache))
    above = lax.ppermute(to_below, "strip", [(s, s + 1) for s in range(ROW_STRIPS - 1)])
    below = lax.ppermute(to_above, "strip", [(s + 1, s) for s in range(ROW_STRIPS - 1)])

    flops = 2 * rows * 3 * channels * channels
    two_local, one_local, inner, gain = call(
        conv_local_body,
        "conv_local",
        [
            ((rows, channels), F32),
            ((rows, channels), F32),
            ((2, rows, 3 * channels), BF16),
            ((1, channels), F32),
        ],
        [SMEM, VMEM, VMEM, VMEM, VMEM],
        4 * flops,
    )(frame_number, feat, frame_cache, norm_gain, weight)

    def conv_edges(name, frame_tap, local_sum):
        return call(
            functools.partial(conv_edges_body, frame_tap),
            name,
            [((rows, channels), BF16)],
            [SMEM] + [VMEM] * 5,
            flops,
            [pltpu.VMEM((rows, 3 * channels), BF16)],
        )(frame_number, above, below, gain, weight, local_sum)[0]

    two = lax.ppermute(
        conv_edges("conv_edges_two", 0, two_local),
        "tm",
        [(f, (f + 2) % FRAMES) for f in range(FRAMES)],
    )
    one = lax.ppermute(
        conv_edges("conv_edges_one", 1, one_local),
        "tm",
        [(f, (f + 1) % FRAMES) for f in range(FRAMES)],
    )
    (own,) = call(
        conv_own_body,
        "conv_own",
        [((rows, channels), F32)],
        [VMEM] * 5,
        3 * flops,
        [pltpu.VMEM((2 * width + rows, 3 * channels), BF16)],
    )(above, below, gain, weight, inner)
    hidden, normed = call(
        hidden_body,
        "hidden",
        [((rows, channels), BF16)] * 2,
        [VMEM] * 6,
        rows * channels * 20,
    )(feat, own, one, two, conv_bias.reshape(1, channels), attn_gain.reshape(1, channels))
    query, shift = call(
        query_body,
        "query",
        [((rows, channels), BF16), ((1, channels), F32)],
        [VMEM] * 3,
        4 * rows * channels * channels,
    )(normed, qkv_weight, qkv_bias)

    def attend(name, given, pieces, state=(), strips=()):
        if strips:
            outs = [((rows + STAT_ROWS, channels), BF16)] * len(strips)
        else:
            outs = [((GROUP * rows, channels + LANES), F32), ((GROUP * rows, LANES), F32)]
        if not state:
            outs.append(((GROUP * rows, channels), BF16))
        keys = sum(piece.shape[0] for piece in pieces)
        return call(
            functools.partial(attend_body, len(pieces), not state, strips),
            name,
            outs,
            [VMEM] * (len(given) + len(pieces) + len(state)),
            4 * (len(strips) or GROUP) * rows * keys * channels,
            [pltpu.VMEM((keys, channels + LANES), BF16)],
            32 << 20,
        )(*given, *pieces, *state)

    queries = [query] + [along_y(query, -by) for by in range(1, GROUP)]
    forward, backward = [normed], [normed]
    for step in range(3):
        forward.append(along_z(forward[-1], 1))
        backward.append(along_z(backward[-1], -1))
        if step == 0:
            forward[1], backward[1], _ = lax.optimization_barrier(
                (forward[1], backward[1], query)
            )
        if step == 1:
            forward[2], backward[2], queries[1], queries[3] = lax.optimization_barrier(
                (forward[2], backward[2], queries[1], queries[3])
            )
    *state, query_rows = attend("attend_near", queries, forward[:3] + backward[1:2])
    forward[3], backward[3], *state = lax.optimization_barrier((forward[3], backward[3], *state))
    last = [along_z(forward[3][:half], 1), along_z(backward[3][half:], -1)]
    state = attend("attend_far", [query_rows], [backward[2], forward[3], backward[3]], state)
    parts = {}
    for strips in ((2,), (1, 3), (0,)):
        name = "attend_last_" + "_".join(map(str, strips))
        parts.update(zip(strips, attend(name, [query_rows], last, state, strips)))
    arrived = {by: along_y(parts[by], by) for by in (2, 1, 3)}
    arrived = [arrived[by] for by in range(1, GROUP)]
    (mixed,) = call(
        merge_body,
        "merge",
        [((rows, channels), BF16)],
        [VMEM] * 10,
        4 * rows * channels * channels,
    )(parts[0], *arrived, shift, hidden, qkv_weight, qkv_bias, out_weight, out_bias.reshape(1, channels))
    return mixed.reshape(feature.shape)


def solution(mesh):
    in_specs = (P("tm", "strip", None, None), P(None, "strip", None, None)) + (P(),) * 8
    out_specs = P("tm", "strip", None, None)
    return jax.shard_map(local, mesh=mesh, in_specs=in_specs, out_specs=out_specs, check_vma=False)
```

```python
import functools
import math

import jax
import jax.numpy as jnp
from jax import lax
from jax.experimental import pallas as pl
from jax.experimental.pallas import tpu as pltpu
from jax.sharding import PartitionSpec as P

EPSILON = 1e-06
FRAMES = 8
ROW_STRIPS = 32
RING = 8
GROUP = 4
STAT_ROWS = 16
LANES = 128
BLOCKS = 2
VMEM = pl.BlockSpec(memory_space=pltpu.VMEM)
SMEM = pl.BlockSpec(memory_space=pltpu.SMEM)
HBM = pl.BlockSpec(memory_space=pltpu.HBM)
F32 = jnp.float32
BF16 = jnp.bfloat16
VMEM_LIMIT = 16 << 20


def pinned(x):
    return pltpu.with_memory_space_constraint(x, pltpu.HBM)


def call(body, name, outs, in_specs, flops, scratch=(), limit=VMEM_LIMIT):
    return pl.pallas_call(
        body,
        name=name,
        out_shape=[jax.ShapeDtypeStruct(*out) for out in outs],
        in_specs=in_specs,
        out_specs=[VMEM] * len(outs),
        scratch_shapes=list(scratch),
        cost_estimate=pl.CostEstimate(flops=int(flops), bytes_accessed=2 << 20, transcendentals=0),
        compiler_params=pltpu.CompilerParams(vmem_limit_bytes=limit),
    )


def rms_scaled(values, gain):
    mean_square = jnp.mean(values * values, axis=-1, keepdims=True)
    return values * lax.rsqrt(mean_square + EPSILON) * gain


def activate(row, gain):
    u = rms_scaled(row.astype(F32), gain)
    return u / (1.0 + jnp.exp(-u))


def put_columns(target, place, row):
    width, channels = row.shape
    column = lax.broadcasted_iota(jnp.int32, row.shape, 0)
    left = jnp.where(column == 0, 0.0, pltpu.roll(row, 1, 0))
    right = jnp.where(column == width - 1, 0.0, pltpu.roll(row, width - 1, 0))
    rows = pl.ds(place * width, width)
    target[rows, 0:channels] = left.astype(BF16)
    target[rows, channels : 2 * channels] = row.astype(BF16)
    target[rows, 2 * channels : 3 * channels] = right.astype(BF16)


def halo_body(feature, frame_cache, to_below, to_above, cache_to_below, cache_to_above, sems):
    last = feature.shape[0] - 1
    copies = [
        pltpu.make_async_copy(feature.at[last], to_below, sems.at[0]),
        pltpu.make_async_copy(feature.at[0], to_above, sems.at[1]),
        pltpu.make_async_copy(frame_cache.at[:, last], cache_to_below, sems.at[2]),
        pltpu.make_async_copy(frame_cache.at[:, 0], cache_to_above, sems.at[3]),
    ]
    for copy in copies:
        copy.start()
    for copy in copies:
        copy.wait()


def conv_local_body(feat, gain, weight, two_later, one_later, columns, row_gain):
    width = feat.shape[1]
    scale = gain[...].reshape(1, -1)
    row_gain[...] = scale
    for row in range(2):
        put_columns(columns, row, activate(feat[row], scale))
    for frame_tap, out in ((0, two_later), (1, one_later)):
        out[...] = jnp.dot(columns[...], weight[frame_tap, 1], preferred_element_type=F32)
        for side in range(2):
            out[pl.ds((1 - side) * width, width), :] += jnp.dot(
                columns[side * width : (side + 1) * width, :],
                weight[frame_tap, 2 * side],
                preferred_element_type=F32,
            )


def conv_edges_body(frame_tap, above, below, gain, weight, local_sum, out, columns):
    width = above.shape[0]
    for side, halo in enumerate((above, below)):
        put_columns(columns, side, activate(halo[...], gain[...]))
        rows = pl.ds(side * width, width)
        product = jnp.dot(
            columns[side * width : (side + 1) * width, :],
            weight[frame_tap, 2 * side],
            preferred_element_type=F32,
        )
        out[rows, :] = (local_sum[rows, :] + product).astype(BF16)


def conv_own_body(above, below, gain, weight, inner, own, columns, held, sems):
    width = above.shape[0]
    rows = own.shape[0]
    copies = []
    for row_tap in range(3):
        copies.append(pltpu.make_async_copy(weight.at[2, row_tap], held.at[row_tap], sems.at[row_tap]))
        copies[row_tap].start()
    put_columns(columns, 0, activate(above[...], gain[...]))
    columns[width : width + rows, :] = inner[...]
    put_columns(columns, 1 + rows // width, activate(below[...], gain[...]))
    for row_tap in range(3):
        copies[row_tap].wait()
        product = jnp.dot(
            columns[row_tap * width : row_tap * width + rows, :],
            held[row_tap],
            preferred_element_type=F32,
        )
        if row_tap == 0:
            own[...] = product
        else:
            own[...] += product


def conv_cache_body(frame, frame_cache, above, below, weight, sums, columns, cache, held, sems,
                    cache_sem):
    width = above.shape[1]
    rows = sums.shape[0]
    sums[...] = jnp.zeros(sums.shape, F32)

    @pl.when(frame[0] <= 1)
    def _():
        fetch = pltpu.make_async_copy(frame_cache, cache, cache_sem)
        fetch.start()
        copies = []
        for place in range(6):
            source = weight.at[place // 3, place % 3]
            copies.append(pltpu.make_async_copy(source, held.at[place], sems.at[place]))
            copies[place].start()
        fetch.wait()
        for copy in copies:
            copy.wait()

        def add_cache(number, frame_tap):
            around = (above[number], cache[number, 0], cache[number, 1], below[number])
            for place, row in enumerate(around):
                put_columns(columns, place, row.astype(F32))
            for row_tap in range(3):
                sums[...] += jnp.dot(
                    columns[row_tap * width : row_tap * width + rows, :],
                    held[3 * frame_tap + row_tap],
                    preferred_element_type=F32,
                )

        add_cache(1, 1 - frame[0])

        @pl.when(frame[0] == 0)
        def _():
            add_cache(0, 0)


def hidden_body(feat, own, cached, one, two, bias, gain, hidden, normed):
    values = feat[...].astype(F32).reshape(own.shape)
    branch = own[...] + cached[...] + one[...].astype(F32) + two[...].astype(F32) + bias[...]
    result = (values + branch).astype(BF16)
    hidden[...] = result
    normed[...] = rms_scaled(result.astype(F32), gain[...]).astype(BF16)


def query_body(normed, weight, bias, query, shift):
    channels = normed.shape[1]
    scale = math.log2(math.e) / math.sqrt(channels)
    q = jnp.dot(normed[...], weight[:, :channels], preferred_element_type=F32) + bias[:, :channels]
    q = q.astype(BF16)
    absorbed = lax.dot_general(
        q, weight[:, channels : 2 * channels], (((1,), (1,)), ((), ())), preferred_element_type=F32
    )
    query[...] = (absorbed * scale).astype(BF16)
    key_bias = bias[:, channels : 2 * channels]
    shift[...] = as_row(jnp.sum(q.astype(F32) * key_bias, axis=-1, keepdims=True) * scale, channels)


def as_row(column, width):
    shape = column.shape[0], width
    row = lax.broadcasted_iota(jnp.int32, shape, 0)
    lane = lax.broadcasted_iota(jnp.int32, shape, 1)
    return jnp.sum(jnp.where(row == lane, column, 0.0), axis=0, keepdims=True)


def widen(lanes, width):
    return jnp.concatenate([lanes] * (-(-width // LANES)), axis=1)[:, :width]


def attend_body(chunks, first, strips, *refs):
    count = GROUP if first else 1
    given, refs = refs[:count], refs[count:]
    pieces, refs = refs[:chunks], refs[chunks:]
    if not first:
        (total_in, top_in), refs = refs[:2], refs[2:]
    outs, keys = refs[:-1], refs[-1]
    channels = pieces[0].shape[1]
    if first:
        queries = outs[2]
        strip = given[0].shape[0]
        for number, query in enumerate(given):
            queries[number * strip : (number + 1) * strip, :] = query[...]
    else:
        queries = given[0]
    strip = queries.shape[0] // GROUP
    start = 0
    for piece in pieces:
        keys[start : start + piece.shape[0], :channels] = piece[...]
        start += piece.shape[0]
    keys[:, channels:] = jnp.ones((start, LANES), BF16)
    if strips:
        blocks = [slice(number * strip, (number + 1) * strip) for number in strips]
    else:
        rows = queries.shape[0] // BLOCKS
        blocks = [slice(block * rows, (block + 1) * rows) for block in range(BLOCKS)]
    for number, block in enumerate(blocks):
        scores = lax.dot_general(
            queries[block, :], keys[:, :channels], (((1,), (1,)), ((), ())),
            preferred_element_type=F32,
        )
        top = jnp.broadcast_to(jnp.max(scores, axis=1, keepdims=True), (scores.shape[0], LANES))
        if not first:
            old_top = top_in[block, :]
            top = jnp.maximum(top, old_top)
        weights = jnp.exp2(scores - widen(top, start)).astype(BF16)
        total = jnp.dot(weights, keys[...], preferred_element_type=F32)
        if not first:
            factor = jnp.exp2(old_top - top)
            total = total + total_in[block, :] * widen(factor, channels + LANES)
        if not strips:
            outs[0][block, :] = total
            outs[1][block, :] = top
            continue
        out = outs[number]
        denominator = total[:, channels:]
        out[:strip, :] = (total[:, :channels] * widen(1.0 / denominator, channels)).astype(BF16)
        level = as_row(widen(top + jnp.log2(denominator), channels), channels)
        high = level.astype(BF16).astype(F32)
        middle = (level - high).astype(BF16).astype(F32)
        low = level - high - middle
        stat = lax.broadcasted_iota(jnp.int32, (STAT_ROWS, channels), 0)
        stats = jnp.where(stat == 0, high, jnp.where(stat == 1, middle, jnp.where(stat == 2, low, 0.0)))
        out[strip:, :] = stats.astype(BF16)


def merge_body(part0, part1, part2, part3, shift, hidden, weight, bias, out_weight, out_bias, mixed):
    rows, channels = hidden.shape
    parts = (part0, part1, part2, part3)
    levels = []
    for part in parts:
        stats = part[rows:, :].astype(F32)
        levels.append(stats[0:1] + stats[1:2] + stats[2:3] + shift[...])
    top = functools.reduce(jnp.maximum, levels)
    shares = [jnp.exp2(level - top) for level in levels]
    inverse = 1.0 / sum(shares)
    shares = jnp.concatenate([share * inverse for share in shares] * 2, axis=0)
    shares = jnp.transpose(shares)[:rows]
    total = sum(
        shares[:, number : number + 1] * part[:rows, :].astype(F32)
        for number, part in enumerate(parts)
    )
    attended = jnp.dot(
        total.astype(BF16), weight[:, 2 * channels :], preferred_element_type=F32
    ) + bias[:, 2 * channels :]
    result = jnp.dot(attended.astype(BF16), out_weight[...], preferred_element_type=F32)
    result = result + out_bias[...] + hidden[...].astype(F32)
    mixed[...] = result.astype(BF16)


def along_y(x, by):
    pairs = [
        (z * GROUP + y, z * GROUP + (y + by) % GROUP) for z in range(RING) for y in range(GROUP)
    ]
    return lax.ppermute(x, "strip", pairs)


def along_z(x, by):
    pairs = [
        (z * GROUP + y, (z + by) % RING * GROUP + y) for z in range(RING) for y in range(GROUP)
    ]
    return lax.ppermute(x, "strip", pairs)


def local(
    feature,
    frame_cache,
    norm_gain,
    conv_weight,
    conv_bias,
    attn_gain,
    qkv_weight,
    qkv_bias,
    out_weight,
    out_bias,
):
    _, height, width, channels = feature.shape
    rows = height * width
    half = rows // 2
    feat = feature[0]
    frame = lax.axis_index("tm")
    weight = conv_weight.reshape(3, 3, 3 * channels, channels)
    qkv_bias = qkv_bias.reshape(1, 3 * channels)

    cache_rows, weight_rows = pinned(frame_cache), pinned(weight)
    to_below, to_above, cache_to_below, cache_to_above = call(
        halo_body,
        "halo",
        [((width, channels), BF16)] * 2 + [((2, width, channels), BF16)] * 2,
        [HBM, HBM],
        20 << 30,
        [pltpu.SemaphoreType.DMA((4,))],
    )(pinned(feat), cache_rows)
    down = [(s, s + 1) for s in range(ROW_STRIPS - 1)]
    up = [(s + 1, s) for s in range(ROW_STRIPS - 1)]
    above = lax.ppermute(to_below, "strip", down)
    below = lax.ppermute(to_above, "strip", up)

    def of_first_two(pairs):
        return [(f * ROW_STRIPS + a, f * ROW_STRIPS + b) for f in range(2) for a, b in pairs]

    cache_above = lax.ppermute(cache_to_below, ("tm", "strip"), of_first_two(down))
    cache_below = lax.ppermute(cache_to_above, ("tm", "strip"), of_first_two(up))

    flops = 2 * rows * 3 * channels * channels
    two_local, one_local, inner, gain = call(
        conv_local_body,
        "conv_local",
        [
            ((rows, channels), F32),
            ((rows, channels), F32),
            ((rows, 3 * channels), BF16),
            ((1, channels), F32),
        ],
        [VMEM] * 3,
        4 * flops,
    )(feat, norm_gain, weight)

    def conv_edges(name, frame_tap, local_sum):
        return call(
            functools.partial(conv_edges_body, frame_tap),
            name,
            [((rows, channels), BF16)],
            [VMEM] * 5,
            flops,
            [pltpu.VMEM((rows, 3 * channels), BF16)],
        )(above, below, gain, weight, local_sum)[0]

    two = lax.ppermute(
        conv_edges("conv_edges_two", 0, two_local), "tm", [(f, f + 2) for f in range(FRAMES - 2)]
    )
    one = lax.ppermute(
        conv_edges("conv_edges_one", 1, one_local), "tm", [(f, f + 1) for f in range(FRAMES - 1)]
    )
    (own,) = call(
        conv_own_body,
        "conv_own",
        [((rows, channels), F32)],
        [VMEM, VMEM, VMEM, HBM, VMEM],
        3 * flops,
        [
            pltpu.VMEM((2 * width + rows, 3 * channels), BF16),
            pltpu.VMEM((3, 3 * channels, channels), BF16),
            pltpu.SemaphoreType.DMA((3,)),
        ],
    )(above, below, gain, weight_rows, inner)
    (cached,) = call(
        conv_cache_body,
        "conv_cache",
        [((rows, channels), F32)],
        [SMEM, HBM, VMEM, VMEM, HBM],
        flops,
        [
            pltpu.VMEM((2 * width + rows, 3 * channels), BF16),
            pltpu.VMEM((2, height, width, channels), BF16),
            pltpu.VMEM((6, 3 * channels, channels), BF16),
            pltpu.SemaphoreType.DMA((6,)),
            pltpu.SemaphoreType.DMA,
        ],
    )(
        frame.reshape(1).astype(jnp.int32),
        cache_rows,
        cache_above,
        cache_below,
        weight_rows,
    )
    hidden, normed = call(
        hidden_body,
        "hidden",
        [((rows, channels), BF16)] * 2,
        [VMEM] * 7,
        rows * channels * 20,
    )(feat, own, cached, one, two, conv_bias.reshape(1, channels), attn_gain.reshape(1, channels))
    query, shift = call(
        query_body,
        "query",
        [((rows, channels), BF16), ((1, channels), F32)],
        [VMEM] * 3,
        4 * rows * channels * channels,
    )(normed, qkv_weight, qkv_bias)

    def attend(name, given, pieces, state=(), strips=()):
        if strips:
            outs = [((rows + STAT_ROWS, channels), BF16)] * len(strips)
        else:
            outs = [((GROUP * rows, channels + LANES), F32), ((GROUP * rows, LANES), F32)]
        if not state:
            outs.append(((GROUP * rows, channels), BF16))
        keys = sum(piece.shape[0] for piece in pieces)
        return call(
            functools.partial(attend_body, len(pieces), not state, strips),
            name,
            outs,
            [VMEM] * (len(given) + len(pieces) + len(state)),
            4 * (len(strips) or GROUP) * rows * keys * channels,
            [pltpu.VMEM((keys, channels + LANES), BF16)],
            32 << 20,
        )(*given, *pieces, *state)

    queries = [query] + [along_y(query, -by) for by in range(1, GROUP)]
    forward, backward = [normed], [normed]
    for step in range(3):
        forward.append(along_z(forward[-1], 1))
        backward.append(along_z(backward[-1], -1))
        if step == 0:
            forward[1], backward[1], _ = lax.optimization_barrier(
                (forward[1], backward[1], query)
            )
        if step == 1:
            forward[2], backward[2], queries[1], queries[3] = lax.optimization_barrier(
                (forward[2], backward[2], queries[1], queries[3])
            )
    *state, query_rows = attend("attend_near", queries, forward[:3] + backward[1:2])
    forward[3], backward[3], *state = lax.optimization_barrier((forward[3], backward[3], *state))
    last = [along_z(forward[3][:half], 1), along_z(backward[3][half:], -1)]
    state = attend("attend_far", [query_rows], [backward[2], forward[3], backward[3]], state)
    parts = {}
    for strips in ((2,), (1, 3), (0,)):
        name = "attend_last_" + "_".join(map(str, strips))
        parts.update(zip(strips, attend(name, [query_rows], last, state, strips)))
    arrived = {by: along_y(parts[by], by) for by in (2, 1, 3)}
    arrived = [arrived[by] for by in range(1, GROUP)]
    (mixed,) = call(
        merge_body,
        "merge",
        [((rows, channels), BF16)],
        [VMEM] * 10,
        4 * rows * channels * channels,
    )(parts[0], *arrived, shift, hidden, qkv_weight, qkv_bias, out_weight, out_bias.reshape(1, channels))
    return mixed.reshape(feature.shape)


def solution(mesh):
    in_specs = (P("tm", "strip", None, None), P(None, "strip", None, None)) + (P(),) * 8
    out_specs = P("tm", "strip", None, None)
    return jax.shard_map(local, mesh=mesh, in_specs=in_specs, out_specs=out_specs, check_vma=False)
```

```python
import functools
import math

import jax
import jax.numpy as jnp
from jax import lax
from jax.experimental import pallas as pl
from jax.experimental.pallas import tpu as pltpu
from jax.sharding import PartitionSpec as P

EPSILON = 1e-06
FRAMES = 8
ROW_STRIPS = 32
RING = 8
GROUP = 4
STAT_ROWS = 16
LANES = 128
BLOCKS = 2
VMEM = pl.BlockSpec(memory_space=pltpu.VMEM)
SMEM = pl.BlockSpec(memory_space=pltpu.SMEM)
HBM = pl.BlockSpec(memory_space=pltpu.HBM)
F32 = jnp.float32
BF16 = jnp.bfloat16
VMEM_LIMIT = 16 << 20


def pinned(x):
    return pltpu.with_memory_space_constraint(x, pltpu.HBM)


def call(body, name, outs, in_specs, flops, scratch=(), limit=VMEM_LIMIT):
    return pl.pallas_call(
        body,
        name=name,
        out_shape=[jax.ShapeDtypeStruct(*out) for out in outs],
        in_specs=in_specs,
        out_specs=[VMEM] * len(outs),
        scratch_shapes=list(scratch),
        cost_estimate=pl.CostEstimate(flops=int(flops), bytes_accessed=2 << 20, transcendentals=0),
        compiler_params=pltpu.CompilerParams(vmem_limit_bytes=limit),
    )


def rms_scaled(values, gain):
    mean_square = jnp.mean(values * values, axis=-1, keepdims=True)
    return values * lax.rsqrt(mean_square + EPSILON) * gain


def activate(row, gain):
    u = rms_scaled(row.astype(F32), gain)
    return u / (1.0 + jnp.exp(-u))


def put_columns(target, place, row):
    width, channels = row.shape
    column = lax.broadcasted_iota(jnp.int32, row.shape, 0)
    left = jnp.where(column == 0, 0.0, pltpu.roll(row, 1, 0))
    right = jnp.where(column == width - 1, 0.0, pltpu.roll(row, width - 1, 0))
    rows = pl.ds(place * width, width)
    target[rows, 0:channels] = left.astype(BF16)
    target[rows, channels : 2 * channels] = row.astype(BF16)
    target[rows, 2 * channels : 3 * channels] = right.astype(BF16)


def halo_body(frame, feature, frame_cache, to_below, to_above, sems):
    chosen = jnp.where(frame[0] == FRAMES - 2, 0, 1)
    last = feature.shape[0] - 1
    copies = [
        pltpu.make_async_copy(feature.at[last], to_below.at[0], sems.at[0]),
        pltpu.make_async_copy(frame_cache.at[chosen, last], to_below.at[1], sems.at[1]),
        pltpu.make_async_copy(feature.at[0], to_above.at[0], sems.at[2]),
        pltpu.make_async_copy(frame_cache.at[chosen, 0], to_above.at[1], sems.at[3]),
    ]
    for copy in copies:
        copy.start()
    for copy in copies:
        copy.wait()


def conv_local_body(frame, feat, cache, gain, weight, two_later, one_later, columns, row_gain):
    width = feat.shape[1]
    scale = gain[...].reshape(1, -1)
    row_gain[...] = scale
    for row in range(2):
        put_columns(columns.at[0], row, activate(feat[row], scale))

    @pl.when(frame[0] >= FRAMES - 2)
    def _():
        chosen = jnp.where(frame[0] == FRAMES - 2, 0, 1)
        for row in range(2):
            put_columns(columns.at[1], row, cache[chosen, row].astype(F32))

    for frame_tap, out in ((0, two_later), (1, one_later)):
        source = columns.at[jnp.where(frame[0] >= FRAMES - 2 + frame_tap, 1, 0)]
        out[...] = jnp.dot(source[...], weight[frame_tap, 1], preferred_element_type=F32)
        for side in range(2):
            out[pl.ds((1 - side) * width, width), :] += jnp.dot(
                source[side * width : (side + 1) * width, :],
                weight[frame_tap, 2 * side],
                preferred_element_type=F32,
            )


def conv_edges_body(frame_tap, frame, above, below, gain, weight, local_sum, out, columns):
    width = above.shape[1]
    cached = frame[0] >= FRAMES - 2 + frame_tap

    @pl.when(cached)
    def _():
        for side, halo in enumerate((above, below)):
            put_columns(columns, side, halo[1].astype(F32))

    @pl.when(jnp.logical_not(cached))
    def _():
        for side, halo in enumerate((above, below)):
            put_columns(columns, side, activate(halo[0], gain[...]))

    for side in range(2):
        rows = pl.ds(side * width, width)
        product = jnp.dot(
            columns[side * width : (side + 1) * width, :],
            weight[frame_tap, 2 * side],
            preferred_element_type=F32,
        )
        out[rows, :] = (local_sum[rows, :] + product).astype(BF16)


def conv_own_body(above, below, gain, weight, inner, own, columns):
    width = above.shape[1]
    rows = own.shape[0]
    put_columns(columns, 0, activate(above[0], gain[...]))
    columns[width : width + rows, :] = inner[0]
    put_columns(columns, 1 + rows // width, activate(below[0], gain[...]))
    for row_tap in range(3):
        product = jnp.dot(
            columns[row_tap * width : row_tap * width + rows, :],
            weight[2, row_tap],
            preferred_element_type=F32,
        )
        if row_tap == 0:
            own[...] = product
        else:
            own[...] += product


def hidden_body(feat, own, one, two, bias, gain, hidden, normed):
    values = feat[...].astype(F32).reshape(own.shape)
    branch = own[...] + one[...].astype(F32) + two[...].astype(F32) + bias[...]
    result = (values + branch).astype(BF16)
    hidden[...] = result
    normed[...] = rms_scaled(result.astype(F32), gain[...]).astype(BF16)


def query_body(normed, weight, bias, query, shift):
    channels = normed.shape[1]
    scale = math.log2(math.e) / math.sqrt(channels)
    q = jnp.dot(normed[...], weight[:, :channels], preferred_element_type=F32) + bias[:, :channels]
    q = q.astype(BF16)
    absorbed = lax.dot_general(
        q, weight[:, channels : 2 * channels], (((1,), (1,)), ((), ())), preferred_element_type=F32
    )
    query[...] = (absorbed * scale).astype(BF16)
    key_bias = bias[:, channels : 2 * channels]
    shift[...] = as_row(jnp.sum(q.astype(F32) * key_bias, axis=-1, keepdims=True) * scale, channels)


def as_row(column, width):
    shape = column.shape[0], width
    row = lax.broadcasted_iota(jnp.int32, shape, 0)
    lane = lax.broadcasted_iota(jnp.int32, shape, 1)
    return jnp.sum(jnp.where(row == lane, column, 0.0), axis=0, keepdims=True)


def widen(lanes, width):
    return jnp.concatenate([lanes] * (-(-width // LANES)), axis=1)[:, :width]


def attend_body(chunks, first, strips, *refs):
    count = GROUP if first else 1
    given, refs = refs[:count], refs[count:]
    pieces, refs = refs[:chunks], refs[chunks:]
    if not first:
        (total_in, top_in), refs = refs[:2], refs[2:]
    outs, keys = refs[:-1], refs[-1]
    channels = pieces[0].shape[1]
    if first:
        queries = outs[2]
        strip = given[0].shape[0]
        for number, query in enumerate(given):
            queries[number * strip : (number + 1) * strip, :] = query[...]
    else:
        queries = given[0]
    strip = queries.shape[0] // GROUP
    start = 0
    for piece in pieces:
        keys[start : start + piece.shape[0], :channels] = piece[...]
        start += piece.shape[0]
    keys[:, channels:] = jnp.ones((start, LANES), BF16)
    if strips:
        blocks = [slice(number * strip, (number + 1) * strip) for number in strips]
    else:
        rows = queries.shape[0] // BLOCKS
        blocks = [slice(block * rows, (block + 1) * rows) for block in range(BLOCKS)]
    for number, block in enumerate(blocks):
        scores = lax.dot_general(
            queries[block, :], keys[:, :channels], (((1,), (1,)), ((), ())),
            preferred_element_type=F32,
        )
        top = jnp.broadcast_to(jnp.max(scores, axis=1, keepdims=True), (scores.shape[0], LANES))
        if not first:
            old_top = top_in[block, :]
            top = jnp.maximum(top, old_top)
        weights = jnp.exp2(scores - widen(top, start)).astype(BF16)
        total = jnp.dot(weights, keys[...], preferred_element_type=F32)
        if not first:
            factor = jnp.exp2(old_top - top)
            total = total + total_in[block, :] * widen(factor, channels + LANES)
        if not strips:
            outs[0][block, :] = total
            outs[1][block, :] = top
            continue
        out = outs[number]
        denominator = total[:, channels:]
        out[:strip, :] = (total[:, :channels] * widen(1.0 / denominator, channels)).astype(BF16)
        level = as_row(widen(top + jnp.log2(denominator), channels), channels)
        high = level.astype(BF16).astype(F32)
        middle = (level - high).astype(BF16).astype(F32)
        low = level - high - middle
        stat = lax.broadcasted_iota(jnp.int32, (STAT_ROWS, channels), 0)
        stats = jnp.where(stat == 0, high, jnp.where(stat == 1, middle, jnp.where(stat == 2, low, 0.0)))
        out[strip:, :] = stats.astype(BF16)


def merge_body(part0, part1, part2, part3, shift, hidden, weight, bias, out_weight, out_bias, mixed):
    rows, channels = hidden.shape
    parts = (part0, part1, part2, part3)
    levels = []
    for part in parts:
        stats = part[rows:, :].astype(F32)
        levels.append(stats[0:1] + stats[1:2] + stats[2:3] + shift[...])
    top = functools.reduce(jnp.maximum, levels)
    shares = [jnp.exp2(level - top) for level in levels]
    inverse = 1.0 / sum(shares)
    shares = jnp.concatenate([share * inverse for share in shares] * 2, axis=0)
    shares = jnp.transpose(shares)[:rows]
    total = sum(
        shares[:, number : number + 1] * part[:rows, :].astype(F32)
        for number, part in enumerate(parts)
    )
    attended = jnp.dot(
        total.astype(BF16), weight[:, 2 * channels :], preferred_element_type=F32
    ) + bias[:, 2 * channels :]
    result = jnp.dot(attended.astype(BF16), out_weight[...], preferred_element_type=F32)
    result = result + out_bias[...] + hidden[...].astype(F32)
    mixed[...] = result.astype(BF16)


def along_y(x, by):
    pairs = [
        (z * GROUP + y, z * GROUP + (y + by) % GROUP) for z in range(RING) for y in range(GROUP)
    ]
    return lax.ppermute(x, "strip", pairs)


def along_z(x, by):
    pairs = [
        (z * GROUP + y, (z + by) % RING * GROUP + y) for z in range(RING) for y in range(GROUP)
    ]
    return lax.ppermute(x, "strip", pairs)


def local(
    feature,
    frame_cache,
    norm_gain,
    conv_weight,
    conv_bias,
    attn_gain,
    qkv_weight,
    qkv_bias,
    out_weight,
    out_bias,
):
    _, height, width, channels = feature.shape
    rows = height * width
    half = rows // 2
    feat = feature[0]
    frame = lax.axis_index("tm")
    weight = conv_weight.reshape(3, 3, 3 * channels, channels)
    qkv_bias = qkv_bias.reshape(1, 3 * channels)

    frame_number = frame.reshape(1).astype(jnp.int32)
    to_below, to_above = call(
        halo_body,
        "halo",
        [((2, width, channels), BF16)] * 2,
        [SMEM, HBM, HBM],
        20 << 30,
        [pltpu.SemaphoreType.DMA((4,))],
    )(frame_number, pinned(feat), pinned(frame_cache))
    above = lax.ppermute(to_below, "strip", [(s, s + 1) for s in range(ROW_STRIPS - 1)])
    below = lax.ppermute(to_above, "strip", [(s + 1, s) for s in range(ROW_STRIPS - 1)])

    flops = 2 * rows * 3 * channels * channels
    two_local, one_local, inner, gain = call(
        conv_local_body,
        "conv_local",
        [
            ((rows, channels), F32),
            ((rows, channels), F32),
            ((2, rows, 3 * channels), BF16),
            ((1, channels), F32),
        ],
        [SMEM, VMEM, VMEM, VMEM, VMEM],
        4 * flops,
    )(frame_number, feat, frame_cache, norm_gain, weight)

    def conv_edges(name, frame_tap, local_sum):
        return call(
            functools.partial(conv_edges_body, frame_tap),
            name,
            [((rows, channels), BF16)],
            [SMEM] + [VMEM] * 5,
            flops,
            [pltpu.VMEM((rows, 3 * channels), BF16)],
        )(frame_number, above, below, gain, weight, local_sum)[0]

    two = lax.ppermute(
        conv_edges("conv_edges_two", 0, two_local),
        "tm",
        [(f, (f + 2) % FRAMES) for f in range(FRAMES)],
    )
    one = lax.ppermute(
        conv_edges("conv_edges_one", 1, one_local),
        "tm",
        [(f, (f + 1) % FRAMES) for f in range(FRAMES)],
    )
    (own,) = call(
        conv_own_body,
        "conv_own",
        [((rows, channels), F32)],
        [VMEM] * 5,
        3 * flops,
        [pltpu.VMEM((2 * width + rows, 3 * channels), BF16)],
    )(above, below, gain, weight, inner)
    hidden, normed = call(
        hidden_body,
        "hidden",
        [((rows, channels), BF16)] * 2,
        [VMEM] * 6,
        rows * channels * 20,
    )(feat, own, one, two, conv_bias.reshape(1, channels), attn_gain.reshape(1, channels))
    query, shift = call(
        query_body,
        "query",
        [((rows, channels), BF16), ((1, channels), F32)],
        [VMEM] * 3,
        4 * rows * channels * channels,
    )(normed, qkv_weight, qkv_bias)

    def attend(name, given, pieces, state=(), strips=()):
        if strips:
            outs = [((rows + STAT_ROWS, channels), BF16)] * len(strips)
        else:
            outs = [((GROUP * rows, channels + LANES), F32), ((GROUP * rows, LANES), F32)]
        if not state:
            outs.append(((GROUP * rows, channels), BF16))
        keys = sum(piece.shape[0] for piece in pieces)
        return call(
            functools.partial(attend_body, len(pieces), not state, strips),
            name,
            outs,
            [VMEM] * (len(given) + len(pieces) + len(state)),
            4 * (len(strips) or GROUP) * rows * keys * channels,
            [pltpu.VMEM((keys, channels + LANES), BF16)],
            32 << 20,
        )(*given, *pieces, *state)

    queries = [query] + [along_y(query, -by) for by in range(1, GROUP)]
    forward, backward = [normed], [normed]
    for step in range(3):
        forward.append(along_z(forward[-1], 1))
        backward.append(along_z(backward[-1], -1))
        if step == 0:
            forward[1], backward[1], _ = lax.optimization_barrier(
                (forward[1], backward[1], query)
            )
        if step == 1:
            forward[2], backward[2], queries[1], queries[3] = lax.optimization_barrier(
                (forward[2], backward[2], queries[1], queries[3])
            )
    last = [along_z(forward[2][:half], 2), along_z(backward[2][half:], -2)]
    *state, query_rows = attend("attend_near", queries, forward[:3] + backward[1:3])
    state = attend("attend_far", [query_rows], [forward[3], backward[3]], state)
    parts = {}
    for strips in ((2,), (1, 3), (0,)):
        name = "attend_last_" + "_".join(map(str, strips))
        parts.update(zip(strips, attend(name, [query_rows], last, state, strips)))
    arrived = {by: along_y(parts[by], by) for by in (2, 1, 3)}
    arrived = [arrived[by] for by in range(1, GROUP)]
    (mixed,) = call(
        merge_body,
        "merge",
        [((rows, channels), BF16)],
        [VMEM] * 10,
        4 * rows * channels * channels,
    )(parts[0], *arrived, shift, hidden, qkv_weight, qkv_bias, out_weight, out_bias.reshape(1, channels))
    return mixed.reshape(feature.shape)


def solution(mesh):
    in_specs = (P("tm", "strip", None, None), P(None, "strip", None, None)) + (P(),) * 8
    out_specs = P("tm", "strip", None, None)
    return jax.shard_map(local, mesh=mesh, in_specs=in_specs, out_specs=out_specs, check_vma=False)
```

```python
import functools
import math

import jax
import jax.numpy as jnp
from jax import lax
from jax.experimental import pallas as pl
from jax.experimental.pallas import tpu as pltpu
from jax.sharding import PartitionSpec as P

EPSILON = 1e-06
FRAMES = 8
ROW_STRIPS = 32
RING = 8
GROUP = 4
STAT_ROWS = 16
LANES = 128
MOST = (0, 1, 3)
BLOCKS = 2
VMEM = pl.BlockSpec(memory_space=pltpu.VMEM)
SMEM = pl.BlockSpec(memory_space=pltpu.SMEM)
HBM = pl.BlockSpec(memory_space=pltpu.HBM)
F32 = jnp.float32
BF16 = jnp.bfloat16
VMEM_LIMIT = 16 << 20


def pinned(x):
    return pltpu.with_memory_space_constraint(x, pltpu.HBM)


def call(body, name, outs, in_specs, flops, scratch=(), limit=VMEM_LIMIT):
    return pl.pallas_call(
        body,
        name=name,
        out_shape=[jax.ShapeDtypeStruct(*out) for out in outs],
        in_specs=in_specs,
        out_specs=[VMEM] * len(outs),
        scratch_shapes=list(scratch),
        cost_estimate=pl.CostEstimate(flops=int(flops), bytes_accessed=2 << 20, transcendentals=0),
        compiler_params=pltpu.CompilerParams(vmem_limit_bytes=limit),
    )


def rms_scaled(values, gain):
    mean_square = jnp.mean(values * values, axis=-1, keepdims=True)
    return values * lax.rsqrt(mean_square + EPSILON) * gain


def activate(row, gain):
    u = rms_scaled(row.astype(F32), gain)
    return u / (1.0 + jnp.exp(-u))


def put_columns(target, place, row):
    width, channels = row.shape
    column = lax.broadcasted_iota(jnp.int32, row.shape, 0)
    left = jnp.where(column == 0, 0.0, pltpu.roll(row, 1, 0))
    right = jnp.where(column == width - 1, 0.0, pltpu.roll(row, width - 1, 0))
    rows = pl.ds(place * width, width)
    target[rows, 0:channels] = left.astype(BF16)
    target[rows, channels : 2 * channels] = row.astype(BF16)
    target[rows, 2 * channels : 3 * channels] = right.astype(BF16)


def halo_body(frame, feature, frame_cache, to_below, to_above, sems):
    chosen = jnp.where(frame[0] == FRAMES - 2, 0, 1)
    last = feature.shape[0] - 1
    copies = [
        pltpu.make_async_copy(feature.at[last], to_below.at[0], sems.at[0]),
        pltpu.make_async_copy(frame_cache.at[chosen, last], to_below.at[1], sems.at[1]),
        pltpu.make_async_copy(feature.at[0], to_above.at[0], sems.at[2]),
        pltpu.make_async_copy(frame_cache.at[chosen, 0], to_above.at[1], sems.at[3]),
    ]
    for copy in copies:
        copy.start()
    for copy in copies:
        copy.wait()


def conv_local_body(frame, feat, cache, gain, weight, two_later, one_later, columns, row_gain):
    width = feat.shape[1]
    scale = gain[...].reshape(1, -1)
    row_gain[...] = scale
    for row in range(2):
        put_columns(columns.at[0], row, activate(feat[row], scale))

    @pl.when(frame[0] >= FRAMES - 2)
    def _():
        chosen = jnp.where(frame[0] == FRAMES - 2, 0, 1)
        for row in range(2):
            put_columns(columns.at[1], row, cache[chosen, row].astype(F32))

    for frame_tap, out in ((0, two_later), (1, one_later)):
        source = columns.at[jnp.where(frame[0] >= FRAMES - 2 + frame_tap, 1, 0)]
        out[...] = jnp.dot(source[...], weight[frame_tap, 1], preferred_element_type=F32)
        for side in range(2):
            out[pl.ds((1 - side) * width, width), :] += jnp.dot(
                source[side * width : (side + 1) * width, :],
                weight[frame_tap, 2 * side],
                preferred_element_type=F32,
            )


def conv_edges_body(frame_tap, frame, above, below, gain, weight, local_sum, out, columns):
    width = above.shape[1]
    cached = frame[0] >= FRAMES - 2 + frame_tap

    @pl.when(cached)
    def _():
        for side, halo in enumerate((above, below)):
            put_columns(columns, side, halo[1].astype(F32))

    @pl.when(jnp.logical_not(cached))
    def _():
        for side, halo in enumerate((above, below)):
            put_columns(columns, side, activate(halo[0], gain[...]))

    for side in range(2):
        rows = pl.ds(side * width, width)
        product = jnp.dot(
            columns[side * width : (side + 1) * width, :],
            weight[frame_tap, 2 * side],
            preferred_element_type=F32,
        )
        out[rows, :] = (local_sum[rows, :] + product).astype(BF16)


def conv_own_body(above, below, gain, weight, inner, own, columns):
    width = above.shape[1]
    rows = own.shape[0]
    put_columns(columns, 0, activate(above[0], gain[...]))
    columns[width : width + rows, :] = inner[0]
    put_columns(columns, 1 + rows // width, activate(below[0], gain[...]))
    for row_tap in range(3):
        product = jnp.dot(
            columns[row_tap * width : row_tap * width + rows, :],
            weight[2, row_tap],
            preferred_element_type=F32,
        )
        if row_tap == 0:
            own[...] = product
        else:
            own[...] += product


def hidden_body(feat, own, one, two, bias, gain, hidden, normed):
    values = feat[...].astype(F32).reshape(own.shape)
    branch = own[...] + one[...].astype(F32) + two[...].astype(F32) + bias[...]
    result = (values + branch).astype(BF16)
    hidden[...] = result
    normed[...] = rms_scaled(result.astype(F32), gain[...]).astype(BF16)


def query_body(normed, weight, bias, query, shift):
    channels = normed.shape[1]
    scale = math.log2(math.e) / math.sqrt(channels)
    q = jnp.dot(normed[...], weight[:, :channels], preferred_element_type=F32) + bias[:, :channels]
    q = q.astype(BF16)
    absorbed = lax.dot_general(
        q, weight[:, channels : 2 * channels], (((1,), (1,)), ((), ())), preferred_element_type=F32
    )
    query[...] = (absorbed * scale).astype(BF16)
    key_bias = bias[:, channels : 2 * channels]
    shift[...] = as_row(jnp.sum(q.astype(F32) * key_bias, axis=-1, keepdims=True) * scale, channels)


def as_row(column, width):
    shape = column.shape[0], width
    row = lax.broadcasted_iota(jnp.int32, shape, 0)
    lane = lax.broadcasted_iota(jnp.int32, shape, 1)
    return jnp.sum(jnp.where(row == lane, column, 0.0), axis=0, keepdims=True)


def widen(lanes, width):
    return jnp.concatenate([lanes] * (-(-width // LANES)), axis=1)[:, :width]


def attend_body(chunks, first, strip, strips, *refs):
    count = first or 1
    given, refs = refs[:count], refs[count:]
    pieces, refs = refs[:chunks], refs[chunks:]
    if not first:
        (total_in, top_in), refs = refs[:2], refs[2:]
    outs, keys = refs[:-1], refs[-1]
    channels = pieces[0].shape[1]
    if first:
        queries = outs[2]
        for number, query in enumerate(given):
            queries[number * strip : (number + 1) * strip, :] = query[...]
    else:
        queries = given[0]
    start = 0
    for piece in pieces:
        keys[start : start + piece.shape[0], :channels] = piece[...]
        start += piece.shape[0]
    keys[:, channels:] = jnp.ones((start, LANES), BF16)
    if strips:
        blocks = [slice(number * strip, (number + 1) * strip) for number in strips]
    else:
        count = 1 if queries.shape[0] == strip else BLOCKS
        rows = queries.shape[0] // count
        blocks = [slice(block * rows, (block + 1) * rows) for block in range(count)]
    for number, block in enumerate(blocks):
        scores = lax.dot_general(
            queries[block, :], keys[:, :channels], (((1,), (1,)), ((), ())),
            preferred_element_type=F32,
        )
        top = jnp.broadcast_to(jnp.max(scores, axis=1, keepdims=True), (scores.shape[0], LANES))
        if not first:
            old_top = top_in[block, :]
            top = jnp.maximum(top, old_top)
        weights = jnp.exp2(scores - widen(top, start)).astype(BF16)
        total = jnp.dot(weights, keys[...], preferred_element_type=F32)
        if not first:
            factor = jnp.exp2(old_top - top)
            total = total + total_in[block, :] * widen(factor, channels + LANES)
        if not strips:
            outs[0][block, :] = total
            outs[1][block, :] = top
            continue
        out = outs[number]
        denominator = total[:, channels:]
        out[:strip, :] = (total[:, :channels] * widen(1.0 / denominator, channels)).astype(BF16)
        level = as_row(widen(top + jnp.log2(denominator), channels), channels)
        high = level.astype(BF16).astype(F32)
        middle = (level - high).astype(BF16).astype(F32)
        low = level - high - middle
        stat = lax.broadcasted_iota(jnp.int32, (STAT_ROWS, channels), 0)
        stats = jnp.where(stat == 0, high, jnp.where(stat == 1, middle, jnp.where(stat == 2, low, 0.0)))
        out[strip:, :] = stats.astype(BF16)


def merge_body(part0, part1, part2, part3, shift, hidden, weight, bias, out_weight, out_bias, mixed):
    rows, channels = hidden.shape
    parts = (part0, part1, part2, part3)
    levels = []
    for part in parts:
        stats = part[rows:, :].astype(F32)
        levels.append(stats[0:1] + stats[1:2] + stats[2:3] + shift[...])
    top = functools.reduce(jnp.maximum, levels)
    shares = [jnp.exp2(level - top) for level in levels]
    inverse = 1.0 / sum(shares)
    shares = jnp.concatenate([share * inverse for share in shares] * 2, axis=0)
    shares = jnp.transpose(shares)[:rows]
    total = sum(
        shares[:, number : number + 1] * part[:rows, :].astype(F32)
        for number, part in enumerate(parts)
    )
    attended = jnp.dot(
        total.astype(BF16), weight[:, 2 * channels :], preferred_element_type=F32
    ) + bias[:, 2 * channels :]
    result = jnp.dot(attended.astype(BF16), out_weight[...], preferred_element_type=F32)
    result = result + out_bias[...] + hidden[...].astype(F32)
    mixed[...] = result.astype(BF16)


def along_y(x, by):
    pairs = [
        (z * GROUP + y, z * GROUP + (y + by) % GROUP) for z in range(RING) for y in range(GROUP)
    ]
    return lax.ppermute(x, "strip", pairs)


def along_z(x, by):
    pairs = [
        (z * GROUP + y, (z + by) % RING * GROUP + y) for z in range(RING) for y in range(GROUP)
    ]
    return lax.ppermute(x, "strip", pairs)


def local(
    feature,
    frame_cache,
    norm_gain,
    conv_weight,
    conv_bias,
    attn_gain,
    qkv_weight,
    qkv_bias,
    out_weight,
    out_bias,
):
    _, height, width, channels = feature.shape
    rows = height * width
    half = rows // 2
    feat = feature[0]
    frame = lax.axis_index("tm")
    weight = conv_weight.reshape(3, 3, 3 * channels, channels)
    qkv_bias = qkv_bias.reshape(1, 3 * channels)

    frame_number = frame.reshape(1).astype(jnp.int32)
    to_below, to_above = call(
        halo_body,
        "halo",
        [((2, width, channels), BF16)] * 2,
        [SMEM, HBM, HBM],
        20 << 30,
        [pltpu.SemaphoreType.DMA((4,))],
    )(frame_number, pinned(feat), pinned(frame_cache))
    above = lax.ppermute(to_below, "strip", [(s, s + 1) for s in range(ROW_STRIPS - 1)])
    below = lax.ppermute(to_above, "strip", [(s + 1, s) for s in range(ROW_STRIPS - 1)])

    flops = 2 * rows * 3 * channels * channels
    two_local, one_local, inner, gain = call(
        conv_local_body,
        "conv_local",
        [
            ((rows, channels), F32),
            ((rows, channels), F32),
            ((2, rows, 3 * channels), BF16),
            ((1, channels), F32),
        ],
        [SMEM, VMEM, VMEM, VMEM, VMEM],
        4 * flops,
    )(frame_number, feat, frame_cache, norm_gain, weight)

    def conv_edges(name, frame_tap, local_sum):
        return call(
            functools.partial(conv_edges_body, frame_tap),
            name,
            [((rows, channels), BF16)],
            [SMEM] + [VMEM] * 5,
            flops,
            [pltpu.VMEM((rows, 3 * channels), BF16)],
        )(frame_number, above, below, gain, weight, local_sum)[0]

    two = lax.ppermute(
        conv_edges("conv_edges_two", 0, two_local),
        "tm",
        [(f, (f + 2) % FRAMES) for f in range(FRAMES)],
    )
    one = lax.ppermute(
        conv_edges("conv_edges_one", 1, one_local),
        "tm",
        [(f, (f + 1) % FRAMES) for f in range(FRAMES)],
    )
    (own,) = call(
        conv_own_body,
        "conv_own",
        [((rows, channels), F32)],
        [VMEM] * 5,
        3 * flops,
        [pltpu.VMEM((2 * width + rows, 3 * channels), BF16)],
    )(above, below, gain, weight, inner)
    hidden, normed = call(
        hidden_body,
        "hidden",
        [((rows, channels), BF16)] * 2,
        [VMEM] * 6,
        rows * channels * 20,
    )(feat, own, one, two, conv_bias.reshape(1, channels), attn_gain.reshape(1, channels))
    query, shift = call(
        query_body,
        "query",
        [((rows, channels), BF16), ((1, channels), F32)],
        [VMEM] * 3,
        4 * rows * channels * channels,
    )(normed, qkv_weight, qkv_bias)

    def attend(name, given, pieces, state=(), strips=()):
        count = sum(x.shape[0] for x in given)
        if strips:
            outs = [((rows + STAT_ROWS, channels), BF16)] * len(strips)
        else:
            outs = [((count, channels + LANES), F32), ((count, LANES), F32)]
        if not state:
            outs.append(((count, channels), BF16))
        keys = sum(piece.shape[0] for piece in pieces)
        return call(
            functools.partial(attend_body, len(pieces), 0 if state else len(given), rows, strips),
            name,
            outs,
            [VMEM] * (len(given) + len(pieces) + len(state)),
            4 * (len(strips) * rows or count) * keys * channels,
            [pltpu.VMEM((keys, channels + LANES), BF16)],
            32 << 20,
        )(*given, *pieces, *state)

    queries = [query] + [along_y(query, -by) for by in range(1, GROUP)]
    forward, backward = [normed], [normed]
    for step in range(3):
        forward.append(along_z(forward[-1], 1))
        backward.append(along_z(backward[-1], -1))
        if step == 0:
            forward[1], backward[1], _ = lax.optimization_barrier(
                (forward[1], backward[1], query)
            )
        if step == 1:
            *most, most_rows = attend(
                "attend_most_near",
                [queries[number] for number in MOST],
                [normed, forward[1], backward[1]],
            )
            forward[2], backward[2], *most = lax.optimization_barrier(
                (forward[2], backward[2], *most)
            )
    last = [along_z(forward[2][:half], 2), along_z(backward[2][half:], -2)]
    most = attend("attend_most_middle", [most_rows], [forward[2], backward[2]], most)
    most = attend("attend_most_far", [most_rows], [forward[3], backward[3]], most)
    *other, other_rows = attend("attend_other", [queries[2]], forward + backward[1:])
    last[0], last[1], *most = lax.optimization_barrier((*last, *most))
    parts = [None] * GROUP
    (parts[2],) = attend("attend_last_2", [other_rows], last, other, (0,))
    parts[1], parts[3] = attend("attend_last_1_3", [most_rows], last, most, (1, 2))
    (parts[0],) = attend("attend_last_0", [most_rows], last, most, (0,))
    arrived = {by: along_y(parts[by], by) for by in (2, 1, 3)}
    arrived = [arrived[by] for by in range(1, GROUP)]
    (mixed,) = call(
        merge_body,
        "merge",
        [((rows, channels), BF16)],
        [VMEM] * 10,
        4 * rows * channels * channels,
    )(parts[0], *arrived, shift, hidden, qkv_weight, qkv_bias, out_weight, out_bias.reshape(1, channels))
    return mixed.reshape(feature.shape)


def solution(mesh):
    in_specs = (P("tm", "strip", None, None), P(None, "strip", None, None)) + (P(),) * 8
    out_specs = P("tm", "strip", None, None)
    return jax.shard_map(local, mesh=mesh, in_specs=in_specs, out_specs=out_specs, check_vma=False)
```

```python
import functools
import math

import jax
import jax.numpy as jnp
from jax import lax
from jax.experimental import pallas as pl
from jax.experimental.pallas import tpu as pltpu
from jax.sharding import PartitionSpec as P

EPSILON = 1e-06
FRAMES = 8
ROW_STRIPS = 32
RING = 8
GROUP = 4
STAT_ROWS = 16
LANES = 128
BLOCKS = 2
VMEM = pl.BlockSpec(memory_space=pltpu.VMEM)
SMEM = pl.BlockSpec(memory_space=pltpu.SMEM)
HBM = pl.BlockSpec(memory_space=pltpu.HBM)
F32 = jnp.float32
BF16 = jnp.bfloat16
VMEM_LIMIT = 16 << 20


def pinned(x):
    return pltpu.with_memory_space_constraint(x, pltpu.HBM)


def call(body, name, outs, in_specs, flops, scratch=(), limit=VMEM_LIMIT, out_spec=VMEM):
    return pl.pallas_call(
        body,
        name=name,
        out_shape=[jax.ShapeDtypeStruct(*out) for out in outs],
        in_specs=in_specs,
        out_specs=[out_spec] * len(outs),
        scratch_shapes=list(scratch),
        cost_estimate=pl.CostEstimate(flops=int(flops), bytes_accessed=2 << 20, transcendentals=0),
        compiler_params=pltpu.CompilerParams(vmem_limit_bytes=limit),
    )


def rms_scaled(values, gain):
    mean_square = jnp.mean(values * values, axis=-1, keepdims=True)
    return values * lax.rsqrt(mean_square + EPSILON) * gain


def activate(row, gain):
    u = rms_scaled(row.astype(F32), gain)
    return u / (1.0 + jnp.exp(-u))


def put_columns(target, place, row):
    width, channels = row.shape
    column = lax.broadcasted_iota(jnp.int32, row.shape, 0)
    left = jnp.where(column == 0, 0.0, pltpu.roll(row, 1, 0))
    right = jnp.where(column == width - 1, 0.0, pltpu.roll(row, width - 1, 0))
    rows = pl.ds(place * width, width)
    target[rows, 0:channels] = left.astype(BF16)
    target[rows, channels : 2 * channels] = row.astype(BF16)
    target[rows, 2 * channels : 3 * channels] = right.astype(BF16)


def halo_body(frame, feature, frame_cache, to_below, to_above, sems):
    chosen = jnp.where(frame[0] == FRAMES - 2, 0, 1)
    last = feature.shape[0] - 1
    copies = [
        pltpu.make_async_copy(feature.at[last], to_below.at[0], sems.at[0]),
        pltpu.make_async_copy(frame_cache.at[chosen, last], to_below.at[1], sems.at[1]),
        pltpu.make_async_copy(feature.at[0], to_above.at[0], sems.at[2]),
        pltpu.make_async_copy(frame_cache.at[chosen, 0], to_above.at[1], sems.at[3]),
    ]
    for copy in copies:
        copy.start()
    for copy in copies:
        copy.wait()


def conv_local_body(frame, feat, cache, gain, weight, two_later, one_later, columns, row_gain):
    width = feat.shape[1]
    scale = gain[...].reshape(1, -1)
    row_gain[...] = scale
    for row in range(2):
        put_columns(columns.at[0], row, activate(feat[row], scale))

    @pl.when(frame[0] >= FRAMES - 2)
    def _():
        chosen = jnp.where(frame[0] == FRAMES - 2, 0, 1)
        for row in range(2):
            put_columns(columns.at[1], row, cache[chosen, row].astype(F32))

    for frame_tap, out in ((0, two_later), (1, one_later)):
        source = columns.at[jnp.where(frame[0] >= FRAMES - 2 + frame_tap, 1, 0)]
        out[...] = jnp.dot(source[...], weight[frame_tap, 1], preferred_element_type=F32)
        for side in range(2):
            out[pl.ds((1 - side) * width, width), :] += jnp.dot(
                source[side * width : (side + 1) * width, :],
                weight[frame_tap, 2 * side],
                preferred_element_type=F32,
            )


def conv_edges_body(frame_tap, frame, above, below, gain, weight, local_sum, out, columns):
    width = above.shape[1]
    cached = frame[0] >= FRAMES - 2 + frame_tap

    @pl.when(cached)
    def _():
        for side, halo in enumerate((above, below)):
            put_columns(columns, side, halo[1].astype(F32))

    @pl.when(jnp.logical_not(cached))
    def _():
        for side, halo in enumerate((above, below)):
            put_columns(columns, side, activate(halo[0], gain[...]))

    for side in range(2):
        rows = pl.ds(side * width, width)
        product = jnp.dot(
            columns[side * width : (side + 1) * width, :],
            weight[frame_tap, 2 * side],
            preferred_element_type=F32,
        )
        out[rows, :] = (local_sum[rows, :] + product).astype(BF16)


def conv_own_body(above, below, gain, weight, inner, own, columns):
    width = above.shape[1]
    rows = own.shape[0]
    put_columns(columns, 0, activate(above[0], gain[...]))
    columns[width : width + rows, :] = inner[0]
    put_columns(columns, 1 + rows // width, activate(below[0], gain[...]))
    for row_tap in range(3):
        product = jnp.dot(
            columns[row_tap * width : row_tap * width + rows, :],
            weight[2, row_tap],
            preferred_element_type=F32,
        )
        if row_tap == 0:
            own[...] = product
        else:
            own[...] += product


def hidden_body(feat, own, one, two, bias, gain, hidden, normed):
    values = feat[...].astype(F32).reshape(own.shape)
    branch = own[...] + one[...].astype(F32) + two[...].astype(F32) + bias[...]
    result = (values + branch).astype(BF16)
    hidden[...] = result
    normed[...] = rms_scaled(result.astype(F32), gain[...]).astype(BF16)


def query_body(normed, weight, bias, query, shift):
    channels = normed.shape[1]
    scale = math.log2(math.e) / math.sqrt(channels)
    q = jnp.dot(normed[...], weight[:, :channels], preferred_element_type=F32) + bias[:, :channels]
    q = q.astype(BF16)
    absorbed = lax.dot_general(
        q, weight[:, channels : 2 * channels], (((1,), (1,)), ((), ())), preferred_element_type=F32
    )
    query[...] = (absorbed * scale).astype(BF16)
    key_bias = bias[:, channels : 2 * channels]
    shift[...] = as_row(jnp.sum(q.astype(F32) * key_bias, axis=-1, keepdims=True) * scale, channels)


def as_row(column, width):
    shape = column.shape[0], width
    row = lax.broadcasted_iota(jnp.int32, shape, 0)
    lane = lax.broadcasted_iota(jnp.int32, shape, 1)
    return jnp.sum(jnp.where(row == lane, column, 0.0), axis=0, keepdims=True)


def widen(lanes, width):
    return jnp.concatenate([lanes] * (-(-width // LANES)), axis=1)[:, :width]


def attend_body(chunks, first, strips, *refs):
    count = GROUP if first else 1
    given, refs = refs[:count], refs[count:]
    pieces, refs = refs[:chunks], refs[chunks:]
    if not first:
        (total_in, top_in), refs = refs[:2], refs[2:]
    outs, keys = refs[:-1], refs[-1]
    channels = pieces[0].shape[1]
    if first:
        queries = outs[2]
        strip = given[0].shape[0]
        for number, query in enumerate(given):
            queries[number * strip : (number + 1) * strip, :] = query[...]
    else:
        queries = given[0]
    strip = queries.shape[0] // GROUP
    start = 0
    for piece in pieces:
        keys[start : start + piece.shape[0], :channels] = piece[...]
        start += piece.shape[0]
    keys[:, channels:] = jnp.ones((start, LANES), BF16)
    if strips:
        blocks = [slice(number * strip, (number + 1) * strip) for number in strips]
    else:
        rows = queries.shape[0] // BLOCKS
        blocks = [slice(block * rows, (block + 1) * rows) for block in range(BLOCKS)]
    for number, block in enumerate(blocks):
        scores = lax.dot_general(
            queries[block, :], keys[:, :channels], (((1,), (1,)), ((), ())),
            preferred_element_type=F32,
        )
        top = jnp.broadcast_to(jnp.max(scores, axis=1, keepdims=True), (scores.shape[0], LANES))
        if not first:
            old_top = top_in[block, :]
            top = jnp.maximum(top, old_top)
        weights = jnp.exp2(scores - widen(top, start)).astype(BF16)
        total = jnp.dot(weights, keys[...], preferred_element_type=F32)
        if not first:
            factor = jnp.exp2(old_top - top)
            total = total + total_in[block, :] * widen(factor, channels + LANES)
        if not strips:
            outs[0][block, :] = total
            outs[1][block, :] = top
            continue
        out = outs[number]
        denominator = total[:, channels:]
        out[:strip, :] = (total[:, :channels] * widen(1.0 / denominator, channels)).astype(BF16)
        level = as_row(widen(top + jnp.log2(denominator), channels), channels)
        high = level.astype(BF16).astype(F32)
        middle = (level - high).astype(BF16).astype(F32)
        low = level - high - middle
        stat = lax.broadcasted_iota(jnp.int32, (STAT_ROWS, channels), 0)
        stats = jnp.where(stat == 0, high, jnp.where(stat == 1, middle, jnp.where(stat == 2, low, 0.0)))
        out[strip:, :] = stats.astype(BF16)


def fold_body(weight, bias, out_weight, out_bias, folded, folded_bias):
    channels = out_weight.shape[0]
    folded[...] = jnp.dot(
        weight[:, 2 * channels :], out_weight[...], preferred_element_type=F32
    ).astype(BF16)
    value_bias = bias[:, 2 * channels :]
    high = value_bias.astype(BF16)
    low = (value_bias - high.astype(F32)).astype(BF16)
    both = jnp.concatenate([high, low] * 8, axis=0)
    product = jnp.dot(both, out_weight[...], preferred_element_type=F32)
    folded_bias[...] = product[0:1] + product[1:2] + out_bias[...]


def merge_body(part0, part1, part2, part3, shift, hidden, weight, bias, mixed, buffer, sems):
    rows = hidden.shape[0]
    half = rows // 2
    parts = (part0, part1, part2, part3)
    levels = []
    for part in parts:
        stats = part[rows:, :].astype(F32)
        levels.append(stats[0:1] + stats[1:2] + stats[2:3] + shift[...])
    top = functools.reduce(jnp.maximum, levels)
    shares = [jnp.exp2(level - top) for level in levels]
    inverse = 1.0 / sum(shares)
    shares = jnp.concatenate([share * inverse for share in shares] * 2, axis=0)
    shares = jnp.transpose(shares)[:rows]
    copies = []
    for side in range(2):
        inside = slice(side * half, (side + 1) * half)
        total = sum(
            shares[inside, number : number + 1] * part[inside, :].astype(F32)
            for number, part in enumerate(parts)
        )
        result = jnp.dot(total.astype(BF16), weight[...], preferred_element_type=F32)
        result = result + bias[...] + hidden[inside, :].astype(F32)
        buffer[inside, :] = result.astype(BF16)
        copies.append(pltpu.make_async_copy(buffer.at[inside], mixed.at[inside], sems.at[side]))
        copies[side].start()
    for copy in copies:
        copy.wait()


def along_y(x, by):
    pairs = [
        (z * GROUP + y, z * GROUP + (y + by) % GROUP) for z in range(RING) for y in range(GROUP)
    ]
    return lax.ppermute(x, "strip", pairs)


def along_z(x, by):
    pairs = [
        (z * GROUP + y, (z + by) % RING * GROUP + y) for z in range(RING) for y in range(GROUP)
    ]
    return lax.ppermute(x, "strip", pairs)


def local(
    feature,
    frame_cache,
    norm_gain,
    conv_weight,
    conv_bias,
    attn_gain,
    qkv_weight,
    qkv_bias,
    out_weight,
    out_bias,
):
    _, height, width, channels = feature.shape
    rows = height * width
    half = rows // 2
    feat = feature[0]
    frame = lax.axis_index("tm")
    weight = conv_weight.reshape(3, 3, 3 * channels, channels)
    qkv_bias = qkv_bias.reshape(1, 3 * channels)

    frame_number = frame.reshape(1).astype(jnp.int32)
    to_below, to_above = call(
        halo_body,
        "halo",
        [((2, width, channels), BF16)] * 2,
        [SMEM, HBM, HBM],
        20 << 30,
        [pltpu.SemaphoreType.DMA((4,))],
    )(frame_number, pinned(feat), pinned(frame_cache))
    above = lax.ppermute(to_below, "strip", [(s, s + 1) for s in range(ROW_STRIPS - 1)])
    below = lax.ppermute(to_above, "strip", [(s + 1, s) for s in range(ROW_STRIPS - 1)])

    flops = 2 * rows * 3 * channels * channels
    two_local, one_local, inner, gain = call(
        conv_local_body,
        "conv_local",
        [
            ((rows, channels), F32),
            ((rows, channels), F32),
            ((2, rows, 3 * channels), BF16),
            ((1, channels), F32),
        ],
        [SMEM, VMEM, VMEM, VMEM, VMEM],
        4 * flops,
    )(frame_number, feat, frame_cache, norm_gain, weight)

    def conv_edges(name, frame_tap, local_sum):
        return call(
            functools.partial(conv_edges_body, frame_tap),
            name,
            [((rows, channels), BF16)],
            [SMEM] + [VMEM] * 5,
            flops,
            [pltpu.VMEM((rows, 3 * channels), BF16)],
        )(frame_number, above, below, gain, weight, local_sum)[0]

    two = lax.ppermute(
        conv_edges("conv_edges_two", 0, two_local),
        "tm",
        [(f, (f + 2) % FRAMES) for f in range(FRAMES)],
    )
    one = lax.ppermute(
        conv_edges("conv_edges_one", 1, one_local),
        "tm",
        [(f, (f + 1) % FRAMES) for f in range(FRAMES)],
    )
    (own,) = call(
        conv_own_body,
        "conv_own",
        [((rows, channels), F32)],
        [VMEM] * 5,
        3 * flops,
        [pltpu.VMEM((2 * width + rows, 3 * channels), BF16)],
    )(above, below, gain, weight, inner)
    hidden, normed = call(
        hidden_body,
        "hidden",
        [((rows, channels), BF16)] * 2,
        [VMEM] * 6,
        rows * channels * 20,
    )(feat, own, one, two, conv_bias.reshape(1, channels), attn_gain.reshape(1, channels))
    query, shift = call(
        query_body,
        "query",
        [((rows, channels), BF16), ((1, channels), F32)],
        [VMEM] * 3,
        4 * rows * channels * channels,
    )(normed, qkv_weight, qkv_bias)

    def attend(name, given, pieces, state=(), strips=()):
        if strips:
            outs = [((rows + STAT_ROWS, channels), BF16)] * len(strips)
        else:
            outs = [((GROUP * rows, channels + LANES), F32), ((GROUP * rows, LANES), F32)]
        if not state:
            outs.append(((GROUP * rows, channels), BF16))
        keys = sum(piece.shape[0] for piece in pieces)
        return call(
            functools.partial(attend_body, len(pieces), not state, strips),
            name,
            outs,
            [VMEM] * (len(given) + len(pieces) + len(state)),
            4 * (len(strips) or GROUP) * rows * keys * channels,
            [pltpu.VMEM((keys, channels + LANES), BF16)],
            32 << 20,
        )(*given, *pieces, *state)

    queries = [query] + [along_y(query, -by) for by in range(1, GROUP)]
    forward, backward = [normed], [normed]
    for step in range(3):
        forward.append(along_z(forward[-1], 1))
        backward.append(along_z(backward[-1], -1))
        if step == 0:
            forward[1], backward[1], _ = lax.optimization_barrier(
                (forward[1], backward[1], query)
            )
        if step == 1:
            forward[2], backward[2], queries[1], queries[3] = lax.optimization_barrier(
                (forward[2], backward[2], queries[1], queries[3])
            )
    *state, query_rows = attend("attend_near", queries, forward[:3] + backward[1:2])
    forward[3], backward[3], *state = lax.optimization_barrier((forward[3], backward[3], *state))
    last = [along_z(forward[3][:half], 1), along_z(backward[3][half:], -1)]
    state = attend("attend_far", [query_rows], [backward[2], forward[3], backward[3]], state)
    parts = {}
    for strips in ((2,), (1, 3), (0,)):
        name = "attend_last_" + "_".join(map(str, strips))
        parts.update(zip(strips, attend(name, [query_rows], last, state, strips)))
    arrived = {by: along_y(parts[by], by) for by in (2, 1, 3)}
    arrived = [arrived[by] for by in range(1, GROUP)]
    late_weight, _ = lax.optimization_barrier((out_weight, parts[0]))
    folded, folded_bias = call(
        fold_body,
        "fold",
        [((channels, channels), BF16), ((1, channels), F32)],
        [VMEM] * 4,
        2 * channels**3,
    )(qkv_weight, qkv_bias, late_weight, out_bias.reshape(1, channels))
    (mixed,) = call(
        merge_body,
        "merge",
        [((rows, channels), BF16)],
        [VMEM] * 8,
        2 * rows * channels * channels,
        [pltpu.VMEM((rows, channels), BF16), pltpu.SemaphoreType.DMA((2,))],
        out_spec=HBM,
    )(parts[0], *arrived, shift, hidden, folded, folded_bias)
    return mixed.reshape(feature.shape)


def solution(mesh):
    in_specs = (P("tm", "strip", None, None), P(None, "strip", None, None)) + (P(),) * 8
    out_specs = P("tm", "strip", None, None)
    return jax.shard_map(local, mesh=mesh, in_specs=in_specs, out_specs=out_specs, check_vma=False)
```

```python
import functools
import math

import jax
import jax.numpy as jnp
from jax import lax
from jax.experimental import pallas as pl
from jax.experimental.pallas import tpu as pltpu
from jax.sharding import PartitionSpec as P

EPSILON = 1e-06
FRAMES = 8
ROW_STRIPS = 32
RING = 8
GROUP = 4
STAT_ROWS = 16
LANES = 128
BLOCKS = 2
VMEM = pl.BlockSpec(memory_space=pltpu.VMEM)
SMEM = pl.BlockSpec(memory_space=pltpu.SMEM)
HBM = pl.BlockSpec(memory_space=pltpu.HBM)
F32 = jnp.float32
BF16 = jnp.bfloat16
VMEM_LIMIT = 16 << 20


def pinned(x):
    return pltpu.with_memory_space_constraint(x, pltpu.HBM)


def call(body, name, outs, in_specs, flops, scratch=(), limit=VMEM_LIMIT, out_spec=VMEM):
    return pl.pallas_call(
        body,
        name=name,
        out_shape=[jax.ShapeDtypeStruct(*out) for out in outs],
        in_specs=in_specs,
        out_specs=[out_spec] * len(outs),
        scratch_shapes=list(scratch),
        cost_estimate=pl.CostEstimate(flops=int(flops), bytes_accessed=2 << 20, transcendentals=0),
        compiler_params=pltpu.CompilerParams(vmem_limit_bytes=limit),
    )


def rms_scaled(values, gain):
    mean_square = jnp.mean(values * values, axis=-1, keepdims=True)
    return values * lax.rsqrt(mean_square + EPSILON) * gain


def activate(row, gain):
    u = rms_scaled(row.astype(F32), gain)
    return u / (1.0 + jnp.exp(-u))


def put_columns(target, place, row):
    width, channels = row.shape
    column = lax.broadcasted_iota(jnp.int32, row.shape, 0)
    left = jnp.where(column == 0, 0.0, pltpu.roll(row, 1, 0))
    right = jnp.where(column == width - 1, 0.0, pltpu.roll(row, width - 1, 0))
    rows = pl.ds(place * width, width)
    target[rows, 0:channels] = left.astype(BF16)
    target[rows, channels : 2 * channels] = row.astype(BF16)
    target[rows, 2 * channels : 3 * channels] = right.astype(BF16)


def halo_body(frame, feature, frame_cache, to_below, to_above, sems):
    chosen = jnp.where(frame[0] == FRAMES - 2, 0, 1)
    last = feature.shape[0] - 1
    copies = [
        pltpu.make_async_copy(feature.at[last], to_below.at[0], sems.at[0]),
        pltpu.make_async_copy(frame_cache.at[chosen, last], to_below.at[1], sems.at[1]),
        pltpu.make_async_copy(feature.at[0], to_above.at[0], sems.at[2]),
        pltpu.make_async_copy(frame_cache.at[chosen, 0], to_above.at[1], sems.at[3]),
    ]
    for copy in copies:
        copy.start()
    for copy in copies:
        copy.wait()


def conv_local_body(frame, feature, frame_cache, norm_gain, weight, two_later, one_later, outer,
                    columns, row_gain, feat, cache, gain, middle, sems, feat_sem, cache_sem, gain_sem):
    width = feat.shape[1]
    chosen = jnp.where(frame[0] == FRAMES - 2, 0, 1)
    fetch_gain = pltpu.make_async_copy(norm_gain, gain, gain_sem)
    fetch_feat = pltpu.make_async_copy(feature, feat, feat_sem)
    fetch_cache = pltpu.make_async_copy(frame_cache.at[chosen], cache, cache_sem)
    fetch_gain.start()
    fetch_feat.start()
    fetch_cache.start()
    copies, weights = {}, {}
    for frame_tap in range(2):
        for row_tap in (1, 0, 2):
            place = frame_tap, row_tap
            if row_tap == 1:
                weights[place] = middle.at[frame_tap]
            else:
                weights[place] = outer.at[frame_tap, row_tap // 2]
            copies[place] = pltpu.make_async_copy(weight.at[place], weights[place], sems.at[place])
            copies[place].start()
    fetch_gain.wait()
    fetch_feat.wait()
    fetch_cache.wait()
    scale = gain[...].reshape(1, -1)
    row_gain[...] = scale
    for row in range(2):
        put_columns(columns.at[0], row, activate(feat[row], scale))

    @pl.when(frame[0] >= FRAMES - 2)
    def _():
        for row in range(2):
            put_columns(columns.at[1], row, cache[row].astype(F32))

    for frame_tap, out in ((0, two_later), (1, one_later)):
        source = columns.at[jnp.where(frame[0] >= FRAMES - 2 + frame_tap, 1, 0)]
        copies[frame_tap, 1].wait()
        out[...] = jnp.dot(source[...], weights[frame_tap, 1][...], preferred_element_type=F32)
        for side in range(2):
            copies[frame_tap, 2 * side].wait()
            out[pl.ds((1 - side) * width, width), :] += jnp.dot(
                source[side * width : (side + 1) * width, :],
                weights[frame_tap, 2 * side][...],
                preferred_element_type=F32,
            )


def conv_edges_body(frame_tap, frame, above, below, gain, outer, local_sum, out, columns):
    width = above.shape[1]
    cached = frame[0] >= FRAMES - 2 + frame_tap

    @pl.when(cached)
    def _():
        for side, halo in enumerate((above, below)):
            put_columns(columns, side, halo[1].astype(F32))

    @pl.when(jnp.logical_not(cached))
    def _():
        for side, halo in enumerate((above, below)):
            put_columns(columns, side, activate(halo[0], gain[...]))

    for side in range(2):
        rows = pl.ds(side * width, width)
        product = jnp.dot(
            columns[side * width : (side + 1) * width, :],
            outer[frame_tap, side],
            preferred_element_type=F32,
        )
        out[rows, :] = (local_sum[rows, :] + product).astype(BF16)


def conv_own_body(above, below, gain, weight, inner, own, columns, held, sems):
    width = above.shape[1]
    rows = own.shape[0]
    copies = []
    for row_tap in range(3):
        copies.append(pltpu.make_async_copy(weight.at[2, row_tap], held.at[row_tap], sems.at[row_tap]))
        copies[row_tap].start()
    put_columns(columns, 0, activate(above[0], gain[...]))
    columns[width : width + rows, :] = inner[0]
    put_columns(columns, 1 + rows // width, activate(below[0], gain[...]))
    for row_tap in range(3):
        copies[row_tap].wait()
        product = jnp.dot(
            columns[row_tap * width : row_tap * width + rows, :],
            held[row_tap],
            preferred_element_type=F32,
        )
        if row_tap == 0:
            own[...] = product
        else:
            own[...] += product


def hidden_body(feat, own, one, two, bias, gain, hidden, normed):
    values = feat[...].astype(F32).reshape(own.shape)
    branch = own[...] + one[...].astype(F32) + two[...].astype(F32) + bias[...]
    result = (values + branch).astype(BF16)
    hidden[...] = result
    normed[...] = rms_scaled(result.astype(F32), gain[...]).astype(BF16)


def query_body(normed, weight, bias, query, shift):
    channels = normed.shape[1]
    scale = math.log2(math.e) / math.sqrt(channels)
    q = jnp.dot(normed[...], weight[:, :channels], preferred_element_type=F32) + bias[:, :channels]
    q = q.astype(BF16)
    absorbed = lax.dot_general(
        q, weight[:, channels : 2 * channels], (((1,), (1,)), ((), ())), preferred_element_type=F32
    )
    query[...] = (absorbed * scale).astype(BF16)
    key_bias = bias[:, channels : 2 * channels]
    shift[...] = as_row(jnp.sum(q.astype(F32) * key_bias, axis=-1, keepdims=True) * scale, channels)


def as_row(column, width):
    shape = column.shape[0], width
    row = lax.broadcasted_iota(jnp.int32, shape, 0)
    lane = lax.broadcasted_iota(jnp.int32, shape, 1)
    return jnp.sum(jnp.where(row == lane, column, 0.0), axis=0, keepdims=True)


def widen(lanes, width):
    return jnp.concatenate([lanes] * (-(-width // LANES)), axis=1)[:, :width]


def attend_body(chunks, first, strips, *refs):
    count = GROUP if first else 1
    given, refs = refs[:count], refs[count:]
    pieces, refs = refs[:chunks], refs[chunks:]
    if not first:
        (total_in, top_in), refs = refs[:2], refs[2:]
    outs, keys = refs[:-1], refs[-1]
    channels = pieces[0].shape[1]
    if first:
        queries = outs[2]
        strip = given[0].shape[0]
        for number, query in enumerate(given):
            queries[number * strip : (number + 1) * strip, :] = query[...]
    else:
        queries = given[0]
    strip = queries.shape[0] // GROUP
    start = 0
    for piece in pieces:
        keys[start : start + piece.shape[0], :channels] = piece[...]
        start += piece.shape[0]
    keys[:, channels:] = jnp.ones((start, LANES), BF16)
    if strips:
        blocks = [slice(number * strip, (number + 1) * strip) for number in strips]
    else:
        rows = queries.shape[0] // BLOCKS
        blocks = [slice(block * rows, (block + 1) * rows) for block in range(BLOCKS)]
    for number, block in enumerate(blocks):
        scores = lax.dot_general(
            queries[block, :], keys[:, :channels], (((1,), (1,)), ((), ())),
            preferred_element_type=F32,
        )
        top = jnp.broadcast_to(jnp.max(scores, axis=1, keepdims=True), (scores.shape[0], LANES))
        if not first:
            old_top = top_in[block, :]
            top = jnp.maximum(top, old_top)
        weights = jnp.exp2(scores - widen(top, start)).astype(BF16)
        total = jnp.dot(weights, keys[...], preferred_element_type=F32)
        if not first:
            factor = jnp.exp2(old_top - top)
            total = total + total_in[block, :] * widen(factor, channels + LANES)
        if not strips:
            outs[0][block, :] = total
            outs[1][block, :] = top
            continue
        out = outs[number]
        denominator = total[:, channels:]
        out[:strip, :] = (total[:, :channels] * widen(1.0 / denominator, channels)).astype(BF16)
        level = as_row(widen(top + jnp.log2(denominator), channels), channels)
        high = level.astype(BF16).astype(F32)
        middle = (level - high).astype(BF16).astype(F32)
        low = level - high - middle
        stat = lax.broadcasted_iota(jnp.int32, (STAT_ROWS, channels), 0)
        stats = jnp.where(stat == 0, high, jnp.where(stat == 1, middle, jnp.where(stat == 2, low, 0.0)))
        out[strip:, :] = stats.astype(BF16)


def fold_body(weight, bias, out_weight, out_bias, folded, folded_bias):
    channels = out_weight.shape[0]
    folded[...] = jnp.dot(
        weight[:, 2 * channels :], out_weight[...], preferred_element_type=F32
    ).astype(BF16)
    value_bias = bias[:, 2 * channels :]
    high = value_bias.astype(BF16)
    low = (value_bias - high.astype(F32)).astype(BF16)
    both = jnp.concatenate([high, low] * 8, axis=0)
    product = jnp.dot(both, out_weight[...], preferred_element_type=F32)
    folded_bias[...] = product[0:1] + product[1:2] + out_bias[...]


def merge_body(part0, part1, part2, part3, shift, hidden, weight, bias, mixed, buffer, sems):
    rows = hidden.shape[0]
    half = rows // 2
    parts = (part0, part1, part2, part3)
    levels = []
    for part in parts:
        stats = part[rows:, :].astype(F32)
        levels.append(stats[0:1] + stats[1:2] + stats[2:3] + shift[...])
    top = functools.reduce(jnp.maximum, levels)
    shares = [jnp.exp2(level - top) for level in levels]
    inverse = 1.0 / sum(shares)
    shares = jnp.concatenate([share * inverse for share in shares] * 2, axis=0)
    shares = jnp.transpose(shares)[:rows]
    copies = []
    for side in range(2):
        inside = slice(side * half, (side + 1) * half)
        total = sum(
            shares[inside, number : number + 1] * part[inside, :].astype(F32)
            for number, part in enumerate(parts)
        )
        result = jnp.dot(total.astype(BF16), weight[...], preferred_element_type=F32)
        result = result + bias[...] + hidden[inside, :].astype(F32)
        buffer[inside, :] = result.astype(BF16)
        copies.append(pltpu.make_async_copy(buffer.at[inside], mixed.at[inside], sems.at[side]))
        copies[side].start()
    for copy in copies:
        copy.wait()


def along_y(x, by):
    pairs = [
        (z * GROUP + y, z * GROUP + (y + by) % GROUP) for z in range(RING) for y in range(GROUP)
    ]
    return lax.ppermute(x, "strip", pairs)


def along_z(x, by):
    pairs = [
        (z * GROUP + y, (z + by) % RING * GROUP + y) for z in range(RING) for y in range(GROUP)
    ]
    return lax.ppermute(x, "strip", pairs)


def local(
    feature,
    frame_cache,
    norm_gain,
    conv_weight,
    conv_bias,
    attn_gain,
    qkv_weight,
    qkv_bias,
    out_weight,
    out_bias,
):
    _, height, width, channels = feature.shape
    rows = height * width
    half = rows // 2
    feat = feature[0]
    frame = lax.axis_index("tm")
    weight = pinned(conv_weight.reshape(3, 3, 3 * channels, channels))
    qkv_bias = qkv_bias.reshape(1, 3 * channels)

    frame_number = frame.reshape(1).astype(jnp.int32)
    feature_rows, cache_rows = pinned(feat), pinned(frame_cache)
    to_below, to_above = call(
        halo_body,
        "halo",
        [((2, width, channels), BF16)] * 2,
        [SMEM, HBM, HBM],
        1 << 20,
        [pltpu.SemaphoreType.DMA((4,))],
    )(frame_number, feature_rows, cache_rows)
    above = lax.ppermute(to_below, "strip", [(s, s + 1) for s in range(ROW_STRIPS - 1)])
    below = lax.ppermute(to_above, "strip", [(s + 1, s) for s in range(ROW_STRIPS - 1)])

    flops = 2 * rows * 3 * channels * channels
    two_local, one_local, outer, inner, gain = call(
        conv_local_body,
        "conv_local",
        [
            ((rows, channels), F32),
            ((rows, channels), F32),
            ((2, 2, 3 * channels, channels), BF16),
            ((2, rows, 3 * channels), BF16),
            ((1, channels), F32),
        ],
        [SMEM, HBM, HBM, HBM, HBM],
        4 * flops,
        [
            pltpu.VMEM((height, width, channels), BF16),
            pltpu.VMEM((height, width, channels), BF16),
            pltpu.VMEM((channels,), F32),
            pltpu.VMEM((2, 3 * channels, channels), BF16),
            pltpu.SemaphoreType.DMA((2, 3)),
            pltpu.SemaphoreType.DMA,
            pltpu.SemaphoreType.DMA,
            pltpu.SemaphoreType.DMA,
        ],
    )(frame_number, feature_rows, cache_rows, pinned(norm_gain), weight)

    def conv_edges(name, frame_tap, local_sum):
        return call(
            functools.partial(conv_edges_body, frame_tap),
            name,
            [((rows, channels), BF16)],
            [SMEM] + [VMEM] * 5,
            flops,
            [pltpu.VMEM((rows, 3 * channels), BF16)],
        )(frame_number, above, below, gain, outer, local_sum)[0]

    two = lax.ppermute(
        conv_edges("conv_edges_two", 0, two_local),
        "tm",
        [(f, (f + 2) % FRAMES) for f in range(FRAMES)],
    )
    one = lax.ppermute(
        conv_edges("conv_edges_one", 1, one_local),
        "tm",
        [(f, (f + 1) % FRAMES) for f in range(FRAMES)],
    )
    (own,) = call(
        conv_own_body,
        "conv_own",
        [((rows, channels), F32)],
        [VMEM, VMEM, VMEM, HBM, VMEM],
        3 * flops,
        [
            pltpu.VMEM((2 * width + rows, 3 * channels), BF16),
            pltpu.VMEM((3, 3 * channels, channels), BF16),
            pltpu.SemaphoreType.DMA((3,)),
        ],
    )(above, below, gain, weight, inner)
    hidden, normed = call(
        hidden_body,
        "hidden",
        [((rows, channels), BF16)] * 2,
        [VMEM] * 6,
        rows * channels * 20,
    )(feat, own, one, two, conv_bias.reshape(1, channels), attn_gain.reshape(1, channels))
    query, shift = call(
        query_body,
        "query",
        [((rows, channels), BF16), ((1, channels), F32)],
        [VMEM] * 3,
        4 * rows * channels * channels,
    )(normed, qkv_weight, qkv_bias)

    def attend(name, given, pieces, state=(), strips=()):
        if strips:
            outs = [((rows + STAT_ROWS, channels), BF16)] * len(strips)
        else:
            outs = [((GROUP * rows, channels + LANES), F32), ((GROUP * rows, LANES), F32)]
        if not state:
            outs.append(((GROUP * rows, channels), BF16))
        keys = sum(piece.shape[0] for piece in pieces)
        return call(
            functools.partial(attend_body, len(pieces), not state, strips),
            name,
            outs,
            [VMEM] * (len(given) + len(pieces) + len(state)),
            4 * (len(strips) or GROUP) * rows * keys * channels,
            [pltpu.VMEM((keys, channels + LANES), BF16)],
            32 << 20,
        )(*given, *pieces, *state)

    queries = [query] + [along_y(query, -by) for by in range(1, GROUP)]
    forward, backward = [normed], [normed]
    for step in range(3):
        forward.append(along_z(forward[-1], 1))
        backward.append(along_z(backward[-1], -1))
        if step == 0:
            forward[1], backward[1], _ = lax.optimization_barrier(
                (forward[1], backward[1], query)
            )
        if step == 1:
            forward[2], backward[2], queries[1], queries[3] = lax.optimization_barrier(
                (forward[2], backward[2], queries[1], queries[3])
            )
    *state, query_rows = attend("attend_near", queries, forward[:3] + backward[1:2])
    forward[3], backward[3], *state = lax.optimization_barrier((forward[3], backward[3], *state))
    last = [along_z(forward[3][:half], 1), along_z(backward[3][half:], -1)]
    state = attend("attend_far", [query_rows], [backward[2], forward[3], backward[3]], state)
    parts = {}
    for strips in ((2,), (1, 3), (0,)):
        name = "attend_last_" + "_".join(map(str, strips))
        parts.update(zip(strips, attend(name, [query_rows], last, state, strips)))
    arrived = {by: along_y(parts[by], by) for by in (2, 1, 3)}
    arrived = [arrived[by] for by in range(1, GROUP)]
    late_weight, _ = lax.optimization_barrier((out_weight, parts[0]))
    folded, folded_bias = call(
        fold_body,
        "fold",
        [((channels, channels), BF16), ((1, channels), F32)],
        [VMEM] * 4,
        2 * channels**3,
    )(qkv_weight, qkv_bias, late_weight, out_bias.reshape(1, channels))
    (mixed,) = call(
        merge_body,
        "merge",
        [((rows, channels), BF16)],
        [VMEM] * 8,
        2 * rows * channels * channels,
        [pltpu.VMEM((rows, channels), BF16), pltpu.SemaphoreType.DMA((2,))],
        out_spec=HBM,
    )(parts[0], *arrived, shift, hidden, folded, folded_bias)
    return mixed.reshape(feature.shape)


def solution(mesh):
    in_specs = (P("tm", "strip", None, None), P(None, "strip", None, None)) + (P(),) * 8
    out_specs = P("tm", "strip", None, None)
    return jax.shard_map(local, mesh=mesh, in_specs=in_specs, out_specs=out_specs, check_vma=False)
```
